32 devices in a mesh: groups: 2 (over y), sample: 4 (over z), tensor: 4 (over x, core).
Axes of the slice: x: 2, y: 2, z: 4, core: 2. Of those that a mesh axis runs over, the one named last changes fastest.
Arguments:
- queries: bfloat16 [4, 128, 8192], P(None, ('groups', 'sample'), 'tensor'), parts along dimension 1, may hold values from -8 to 8
- new_kv: bfloat16 [4, 128, 2048], P(None, ('groups', 'sample'), 'tensor'), parts along dimension 1, may hold values from -5 to 5
- gen_kv: bfloat16 [128, 512, 2048], P(('groups', 'sample'), None, 'tensor'), parts along dimension 0, may hold values from -5 to 5
- prefix_kv: bfloat16 [8, 256, 2048], P(('groups', 'sample'), None, 'tensor'), parts along dimension 0, may hold values from -5 to 5
- slot_prompt: int32 [8], P(('groups', 'sample')), parts along dimension 0, may hold values from 0 to 3, each once
- prefix_blocks: int32 [8], P(('groups', 'sample')), parts along dimension 0, may hold values from 1 to 2, as said below
- gen_len: int32 [128], P(('groups', 'sample')), parts along dimension 0, may hold values from 1 to 512, as said below
- out_weight: bfloat16 [8192, 4096], P('tensor', 'sample'), may hold values from -0.75 to 0.75
Outputs:
- mixed: bfloat16 [4, 128, 4096], P(None, ('groups', 'sample'), 'tensor'), parts along dimension 1
The draws below stay inside these ranges and needn't reach their ends.
There are 2 independent parts, one for each index of `groups`. The reference program is written for one: setup_inputs(seed, part) draws one part's arguments, and reference() takes and returns one part's arrays. A program takes and returns all parts, laid end to end along the dimension named above; an argument that names none is the same for every part. Nothing has to cross between parts.
Inputs may be any that keep to these rules, and one draw needn't show every extreme that they name: `slot_prompt`: each slot holds one prompt's prefix and every prompt has a slot. `prefix_blocks`: some slot has 2 valid blocks. `gen_len`: some sequence has generated 512 tokens.
All inputs are finite; a program needn't handle non-finite values.
Results may differ from the reference program's by a relative error of at most 0.0057.
Values may be sent and summed in bfloat16 or wider, within the bound.
No kernel may reach another device: no remote copies, remote signals or barrier semaphores. Data moves between devices by JAX's collectives and lax.ppermute only.
A program may use at most 128 MiB of HBM per device.

```python
import jax
import jax.numpy as jnp
from jax import lax

D = 4096
QH = 64
KVH = 8
HD = 128
SAMPLES = 16
STEPS = 4
BLOCK = 128
PBLK = 2
GEN = 512
PROMPTS = 4
ROWS = 64


def draw_queries(key, part):
    base = jnp.clip(jax.random.normal(jax.random.fold_in(key, 11), (STEPS, ROWS, QH * HD), jnp.float32), -6.0, 6.0)
    return base.astype(jnp.bfloat16)


def draw_prefix_kv(key, part):
    base = jnp.clip(jax.random.normal(jax.random.fold_in(key, 12), (PROMPTS, PBLK * BLOCK, KVH, 2, HD), jnp.float32), -5.0, 5.0)
    return base.reshape(PROMPTS, PBLK * BLOCK, KVH * 2 * HD).astype(jnp.bfloat16)


def draw_prefix_blocks(key, part):
    values = jax.random.randint(jax.random.fold_in(key, 13), (PROMPTS,), 1, PBLK + 1, dtype=jnp.int32)
    where_full = jax.random.randint(jax.random.fold_in(key, 14), (), 0, PROMPTS, dtype=jnp.int32)
    return values.at[where_full].set(PBLK)


def draw_gen_len(key, part):
    values = jax.random.randint(jax.random.fold_in(key, 15), (ROWS,), 1, GEN + 1, dtype=jnp.int32)
    where_full = jax.random.randint(jax.random.fold_in(key, 16), (), 0, ROWS, dtype=jnp.int32)
    return values.at[where_full].set(GEN)


def steps_of(key, dims, shards, least, high):
    def one(position, blocks):
        steps = jax.random.uniform(jax.random.fold_in(jax.random.fold_in(key, 6), position), (blocks,), jnp.float32, least / len(shards), high / len(shards))
        return jnp.repeat(jnp.exp(steps), dims[position] // blocks).reshape((-1,) + (1,) * (len(dims) - position - 1))

    level = one(*shards[0])
    for cut in shards[1:]:
        level = level * one(*cut)
    return level


def normal_values(stream_key, dims, scale, limit, shards=(), kind=jnp.bfloat16):
    level = steps_of(stream_key, dims, shards, -0.22, 0.18) if shards else 1.0
    values = jax.random.normal(stream_key, dims, jnp.float32) * scale * level
    return jnp.minimum(jnp.maximum(values, -limit), limit).astype(kind)


def setup_inputs(seed: int = 0, part: int = 0) -> dict:
    streams_of = jax.random.split(jax.random.key(seed), 9)
    part_keys = jax.random.split(jax.random.fold_in(streams_of[8], part), 9)
    return {
        "queries": draw_queries(jax.random.fold_in(jax.random.fold_in(streams_of[8], part), 71), part),
        "new_kv": normal_values(part_keys[1], (STEPS, ROWS, KVH * 2 * HD), 1.0, 5.0, ((1, 4), (2, 4))),
        "gen_kv": normal_values(part_keys[2], (ROWS, GEN, KVH * 2 * HD), 1.0, 5.0, ((0, 4), (2, 4))),
        "prefix_kv": draw_prefix_kv(jax.random.fold_in(jax.random.fold_in(streams_of[8], part), 71), part),
        "slot_prompt": jax.random.permutation(part_keys[4], PROMPTS).astype(jnp.int32),
        "prefix_blocks": draw_prefix_blocks(jax.random.fold_in(jax.random.fold_in(streams_of[8], part), 71), part),
        "gen_len": draw_gen_len(jax.random.fold_in(jax.random.fold_in(streams_of[8], part), 71), part),
        "out_weight": normal_values(streams_of[7], (QH * HD, D), (QH * HD // 128) ** -0.5, 0.75, ((0, 4), (1, 4))),
    }


def split_pairs(cache, heads):
    shaped = cache.reshape(cache.shape[:-1] + (heads, 2, HD))
    return shaped[..., 0, :].astype(jnp.float32), shaped[..., 1, :].astype(jnp.float32)


def attend(queries, fresh, cached, prefix, valid, lengths, heads):
    steps_n, rows_n, width = queries.shape
    group = width // (heads * HD)
    scale = HD ** -0.5
    q_all = queries.reshape(steps_n, rows_n, heads, group, HD).astype(jnp.float32)
    pre_key, pre_val = split_pairs(prefix, heads)
    gen_key, gen_val = split_pairs(cached, heads)
    new_key, new_val = split_pairs(fresh, heads)
    s_pre = jnp.einsum("srkgd,rpkd->srkgp", q_all, pre_key) * scale
    s_gen = jnp.einsum("srkgd,rjkd->srkgj", q_all, gen_key) * scale
    s_new = jnp.einsum("srkgd,urkd->srkgu", q_all, new_key) * scale
    m_pre = (jnp.arange(prefix.shape[1], dtype=jnp.int32)[None, :] < valid[:, None])[None, :, None, None, :]
    m_gen = (jnp.arange(cached.shape[1], dtype=jnp.int32)[None, :] < lengths[:, None])[None, :, None, None, :]
    order = jnp.arange(steps_n, dtype=jnp.int32)
    m_new = (order[None, :] <= order[:, None])[:, None, None, None, :]
    s_pre = jnp.where(m_pre, s_pre, -jnp.inf)
    s_gen = jnp.where(m_gen, s_gen, -jnp.inf)
    s_new = jnp.where(m_new, s_new, -jnp.inf)
    top = jnp.maximum(jnp.maximum(jnp.max(s_pre, -1, keepdims=True), jnp.max(s_gen, -1, keepdims=True)), jnp.max(s_new, -1, keepdims=True))
    e_pre = jnp.exp(s_pre - top)
    e_gen = jnp.exp(s_gen - top)
    e_new = jnp.exp(s_new - top)
    total = jnp.sum(e_pre, -1, keepdims=True) + jnp.sum(e_gen, -1, keepdims=True) + jnp.sum(e_new, -1, keepdims=True)
    w_pre = (e_pre / total).astype(jnp.bfloat16).astype(jnp.float32)
    w_gen = (e_gen / total).astype(jnp.bfloat16).astype(jnp.float32)
    w_new = (e_new / total).astype(jnp.bfloat16).astype(jnp.float32)
    result = jnp.einsum("srkgp,rpkd->srkgd", w_pre, pre_val)
    result = result + jnp.einsum("srkgj,rjkd->srkgd", w_gen, gen_val)
    result = result + jnp.einsum("srkgu,urkd->srkgd", w_new, new_val)
    return result.reshape(steps_n, rows_n, width).astype(jnp.bfloat16)


def reference(queries, new_kv, gen_kv, prefix_kv, slot_prompt, prefix_blocks, gen_len, out_weight):
    inverse = jnp.zeros((PROMPTS,), jnp.int32).at[slot_prompt].set(jnp.arange(PROMPTS, dtype=jnp.int32))
    picked_all = inverse[jnp.arange(ROWS, dtype=jnp.int32) % PROMPTS]

    def one_block(index):
        start = (index * SAMPLES).astype(jnp.int32)
        block_q = lax.dynamic_slice_in_dim(queries, start, SAMPLES, 1)
        fresh = lax.dynamic_slice_in_dim(new_kv, start, SAMPLES, 1)
        cached = lax.dynamic_slice_in_dim(gen_kv, start, SAMPLES, 0)
        lengths = lax.dynamic_slice_in_dim(gen_len, start, SAMPLES, 0)
        picked = lax.dynamic_slice_in_dim(picked_all, start, SAMPLES, 0)
        prefix = jnp.take(prefix_kv, picked, axis=0)
        valid = jnp.take(prefix_blocks, picked) * BLOCK
        return attend(block_q, fresh, cached, prefix, valid, lengths, KVH)

    blocks = lax.map(one_block, jnp.arange(ROWS // SAMPLES, dtype=jnp.int32))
    attended = jnp.transpose(blocks, (1, 0, 2, 3)).reshape(STEPS * ROWS, QH * HD)
    mixed = jnp.dot(attended, out_weight, preferred_element_type=jnp.float32)
    return mixed.astype(jnp.bfloat16).reshape(STEPS, ROWS, D)
```

```python
import functools

import jax
import jax.numpy as jnp
from jax import lax
from jax.experimental import pallas as pl
from jax.experimental.pallas import tpu as pltpu
from jax.sharding import PartitionSpec as P

HD = 128
BLOCK = 128
LOW = -1e30


def nt(a, b):
    return lax.dot_general(a, b, (((1,), (1,)), ((), ())), preferred_element_type=jnp.float32)


def nn(a, b):
    return lax.dot_general(a, b, (((1,), (0,)), ((), ())), preferred_element_type=jnp.float32)


def gen_kernel(steps, heads, group, len_ref, q_ref, new_ref, kv_ref, acc_ref, ml_ref, q_scr):
    row = pl.program_id(0)
    rows = pl.num_programs(0)
    span = steps * group
    per_row = heads * span

    @pl.when(row == 0)
    def _():
        for s in range(steps):
            for hg in range(heads * group):
                tile = q_ref[s, :, hg * HD : (hg + 1) * HD].astype(jnp.float32)
                start = (hg // group) * span + s * group + hg % group
                q_scr[pl.ds(start, q_ref.shape[1], stride=per_row), :] = tile

    scale = HD ** (-0.5)
    length = len_ref[row]
    keys = kv_ref.shape[1]
    col = lax.broadcasted_iota(jnp.int32, (span, keys), 1)
    step_of = lax.broadcasted_iota(jnp.int32, (span, 1), 0) // group
    lane = lax.broadcasted_iota(jnp.int32, (span, HD), 1)
    for h in range(heads):
        base = h * 2 * HD
        q32 = q_scr[pl.ds(pl.multiple_of(row * per_row + h * span, span), span), :]
        k = kv_ref[0, :, base : base + HD]
        v = kv_ref[0, :, base + HD : base + 2 * HD]
        s = nt(q32.astype(jnp.bfloat16), k) * scale
        s = jnp.where(col < length, s, LOW)
        top = jnp.max(s, axis=1, keepdims=True)
        fresh = []
        for u in range(steps):
            ku = new_ref[0, u : u + 1, base : base + HD]
            su = jnp.sum(q32 * ku, axis=1, keepdims=True) * scale
            su = jnp.where(step_of >= u, su, LOW)
            fresh.append(su)
            top = jnp.maximum(top, su)
        e = jnp.exp(s - top)
        total = jnp.sum(e, axis=1, keepdims=True)
        acc = nn(e.astype(jnp.bfloat16), v)
        for u in range(steps):
            eu = jnp.exp(fresh[u] - top)
            total = total + eu
            vu = new_ref[0, u : u + 1, base + HD : base + 2 * HD]
            acc = acc + eu.astype(jnp.bfloat16).astype(jnp.float32) * vu
        acc_ref[0, h * span : (h + 1) * span, :] = acc
        ml_ref[0, h * span : (h + 1) * span, :] = jnp.where(lane < HD // 2, top, total)


def gen_attention(queries, fresh, cached, lengths, heads):
    steps, rows, width = queries.shape
    group = width // (heads * HD)
    per_row = heads * steps * group
    fresh = jnp.transpose(fresh, (1, 0, 2)).astype(jnp.float32)
    keys, kvw = cached.shape[1:]
    shape = jax.ShapeDtypeStruct((rows, per_row, HD), jnp.float32)
    return pl.pallas_call(
        functools.partial(gen_kernel, steps, heads, group),
        out_shape=(shape, shape),
        grid_spec=pltpu.PrefetchScalarGridSpec(
            num_scalar_prefetch=1,
            grid=(rows,),
            in_specs=[
                pl.BlockSpec((steps, rows, width), lambda r, n: (0, 0, 0)),
                pl.BlockSpec((1, steps, kvw), lambda r, n: (r, 0, 0)),
                pl.BlockSpec((1, keys, kvw), lambda r, n: (r, 0, 0)),
            ],
            out_specs=[
                pl.BlockSpec((1, per_row, HD), lambda r, n: (r, 0, 0)),
                pl.BlockSpec((1, per_row, HD), lambda r, n: (r, 0, 0)),
            ],
            scratch_shapes=[pltpu.VMEM((rows * per_row, HD), jnp.float32)],
        ),
        cost_estimate=pl.CostEstimate(
            flops=4 * rows * per_row * keys * HD,
            bytes_accessed=2 * rows * keys * kvw,
            transcendentals=rows * per_row * keys,
        ),
        name="gen_attention",
    )(lengths, queries, fresh, cached)


def prefix_kernel(
    slots, steps, heads, group, pick_ref, valid_ref, q_ref, acc_ref, ml_ref, *rest
):
    pre_refs = rest[:slots]
    out_ref, pre_scr, q_scr, o_scr, sems = rest[slots:]
    rows = q_ref.shape[1]
    span = steps * group
    per_row = heads * span
    keys = pre_scr.shape[1]
    copies = [
        pltpu.make_async_copy(pre_refs[k].at[0], pre_scr.at[k], sems.at[k]) for k in range(slots)
    ]
    for copy in copies:
        copy.start()
    for s in range(steps):
        for hg in range(heads * group):
            tile = q_ref[s, :, hg * HD : (hg + 1) * HD].astype(jnp.float32)
            start = (hg // group) * span + s * group + hg % group
            q_scr[pl.ds(start, rows, stride=per_row), :] = tile
    for copy in copies:
        copy.wait()
    scale = HD ** (-0.5)
    col = lax.broadcasted_iota(jnp.int32, (span, keys), 1)

    def one(row):
        slot = pick_ref[row]
        length = valid_ref[row]
        for h in range(heads):
            base = h * 2 * HD
            at = pl.ds(pl.multiple_of(row * per_row + h * span, span), span)
            q = q_scr[at, :].astype(jnp.bfloat16)
            k = pre_scr[slot, :, base : base + HD]
            v = pre_scr[slot, :, base + HD : base + 2 * HD]
            s = nt(q, k) * scale
            s = jnp.where(col < length, s, LOW)
            ml = ml_ref[row, h * span : (h + 1) * span, :]
            old_top = ml[:, 0:1]
            old_total = ml[:, HD // 2 : HD // 2 + 1]
            top = jnp.maximum(old_top, jnp.max(s, axis=1, keepdims=True))
            e = jnp.exp(s - top)
            carry = jnp.exp(old_top - top)
            total = jnp.sum(e, axis=1, keepdims=True) + carry * old_total
            acc = nn(e.astype(jnp.bfloat16), v)
            acc = acc + carry * acc_ref[row, h * span : (h + 1) * span, :]
            o_scr[at, :] = acc / total

    unroll = 4 if rows % 4 == 0 else 1

    def body(i, _):
        for j in range(unroll):
            one(i * unroll + j)
        return 0

    lax.fori_loop(0, rows // unroll, body, 0)
    for s in range(steps):
        for hg in range(heads * group):
            start = (hg // group) * span + s * group + hg % group
            tile = o_scr[pl.ds(start, rows, stride=per_row), :]
            out_ref[s, :, hg * HD : (hg + 1) * HD] = tile.astype(jnp.bfloat16)


def prefix_attention(queries, acc, ml, prefixes, picked, valid, heads):
    steps, rows, width = queries.shape
    group = width // (heads * HD)
    per_row = heads * steps * group
    slots = len(prefixes)
    keys, kvw = prefixes[0].shape[1:]
    vmem = pl.BlockSpec(memory_space=pltpu.VMEM)
    return pl.pallas_call(
        functools.partial(prefix_kernel, slots, steps, heads, group),
        out_shape=jax.ShapeDtypeStruct((steps, rows, width), jnp.bfloat16),
        in_specs=[pl.BlockSpec(memory_space=pltpu.SMEM)] * 2
        + [vmem] * 3
        + [pl.BlockSpec(memory_space=pl.ANY)] * slots,
        out_specs=vmem,
        scratch_shapes=[
            pltpu.VMEM((slots, keys, kvw), jnp.bfloat16),
            pltpu.VMEM((rows * per_row, HD), jnp.float32),
            pltpu.VMEM((rows * per_row, HD), jnp.float32),
            pltpu.SemaphoreType.DMA((slots,)),
        ],
        cost_estimate=pl.CostEstimate(
            flops=4 * rows * per_row * keys * HD,
            bytes_accessed=2 * slots * keys * kvw,
            transcendentals=rows * per_row * keys,
        ),
        name="prefix_attention",
    )(picked, valid, queries, acc, ml, *prefixes)


def project_kernel(parts, pos_ref, *refs):
    att_refs = refs[:parts]
    w_ref, keep_ref, send_ref, lhs = refs[parts:]
    steps, rows, width = att_refs[0].shape
    block = steps * rows

    @pl.when(pl.program_id(0) == 0)
    def _():
        for k in range(parts):
            place = pos_ref[k]
            for s in range(steps):
                lhs[place, s * rows : (s + 1) * rows, :] = att_refs[k][s]

    half = parts // 2 * block
    out = nn(lhs[...].reshape(parts * block, width), w_ref[...])
    keep_ref[...] = out[:half]
    send_ref[...] = out[half:]


def project(attended, weight, pos):
    parts = len(attended)
    steps, rows, width = attended[0].shape
    block = steps * rows
    cols = weight.shape[1]
    tile = 256
    half = parts // 2 * block
    shape = jax.ShapeDtypeStruct((half, cols), jnp.float32)
    return pl.pallas_call(
        functools.partial(project_kernel, parts),
        out_shape=(shape, shape),
        grid_spec=pltpu.PrefetchScalarGridSpec(
            num_scalar_prefetch=1,
            grid=(cols // tile,),
            in_specs=[pl.BlockSpec((steps, rows, width), lambda c, p: (0, 0, 0))] * parts
            + [pl.BlockSpec((width, tile), lambda c, p: (0, c))],
            out_specs=[pl.BlockSpec((half, tile), lambda c, p: (0, c))] * 2,
            scratch_shapes=[pltpu.VMEM((parts, block, width), jnp.bfloat16)],
        ),
        cost_estimate=pl.CostEstimate(
            flops=2 * parts * block * width * cols,
            bytes_accessed=2 * width * cols + 8 * half * cols,
            transcendentals=0,
        ),
        name="project",
    )(pos, *attended, weight)


def around(x, size):
    return [
        lax.ppermute(x, "sample", [(i, (i + k) % size) for i in range(size)])
        for k in range(1, size)
    ]


def direct(
    queries, new_kv, gen_kv, prefix_kv, slot_prompt, prefix_blocks, gen_len, out_weight, size
):
    steps, rows, _ = queries.shape
    heads = new_kv.shape[2] // (2 * HD)
    me = lax.axis_index("sample")
    t = lax.axis_index("tensor")
    chip, core = t // 2, t % 2
    prefixes = [prefix_kv] + around(prefix_kv, size)
    ids = jnp.concatenate([slot_prompt, prefix_blocks])[None, :]
    notes = jnp.concatenate([ids] + around(ids, size), axis=0)
    row_prompt = (me * rows + jnp.arange(rows, dtype=jnp.int32)) % size
    hit = row_prompt[:, None] == notes[None, :, 0]
    picked = jnp.sum(jnp.where(hit, jnp.arange(size, dtype=jnp.int32)[None, :], 0), axis=1)
    valid = jnp.sum(jnp.where(hit, notes[None, :, 1], 0), axis=1) * BLOCK
    acc, ml = gen_attention(queries, new_kv, gen_kv, gen_len, heads)
    own = prefix_attention(queries, acc, ml, prefixes, picked, valid, heads)
    attended = [own] + around(own, size)
    source = (me - jnp.arange(size, dtype=jnp.int32)) % size
    keep, send = project(attended, out_weight, source ^ (2 * core + chip))
    got = lax.ppermute(send, "tensor", [(0, 1), (1, 0), (2, 3), (3, 2)])
    halves = (keep + got).astype(jnp.bfloat16)
    block = steps * rows
    arrived = []
    for i in range(2):
        perm = []
        for c in range(size):
            for k in range(size):
                perm.append((c * size + k, (2 * (k % 2) + (i ^ (k // 2))) * size + c))
        piece = lax.ppermute(halves[i * block : (i + 1) * block], ("sample", "tensor"), perm)
        arrived.append(piece.astype(jnp.float32))
    mixed = (arrived[0] + arrived[1]).astype(jnp.bfloat16)
    return mixed.reshape(steps, rows, -1)


def split_pairs(cache, heads):
    shaped = cache.reshape(cache.shape[:-1] + (heads, 2, HD))
    return (shaped[..., 0, :], shaped[..., 1, :])


def attend(queries, fresh, cached, prefix, valid, lengths, heads):
    steps_n, rows_n, width = queries.shape
    group = width // (heads * HD)
    scale = HD ** (-0.5)
    q_all = queries.reshape(steps_n, rows_n, heads, group, HD)
    pre_key, pre_val = split_pairs(prefix, heads)
    gen_key, gen_val = split_pairs(cached, heads)
    new_key, new_val = split_pairs(fresh, heads)
    s_pre = (
        jnp.einsum("srkgd,rpkd->srkgp", q_all, pre_key, preferred_element_type=jnp.float32) * scale
    )
    s_gen = (
        jnp.einsum("srkgd,rjkd->srkgj", q_all, gen_key, preferred_element_type=jnp.float32) * scale
    )
    s_new = (
        jnp.einsum("srkgd,urkd->srkgu", q_all, new_key, preferred_element_type=jnp.float32) * scale
    )
    m_pre = (jnp.arange(prefix.shape[1], dtype=jnp.int32)[None, :] < valid[:, None])[
        None, :, None, None, :
    ]
    m_gen = (jnp.arange(cached.shape[1], dtype=jnp.int32)[None, :] < lengths[:, None])[
        None, :, None, None, :
    ]
    order = jnp.arange(steps_n, dtype=jnp.int32)
    m_new = (order[None, :] <= order[:, None])[:, None, None, None, :]
    s_pre = jnp.where(m_pre, s_pre, -jnp.inf)
    s_gen = jnp.where(m_gen, s_gen, -jnp.inf)
    s_new = jnp.where(m_new, s_new, -jnp.inf)
    top = jnp.maximum(
        jnp.maximum(jnp.max(s_pre, -1, keepdims=True), jnp.max(s_gen, -1, keepdims=True)),
        jnp.max(s_new, -1, keepdims=True),
    )
    e_pre = jnp.exp(s_pre - top)
    e_gen = jnp.exp(s_gen - top)
    e_new = jnp.exp(s_new - top)
    total = (
        jnp.sum(e_pre, -1, keepdims=True)
        + jnp.sum(e_gen, -1, keepdims=True)
        + jnp.sum(e_new, -1, keepdims=True)
    )
    w_pre = (e_pre / total).astype(jnp.bfloat16)
    w_gen = (e_gen / total).astype(jnp.bfloat16)
    w_new = (e_new / total).astype(jnp.bfloat16)
    result = jnp.einsum("srkgp,rpkd->srkgd", w_pre, pre_val, preferred_element_type=jnp.float32)
    result = result + jnp.einsum(
        "srkgj,rjkd->srkgd", w_gen, gen_val, preferred_element_type=jnp.float32
    )
    result = result + jnp.einsum(
        "srkgu,urkd->srkgd", w_new, new_val, preferred_element_type=jnp.float32
    )
    return result.reshape(steps_n, rows_n, width).astype(jnp.bfloat16)


def shards(queries, new_kv, gen_kv, prefix_kv, slot_prompt, prefix_blocks, gen_len, out_weight):
    size = lax.axis_size("sample")
    if size == 4 and lax.axis_size("tensor") == 4 and prefix_kv.shape[0] == 1:
        return direct(
            queries, new_kv, gen_kv, prefix_kv, slot_prompt, prefix_blocks, gen_len, out_weight, size
        )
    steps_n, rows_n, width = queries.shape
    heads_local = new_kv.shape[2] // (2 * HD)
    all_prefix, all_slots, all_blocks = (
        lax.all_gather(prefix_kv, "sample", axis=0, tiled=True),
        lax.all_gather(slot_prompt, "sample", axis=0, tiled=True),
        lax.all_gather(prefix_blocks, "sample", axis=0, tiled=True),
    )
    prompt_total = all_slots.shape[0]
    inverse = (
        jnp.zeros((prompt_total,), jnp.int32)
        .at[all_slots]
        .set(jnp.arange(prompt_total, dtype=jnp.int32))
    )
    row_ids = lax.axis_index("sample") * rows_n + jnp.arange(rows_n, dtype=jnp.int32)
    picked = inverse[row_ids % prompt_total]
    own_prefix = jnp.take(all_prefix, picked, axis=0)
    valid = jnp.take(all_blocks, picked) * BLOCK
    attended = attend(queries, new_kv, gen_kv, own_prefix, valid, gen_len, heads_local)
    partial_sums = jnp.einsum(
        "srh,hc->src",
        attended,
        lax.all_gather(out_weight, "sample", axis=1, tiled=True),
        preferred_element_type=jnp.float32,
    )
    summed = []
    for step in range(steps_n):
        summed.append(
            lax.psum_scatter(partial_sums[step], "tensor", scatter_dimension=1, tiled=True)
        )
    mixed = jnp.stack(summed, axis=0)
    return mixed.astype(jnp.bfloat16)


def solution(mesh):
    in_specs = (
        P(None, ("groups", "sample"), "tensor"),
        P(None, ("groups", "sample"), "tensor"),
        P(("groups", "sample"), None, "tensor"),
        P(("groups", "sample"), None, "tensor"),
        P(("groups", "sample")),
        P(("groups", "sample")),
        P(("groups", "sample")),
        P("tensor", "sample"),
    )
    out_specs = P(None, ("groups", "sample"), "tensor")
    return jax.shard_map(shards, mesh=mesh, in_specs=in_specs, out_specs=out_specs, check_vma=False)
```

```python
import functools

import jax
import jax.numpy as jnp
from jax import lax
from jax.experimental import pallas as pl
from jax.experimental.pallas import tpu as pltpu
from jax.sharding import PartitionSpec as P

HD = 128
BLOCK = 128
LOW = -1e30


def nt(a, b):
    return lax.dot_general(a, b, (((1,), (1,)), ((), ())), preferred_element_type=jnp.float32)


def nn(a, b):
    return lax.dot_general(a, b, (((1,), (0,)), ((), ())), preferred_element_type=jnp.float32)


def regroup_kernel(steps, heads, group, q_ref, out_ref, scr):
    rows = q_ref.shape[1]
    span = steps * group
    per_row = heads * span
    for s in range(steps):
        for hg in range(heads * group):
            tile = q_ref[s, :, hg * HD : (hg + 1) * HD].astype(jnp.float32)
            start = (hg // group) * span + s * group + hg % group
            scr[pl.ds(start, rows, stride=per_row), :] = tile
    for r in range(rows):
        out_ref[r] = scr[r * per_row : (r + 1) * per_row, :].astype(jnp.bfloat16)


def regroup(queries, heads):
    steps, rows, width = queries.shape
    group = width // (heads * HD)
    per_row = heads * steps * group
    return pl.pallas_call(
        functools.partial(regroup_kernel, steps, heads, group),
        out_shape=jax.ShapeDtypeStruct((rows, per_row, HD), jnp.bfloat16),
        in_specs=[pl.BlockSpec(memory_space=pltpu.VMEM)],
        out_specs=pl.BlockSpec(memory_space=pltpu.VMEM),
        scratch_shapes=[pltpu.VMEM((rows * per_row, HD), jnp.float32)],
        compiler_params=pltpu.CompilerParams(vmem_limit_bytes=4 << 20),
        name="regroup",
    )(queries)


def gen_kernel(steps, heads, group, first, len_ref, q_ref, new_ref, kv_ref, acc_ref, ml_ref):
    batch, keys, _ = kv_ref.shape
    span = steps * group
    rows = new_ref.shape[1]
    row = first + pl.program_id(0) * batch
    scale = HD ** (-0.5)
    col = lax.broadcasted_iota(jnp.int32, (span, keys), 1)
    new_col = lax.broadcasted_iota(jnp.int32, (span, steps * rows), 1)
    new_row, new_step = new_col % rows, new_col // rows
    step_of = lax.broadcasted_iota(jnp.int32, (span, steps * rows), 0) // group
    causal = new_step <= step_of
    lane = lax.broadcasted_iota(jnp.int32, (span, HD), 1)
    for h in range(heads):
        base = h * 2 * HD
        at = slice(h * span, (h + 1) * span)
        fresh = new_ref[:, :, base : base + 2 * HD].reshape(steps * rows, 2 * HD)
        qs = [q_ref[b, at, :] for b in range(batch)]
        scores = [nt(qs[b], kv_ref[b, :, base : base + HD]) for b in range(batch)]
        news = nt(jnp.concatenate(qs, axis=0), fresh[:, :HD])
        tops, exps, new_exps = [], [], []
        for b in range(batch):
            s = jnp.where(col < len_ref[row + b], scores[b] * scale, LOW)
            n = news[b * span : (b + 1) * span] * scale
            n = jnp.where(causal & (new_row == row + b), n, LOW)
            top = jnp.maximum(
                jnp.max(s, axis=1, keepdims=True), jnp.max(n, axis=1, keepdims=True)
            )
            e, f = jnp.exp(s - top), jnp.exp(n - top)
            total = jnp.sum(e, axis=1, keepdims=True) + jnp.sum(f, axis=1, keepdims=True)
            ml_ref[b, at, :] = jnp.where(lane < HD // 2, top, total)
            exps.append(e.astype(jnp.bfloat16))
            new_exps.append(f.astype(jnp.bfloat16))
        more = nn(jnp.concatenate(new_exps, axis=0), fresh[:, HD:])
        for b in range(batch):
            acc = nn(exps[b], kv_ref[b, :, base + HD : base + 2 * HD])
            acc_ref[b, at, :] = acc + more[b * span : (b + 1) * span]


def gen_attention(grouped, fresh, cached, lengths, heads, first, count, batch):
    steps, rows, kvw = fresh.shape
    per_row = grouped.shape[1]
    group = per_row // (heads * steps)
    keys = cached.shape[1]
    shape = jax.ShapeDtypeStruct((count, per_row, HD), jnp.float32)
    skip = first // batch
    return pl.pallas_call(
        functools.partial(gen_kernel, steps, heads, group, first),
        out_shape=(shape, shape),
        grid_spec=pltpu.PrefetchScalarGridSpec(
            num_scalar_prefetch=1,
            grid=(count // batch,),
            in_specs=[
                pl.BlockSpec((batch, per_row, HD), lambda r, n: (r + skip, 0, 0)),
                pl.BlockSpec((steps, rows, kvw), lambda r, n: (0, 0, 0)),
                pl.BlockSpec((batch, keys, kvw), lambda r, n: (r + skip, 0, 0)),
            ],
            out_specs=[
                pl.BlockSpec((batch, per_row, HD), lambda r, n: (r, 0, 0)),
                pl.BlockSpec((batch, per_row, HD), lambda r, n: (r, 0, 0)),
            ],
        ),
        compiler_params=pltpu.CompilerParams(vmem_limit_bytes=56 << 20),
        cost_estimate=pl.CostEstimate(
            flops=4 * count * per_row * keys * HD,
            bytes_accessed=2 * count * keys * kvw,
            transcendentals=count * per_row * keys,
        ),
        name="gen_attention",
    )(lengths, grouped, fresh, cached)


def prefix_kernel(slots, parts, steps, heads, group, *refs):
    notes, refs = refs[:slots], refs[slots:]
    pre_refs, refs = refs[:slots], refs[slots:]
    q_ref, refs = refs[0], refs[1:]
    acc_refs, ml_refs, refs = refs[:parts], refs[parts : 2 * parts], refs[2 * parts :]
    out_ref, pre_scr, o_scr = refs
    rows = q_ref.shape[0]
    span = steps * group
    per_row = heads * span
    keys = pre_scr.shape[1]
    per_part = rows // parts
    for k in range(slots):
        pre_scr[notes[k][0, 0]] = pre_refs[k][0]
    scale = HD ** (-0.5)
    col = lax.broadcasted_iota(jnp.int32, (span * rows // slots, keys), 1)
    for prompt in range(slots):
        length = 0
        for k in range(slots):
            length = length + jnp.where(notes[k][0, 0] == prompt, notes[k][0, 1], 0) * BLOCK
        members = list(range(prompt, rows, slots))
        for h in range(heads):
            base = h * 2 * HD
            at = slice(h * span, (h + 1) * span)
            q = jnp.concatenate([q_ref[r, at, :] for r in members], axis=0)
            ml = jnp.concatenate(
                [ml_refs[r // per_part][r % per_part, at, :] for r in members], axis=0
            )
            acc = jnp.concatenate(
                [acc_refs[r // per_part][r % per_part, at, :] for r in members], axis=0
            )
            s = nt(q, pre_scr[prompt, :, base : base + HD]) * scale
            s = jnp.where(col < length, s, LOW)
            old_top = ml[:, 0:1]
            old_total = ml[:, HD // 2 : HD // 2 + 1]
            top = jnp.maximum(old_top, jnp.max(s, axis=1, keepdims=True))
            e = jnp.exp(s - top)
            carry = jnp.exp(old_top - top)
            total = jnp.sum(e, axis=1, keepdims=True) + carry * old_total
            add = nn(e.astype(jnp.bfloat16), pre_scr[prompt, :, base + HD : base + 2 * HD])
            done = (add + carry * acc) / total
            for i, r in enumerate(members):
                o_scr[r * per_row + h * span : r * per_row + (h + 1) * span, :] = done[
                    i * span : (i + 1) * span
                ]
    for s in range(steps):
        for hg in range(heads * group):
            start = (hg // group) * span + s * group + hg % group
            tile = o_scr[pl.ds(start, rows, stride=per_row), :]
            out_ref[s, :, hg * HD : (hg + 1) * HD] = tile.astype(jnp.bfloat16)


def prefix_attention(grouped, sums, notes, prefixes, steps, heads):
    rows, per_row, _ = grouped.shape
    group = per_row // (heads * steps)
    slots = len(prefixes)
    keys, kvw = prefixes[0].shape[1:]
    vmem = pl.BlockSpec(memory_space=pltpu.VMEM)
    accs, mls = [a for a, _ in sums], [m for _, m in sums]
    return pl.pallas_call(
        functools.partial(prefix_kernel, slots, len(sums), steps, heads, group),
        out_shape=jax.ShapeDtypeStruct((steps, rows, heads * group * HD), jnp.bfloat16),
        in_specs=[pl.BlockSpec(memory_space=pltpu.SMEM)] * slots
        + [vmem] * (slots + 1 + 2 * len(sums)),
        out_specs=vmem,
        scratch_shapes=[
            pltpu.VMEM((slots, keys, kvw), jnp.bfloat16),
            pltpu.VMEM((rows * per_row, HD), jnp.float32),
        ],
        compiler_params=pltpu.CompilerParams(vmem_limit_bytes=16 << 20),
        cost_estimate=pl.CostEstimate(
            flops=4 * rows * per_row * keys * HD,
            bytes_accessed=2 * slots * keys * kvw,
            transcendentals=rows * per_row * keys,
        ),
        name="prefix_attention",
    )(*notes, *prefixes, grouped, *accs, *mls)


def project_kernel(parts, pos_ref, *refs):
    att_refs = refs[:parts]
    w_ref, keep_ref, send_ref, lhs = refs[parts:]
    steps, rows, width = att_refs[0].shape
    block = steps * rows

    @pl.when(pl.program_id(0) == 0)
    def _():
        for k in range(parts):
            place = pos_ref[k]
            for s in range(steps):
                lhs[place, s * rows : (s + 1) * rows, :] = att_refs[k][s]

    half = parts // 2 * block
    out = nn(lhs[...].reshape(parts * block, width), w_ref[...])
    keep_ref[...] = out[:half]
    send_ref[...] = out[half:]


def project(attended, weight, pos):
    parts = len(attended)
    steps, rows, width = attended[0].shape
    block = steps * rows
    cols = weight.shape[1]
    tile = 256
    half = parts // 2 * block
    shape = jax.ShapeDtypeStruct((half, cols), jnp.float32)
    return pl.pallas_call(
        functools.partial(project_kernel, parts),
        out_shape=(shape, shape),
        grid_spec=pltpu.PrefetchScalarGridSpec(
            num_scalar_prefetch=1,
            grid=(cols // tile,),
            in_specs=[pl.BlockSpec((steps, rows, width), lambda c, p: (0, 0, 0))] * parts
            + [pl.BlockSpec((width, tile), lambda c, p: (0, c))],
            out_specs=[pl.BlockSpec((half, tile), lambda c, p: (0, c))] * 2,
            scratch_shapes=[pltpu.VMEM((parts, block, width), jnp.bfloat16)],
        ),
        compiler_params=pltpu.CompilerParams(vmem_limit_bytes=16 << 20),
        cost_estimate=pl.CostEstimate(
            flops=2 * parts * block * width * cols,
            bytes_accessed=2 * width * cols + 8 * half * cols,
            transcendentals=0,
        ),
        name="project",
    )(pos, *attended, weight)


def exchange(x, size, flip):
    return lax.ppermute(x, "sample", [(i, i ^ flip) for i in range(size)])


def gather_four(x, size):
    far = exchange(x, size, 3)
    near = exchange(x, size, 1)
    return [x, near, far, exchange(far, size, 1)]


def direct(
    queries, new_kv, gen_kv, prefix_kv, slot_prompt, prefix_blocks, gen_len, out_weight, size
):
    steps, rows, _ = queries.shape
    heads = new_kv.shape[2] // (2 * HD)
    me = lax.axis_index("sample")
    t = lax.axis_index("tensor")
    chip, core = t // 2, t % 2
    flips = (0, 1, 3, 2)
    far = exchange(prefix_kv, size, 3)
    near = exchange(prefix_kv, size, 1)
    ids = jnp.concatenate([slot_prompt, prefix_blocks])[None, :]
    notes = [ids] + [exchange(ids, size, flip) for flip in flips[1:]]
    grouped = regroup(queries, heads)
    half = rows // 2
    attend_gen = functools.partial(gen_attention, grouped, new_kv, gen_kv)
    early = attend_gen(gen_len, heads, 0, half, 4)
    far, early = lax.optimization_barrier((far, early))
    late = attend_gen(gen_len, heads, half, half, 4)
    prefixes = [prefix_kv, near, far, exchange(far, size, 1)]
    sums = [early, late]
    own = prefix_attention(grouped, sums, notes, prefixes, steps, heads)
    attended = gather_four(own, size)
    source = jnp.stack([me ^ flip for flip in flips])
    keep, send = project(attended, out_weight, source ^ (2 * core + chip))
    got = lax.ppermute(send, "tensor", [(0, 1), (1, 0), (2, 3), (3, 2)])
    halves = (keep + got).astype(jnp.bfloat16)
    block = steps * rows
    arrived = []
    for i in range(2):
        perm = []
        for c in range(size):
            for k in range(size):
                perm.append((c * size + k, (2 * (k % 2) + (i ^ (k // 2))) * size + c))
        piece = lax.ppermute(halves[i * block : (i + 1) * block], ("sample", "tensor"), perm)
        arrived.append(piece.astype(jnp.float32))
    mixed = (arrived[0] + arrived[1]).astype(jnp.bfloat16)
    return mixed.reshape(steps, rows, -1)


def split_pairs(cache, heads):
    shaped = cache.reshape(cache.shape[:-1] + (heads, 2, HD))
    return (shaped[..., 0, :], shaped[..., 1, :])


def attend(queries, fresh, cached, prefix, valid, lengths, heads):
    steps_n, rows_n, width = queries.shape
    group = width // (heads * HD)
    scale = HD ** (-0.5)
    q_all = queries.reshape(steps_n, rows_n, heads, group, HD)
    pre_key, pre_val = split_pairs(prefix, heads)
    gen_key, gen_val = split_pairs(cached, heads)
    new_key, new_val = split_pairs(fresh, heads)
    s_pre = (
        jnp.einsum("srkgd,rpkd->srkgp", q_all, pre_key, preferred_element_type=jnp.float32) * scale
    )
    s_gen = (
        jnp.einsum("srkgd,rjkd->srkgj", q_all, gen_key, preferred_element_type=jnp.float32) * scale
    )
    s_new = (
        jnp.einsum("srkgd,urkd->srkgu", q_all, new_key, preferred_element_type=jnp.float32) * scale
    )
    m_pre = (jnp.arange(prefix.shape[1], dtype=jnp.int32)[None, :] < valid[:, None])[
        None, :, None, None, :
    ]
    m_gen = (jnp.arange(cached.shape[1], dtype=jnp.int32)[None, :] < lengths[:, None])[
        None, :, None, None, :
    ]
    order = jnp.arange(steps_n, dtype=jnp.int32)
    m_new = (order[None, :] <= order[:, None])[:, None, None, None, :]
    s_pre = jnp.where(m_pre, s_pre, -jnp.inf)
    s_gen = jnp.where(m_gen, s_gen, -jnp.inf)
    s_new = jnp.where(m_new, s_new, -jnp.inf)
    top = jnp.maximum(
        jnp.maximum(jnp.max(s_pre, -1, keepdims=True), jnp.max(s_gen, -1, keepdims=True)),
        jnp.max(s_new, -1, keepdims=True),
    )
    e_pre = jnp.exp(s_pre - top)
    e_gen = jnp.exp(s_gen - top)
    e_new = jnp.exp(s_new - top)
    total = (
        jnp.sum(e_pre, -1, keepdims=True)
        + jnp.sum(e_gen, -1, keepdims=True)
        + jnp.sum(e_new, -1, keepdims=True)
    )
    w_pre = (e_pre / total).astype(jnp.bfloat16)
    w_gen = (e_gen / total).astype(jnp.bfloat16)
    w_new = (e_new / total).astype(jnp.bfloat16)
    result = jnp.einsum("srkgp,rpkd->srkgd", w_pre, pre_val, preferred_element_type=jnp.float32)
    result = result + jnp.einsum(
        "srkgj,rjkd->srkgd", w_gen, gen_val, preferred_element_type=jnp.float32
    )
    result = result + jnp.einsum(
        "srkgu,urkd->srkgd", w_new, new_val, preferred_element_type=jnp.float32
    )
    return result.reshape(steps_n, rows_n, width).astype(jnp.bfloat16)


def shards(queries, new_kv, gen_kv, prefix_kv, slot_prompt, prefix_blocks, gen_len, out_weight):
    size = lax.axis_size("sample")
    fits = size == 4 and lax.axis_size("tensor") == 4 and prefix_kv.shape[0] == 1
    if fits and queries.shape[1] % 8 == 0:
        return direct(
            queries, new_kv, gen_kv, prefix_kv, slot_prompt, prefix_blocks, gen_len, out_weight, size
        )
    steps_n, rows_n, width = queries.shape
    heads_local = new_kv.shape[2] // (2 * HD)
    all_prefix, all_slots, all_blocks = (
        lax.all_gather(prefix_kv, "sample", axis=0, tiled=True),
        lax.all_gather(slot_prompt, "sample", axis=0, tiled=True),
        lax.all_gather(prefix_blocks, "sample", axis=0, tiled=True),
    )
    prompt_total = all_slots.shape[0]
    inverse = (
        jnp.zeros((prompt_total,), jnp.int32)
        .at[all_slots]
        .set(jnp.arange(prompt_total, dtype=jnp.int32))
    )
    row_ids = lax.axis_index("sample") * rows_n + jnp.arange(rows_n, dtype=jnp.int32)
    picked = inverse[row_ids % prompt_total]
    own_prefix = jnp.take(all_prefix, picked, axis=0)
    valid = jnp.take(all_blocks, picked) * BLOCK
    attended = attend(queries, new_kv, gen_kv, own_prefix, valid, gen_len, heads_local)
    partial_sums = jnp.einsum(
        "srh,hc->src",
        attended,
        lax.all_gather(out_weight, "sample", axis=1, tiled=True),
        preferred_element_type=jnp.float32,
    )
    summed = []
    for step in range(steps_n):
        summed.append(
            lax.psum_scatter(partial_sums[step], "tensor", scatter_dimension=1, tiled=True)
        )
    mixed = jnp.stack(summed, axis=0)
    return mixed.astype(jnp.bfloat16)


def solution(mesh):
    in_specs = (
        P(None, ("groups", "sample"), "tensor"),
        P(None, ("groups", "sample"), "tensor"),
        P(("groups", "sample"), None, "tensor"),
        P(("groups", "sample"), None, "tensor"),
        P(("groups", "sample")),
        P(("groups", "sample")),
        P(("groups", "sample")),
        P("tensor", "sample"),
    )
    out_specs = P(None, ("groups", "sample"), "tensor")
    return jax.shard_map(shards, mesh=mesh, in_specs=in_specs, out_specs=out_specs, check_vma=False)
```

```python
import functools

import jax
import jax.numpy as jnp
from jax import lax
from jax.experimental import pallas as pl
from jax.experimental.pallas import tpu as pltpu
from jax.sharding import PartitionSpec as P

HD = 128
BLOCK = 128
LOW = -1e30
EXTRA = 8


def nt(a, b):
    return lax.dot_general(a, b, (((1,), (1,)), ((), ())), preferred_element_type=jnp.float32)


def nn(a, b):
    return lax.dot_general(a, b, (((1,), (0,)), ((), ())), preferred_element_type=jnp.float32)


def in_hbm(x):
    return pltpu.with_memory_space_constraint(x, pltpu.HBM)


def payload_kernel(prompt_ref, blocks_ref, pre_ref, out_ref, sem):
    keys, kvw = pre_ref.shape[1:]
    copy = pltpu.make_async_copy(pre_ref, out_ref.at[:, pl.ds(0, keys), :], sem)
    copy.start()
    shape = (1, out_ref.shape[1] - keys, kvw // 2)
    out_ref[:, keys:, : kvw // 2] = jnp.full(shape, prompt_ref[0], jnp.float32).astype(jnp.bfloat16)
    out_ref[:, keys:, kvw // 2 :] = jnp.full(shape, blocks_ref[0], jnp.float32).astype(jnp.bfloat16)
    copy.wait()


def make_payload(prefix_kv, slot_prompt, prefix_blocks):
    _, keys, kvw = prefix_kv.shape
    smem = pl.BlockSpec(memory_space=pltpu.SMEM)
    return pl.pallas_call(
        payload_kernel,
        out_shape=jax.ShapeDtypeStruct((1, keys + EXTRA, kvw), prefix_kv.dtype),
        in_specs=[smem, smem, pl.BlockSpec(memory_space=pl.ANY)],
        out_specs=pl.BlockSpec(memory_space=pltpu.VMEM),
        scratch_shapes=[pltpu.SemaphoreType.DMA],
        compiler_params=pltpu.CompilerParams(vmem_limit_bytes=4 << 20),
        name="make_payload",
    )(slot_prompt, prefix_blocks, in_hbm(prefix_kv))


def gen_rows(steps, group, row, len_ref, q_ref, new_ref, kv_ref, acc_ref, ml_ref, q_at):
    batch, keys, kvw = kv_ref.shape
    heads = kvw // (2 * HD)
    span = steps * group
    rows = new_ref.shape[1]
    scale = HD ** (-0.5)
    col = lax.broadcasted_iota(jnp.int32, (span, keys), 1)
    new_col = lax.broadcasted_iota(jnp.int32, (span, steps * rows), 1)
    new_row, new_step = new_col % rows, new_col // rows
    step_of = lax.broadcasted_iota(jnp.int32, (span, steps * rows), 0) // group
    causal = new_step <= step_of
    lane = lax.broadcasted_iota(jnp.int32, (span, HD), 1)
    for h in range(heads):
        base = h * 2 * HD
        at = slice(h * span, (h + 1) * span)
        fresh = new_ref[:, :, base : base + 2 * HD].reshape(steps * rows, 2 * HD)
        qs = [q_ref[q_at + b, at, :] for b in range(batch)]
        scores = [nt(qs[b], kv_ref[b, :, base : base + HD]) for b in range(batch)]
        news = nt(jnp.concatenate(qs, axis=0), fresh[:, :HD])
        exps, new_exps = [], []
        for b in range(batch):
            s = jnp.where(col < len_ref[row + b], scores[b] * scale, LOW)
            n = news[b * span : (b + 1) * span] * scale
            n = jnp.where(causal & (new_row == row + b), n, LOW)
            top = jnp.maximum(
                jnp.max(s, axis=1, keepdims=True), jnp.max(n, axis=1, keepdims=True)
            )
            e, f = jnp.exp(s - top), jnp.exp(n - top)
            total = jnp.sum(e, axis=1, keepdims=True) + jnp.sum(f, axis=1, keepdims=True)
            ml_ref[b, at, :] = jnp.where(lane < HD // 2, top, total)
            exps.append(e.astype(jnp.bfloat16))
            new_exps.append(f.astype(jnp.bfloat16))
        more = nn(jnp.concatenate(new_exps, axis=0), fresh[:, HD:])
        for b in range(batch):
            acc = nn(exps[b], kv_ref[b, :, base + HD : base + 2 * HD])
            acc_ref[b, at, :] = acc + more[b * span : (b + 1) * span]


def early_kernel(
    steps, heads, group, len_ref, q_ref, new_ref, kv_ref, grouped_ref, acc_ref, ml_ref, scr
):
    rows = q_ref.shape[1]
    span = steps * group
    per_row = heads * span
    batch = kv_ref.shape[0]

    @pl.when(pl.program_id(0) == 0)
    def _():
        for s in range(steps):
            for hg in range(heads * group):
                tile = q_ref[s, :, hg * HD : (hg + 1) * HD].astype(jnp.float32)
                start = (hg // group) * span + s * group + hg % group
                scr[pl.ds(start, rows, stride=per_row), :] = tile
        for r in range(rows):
            grouped_ref[r] = scr[r * per_row : (r + 1) * per_row, :].astype(jnp.bfloat16)

    row = pl.program_id(0) * batch
    gen_rows(steps, group, row, len_ref, grouped_ref, new_ref, kv_ref, acc_ref, ml_ref, row)


def late_kernel(steps, group, first, len_ref, q_ref, new_ref, kv_ref, acc_ref, ml_ref):
    row = first + pl.program_id(0) * kv_ref.shape[0]
    gen_rows(steps, group, row, len_ref, q_ref, new_ref, kv_ref, acc_ref, ml_ref, 0)


def gen_attention(queries, grouped, fresh, cached, lengths, heads, first, count, batch):
    steps, rows, width = queries.shape
    kvw = fresh.shape[2]
    group = width // (heads * HD)
    per_row = heads * steps * group
    keys = cached.shape[1]
    sums = jax.ShapeDtypeStruct((count, per_row, HD), jnp.float32)
    skip = first // batch
    tail_specs = [
        pl.BlockSpec((steps, rows, kvw), lambda r, n: (0, 0, 0)),
        pl.BlockSpec((batch, keys, kvw), lambda r, n: (r + skip, 0, 0)),
    ]
    sum_spec = pl.BlockSpec((batch, per_row, HD), lambda r, n: (r, 0, 0))
    if grouped is None:
        kernel = functools.partial(early_kernel, steps, heads, group)
        source = in_hbm(queries)
        in_specs = [pl.BlockSpec((steps, rows, width), lambda r, n: (0, 0, 0))] + tail_specs
        out_shape = (jax.ShapeDtypeStruct((rows, per_row, HD), jnp.bfloat16), sums, sums)
        out_specs = [pl.BlockSpec((rows, per_row, HD), lambda r, n: (0, 0, 0)), sum_spec, sum_spec]
        scratch = [pltpu.VMEM((rows * per_row, HD), jnp.float32)]
        name = "gen_attention_early"
    else:
        kernel = functools.partial(late_kernel, steps, group, first)
        source = grouped
        in_specs = [pl.BlockSpec((batch, per_row, HD), lambda r, n: (r + skip, 0, 0))] + tail_specs
        out_shape = (sums, sums)
        out_specs = [sum_spec, sum_spec]
        scratch = []
        name = "gen_attention_late"
    return pl.pallas_call(
        kernel,
        out_shape=out_shape,
        grid_spec=pltpu.PrefetchScalarGridSpec(
            num_scalar_prefetch=1,
            grid=(count // batch,),
            in_specs=in_specs,
            out_specs=out_specs,
            scratch_shapes=scratch,
        ),
        compiler_params=pltpu.CompilerParams(vmem_limit_bytes=16 << 20),
        cost_estimate=pl.CostEstimate(
            flops=4 * count * per_row * keys * HD,
            bytes_accessed=2 * count * keys * kvw,
            transcendentals=count * per_row * keys,
        ),
        name=name,
    )(lengths, source, in_hbm(fresh), in_hbm(cached))


def add_slot(slots, span, pre_ref, q_ref, acc_refs, ml_refs, put):
    rows = q_ref.shape[0]
    keys = pre_ref.shape[1] - EXTRA
    kvw = pre_ref.shape[2]
    heads = kvw // (2 * HD)
    per_part = rows // len(acc_refs)
    members = rows // slots
    extra = pre_ref[0, keys:, :].astype(jnp.float32)
    prompt = jnp.max(extra[:, :HD]).astype(jnp.int32)
    length = jnp.max(extra[:, kvw // 2 : kvw // 2 + HD]).astype(jnp.int32) * BLOCK
    scale = HD ** (-0.5)
    col = lax.broadcasted_iota(jnp.int32, (span * members, keys), 1)

    def sums_of(refs, i, at):
        return refs[i * slots // per_part][prompt + i * slots % per_part, at, :]

    for h in range(heads):
        base = h * 2 * HD
        at = slice(h * span, (h + 1) * span)
        order = range(members)
        q = jnp.concatenate([q_ref[prompt + i * slots, at, :] for i in order], axis=0)
        ml = jnp.concatenate([sums_of(ml_refs, i, at) for i in order], axis=0)
        acc = jnp.concatenate([sums_of(acc_refs, i, at) for i in order], axis=0)
        s = nt(q, pre_ref[0, :keys, base : base + HD]) * scale
        s = jnp.where(col < length, s, LOW)
        old_top = ml[:, 0:1]
        old_total = ml[:, HD // 2 : HD // 2 + 1]
        top = jnp.maximum(old_top, jnp.max(s, axis=1, keepdims=True))
        e = jnp.exp(s - top)
        carry = jnp.exp(old_top - top)
        total = jnp.sum(e, axis=1, keepdims=True) + carry * old_total
        add = nn(e.astype(jnp.bfloat16), pre_ref[0, :keys, base + HD : base + 2 * HD])
        done = (add + carry * acc) / total
        for i in order:
            put(prompt + i * slots, h, done[i * span : (i + 1) * span])


def first_slots_kernel(slots, parts, span, *refs):
    pre_refs, refs = refs[: slots - 1], refs[slots - 1 :]
    q_ref, refs = refs[0], refs[1:]
    acc_refs, ml_refs, out_ref = refs[:parts], refs[parts : 2 * parts], refs[2 * parts]

    def put(row, h, value):
        out_ref[row, h * span : (h + 1) * span, :] = value

    for pre_ref in pre_refs:
        add_slot(slots, span, pre_ref, q_ref, acc_refs, ml_refs, put)


def last_slot_kernel(slots, parts, steps, group, *refs):
    pre_ref, done_ref, q_ref, refs = refs[0], refs[1], refs[2], refs[3:]
    acc_refs, ml_refs, (out_ref, scr) = refs[:parts], refs[parts : 2 * parts], refs[2 * parts :]
    rows, per_row, _ = q_ref.shape
    span = steps * group
    heads = per_row // span
    for r in range(rows):
        scr[r * per_row : (r + 1) * per_row, :] = done_ref[r]

    def put(row, h, value):
        scr[pl.ds(pl.multiple_of(row * per_row + h * span, span), span), :] = value

    add_slot(slots, span, pre_ref, q_ref, acc_refs, ml_refs, put)
    for s in range(steps):
        for hg in range(heads * group):
            start = (hg // group) * span + s * group + hg % group
            tile = scr[pl.ds(start, rows, stride=per_row), :]
            out_ref[s, :, hg * HD : (hg + 1) * HD] = tile.astype(jnp.bfloat16)


def first_slots(grouped, accs, mls, payloads, steps, heads):
    rows, per_row, _ = grouped.shape
    slots = len(payloads) + 1
    vmem = pl.BlockSpec(memory_space=pltpu.VMEM)
    keys, kvw = payloads[0].shape[1:]
    return pl.pallas_call(
        functools.partial(first_slots_kernel, slots, len(accs), per_row // heads),
        out_shape=jax.ShapeDtypeStruct((rows, per_row, HD), jnp.float32),
        in_specs=[vmem] * (slots + 2 * len(accs)),
        out_specs=vmem,
        compiler_params=pltpu.CompilerParams(vmem_limit_bytes=8 << 20),
        cost_estimate=pl.CostEstimate(
            flops=3 * rows * per_row * keys * HD,
            bytes_accessed=2 * slots * keys * kvw,
            transcendentals=rows * per_row * keys,
        ),
        name="first_slots",
    )(*payloads, grouped, *accs, *mls)


def last_slot(grouped, accs, mls, payload, done, slots, steps, heads):
    rows, per_row, _ = grouped.shape
    group = per_row // (heads * steps)
    vmem = pl.BlockSpec(memory_space=pltpu.VMEM)
    keys, kvw = payload.shape[1:]
    return pl.pallas_call(
        functools.partial(last_slot_kernel, slots, len(accs), steps, group),
        out_shape=jax.ShapeDtypeStruct((steps, rows, heads * group * HD), jnp.bfloat16),
        in_specs=[vmem] * (3 + 2 * len(accs)),
        out_specs=vmem,
        scratch_shapes=[pltpu.VMEM((rows * per_row, HD), jnp.float32)],
        compiler_params=pltpu.CompilerParams(vmem_limit_bytes=8 << 20),
        cost_estimate=pl.CostEstimate(
            flops=rows * per_row * keys * HD,
            bytes_accessed=2 * keys * kvw,
            transcendentals=rows * per_row * keys // slots,
        ),
        name="last_slot",
    )(payload, done, grouped, *accs, *mls)


def project_kernel(parts, pos_ref, *refs):
    att_refs = refs[:parts]
    w_ref, keep_ref, send_ref, lhs = refs[parts:]
    steps, rows, width = att_refs[0].shape
    block = steps * rows

    @pl.when(pl.program_id(0) == 0)
    def _():
        for k in range(parts):
            place = pos_ref[k]
            for s in range(steps):
                lhs[place, s * rows : (s + 1) * rows, :] = att_refs[k][s]

    half = parts // 2 * block
    out = nn(lhs[...].reshape(parts * block, width), w_ref[...])
    keep_ref[...] = out[:half]
    send_ref[...] = out[half:]


def project(attended, weight, pos):
    parts = len(attended)
    steps, rows, width = attended[0].shape
    block = steps * rows
    cols = weight.shape[1]
    tile = 256
    half = parts // 2 * block
    shape = jax.ShapeDtypeStruct((half, cols), jnp.float32)
    return pl.pallas_call(
        functools.partial(project_kernel, parts),
        out_shape=(shape, shape),
        grid_spec=pltpu.PrefetchScalarGridSpec(
            num_scalar_prefetch=1,
            grid=(cols // tile,),
            in_specs=[pl.BlockSpec((steps, rows, width), lambda c, p: (0, 0, 0))] * parts
            + [pl.BlockSpec((width, tile), lambda c, p: (0, c))],
            out_specs=[pl.BlockSpec((half, tile), lambda c, p: (0, c))] * 2,
            scratch_shapes=[pltpu.VMEM((parts, block, width), jnp.bfloat16)],
        ),
        compiler_params=pltpu.CompilerParams(vmem_limit_bytes=16 << 20),
        cost_estimate=pl.CostEstimate(
            flops=2 * parts * block * width * cols,
            bytes_accessed=2 * width * cols + 8 * half * cols,
            transcendentals=0,
        ),
        name="project",
    )(pos, *attended, in_hbm(weight))


def exchange(x, size, flip):
    return lax.ppermute(x, "sample", [(i, i ^ flip) for i in range(size)])


def gather_four(x, size):
    far = exchange(x, size, 3)
    near = exchange(x, size, 1)
    return [x, near, far, exchange(far, size, 1)]


def direct(
    queries, new_kv, gen_kv, prefix_kv, slot_prompt, prefix_blocks, gen_len, out_weight, size
):
    steps, rows, _ = queries.shape
    heads = new_kv.shape[2] // (2 * HD)
    me = lax.axis_index("sample")
    t = lax.axis_index("tensor")
    chip, core = t // 2, t % 2
    flips = (0, 1, 3, 2)
    payload = make_payload(prefix_kv, slot_prompt, prefix_blocks)
    far = exchange(payload, size, 3)
    near = exchange(payload, size, 1)
    half = rows // 2
    grouped, acc0, ml0 = gen_attention(queries, None, new_kv, gen_kv, gen_len, heads, 0, half, 4)
    far, grouped, acc0, ml0 = lax.optimization_barrier((far, grouped, acc0, ml0))
    diag = exchange(far, size, 1)
    acc1, ml1 = gen_attention(queries, grouped, new_kv, gen_kv, gen_len, heads, half, half, 4)
    accs, mls = [acc0, acc1], [ml0, ml1]
    done = first_slots(grouped, accs, mls, [payload, near, far], steps, heads)
    diag, done = lax.optimization_barrier((diag, done))
    own = last_slot(grouped, accs, mls, diag, done, size, steps, heads)
    attended = gather_four(own, size)
    source = jnp.stack([me ^ flip for flip in flips])
    keep, send = project(attended, out_weight, source ^ (2 * core + chip))
    got = lax.ppermute(send, "tensor", [(0, 1), (1, 0), (2, 3), (3, 2)])
    halves = (keep + got).astype(jnp.bfloat16)
    block = steps * rows
    arrived = []
    for i in range(2):
        perm = []
        for c in range(size):
            for k in range(size):
                perm.append((c * size + k, (2 * (k % 2) + (i ^ (k // 2))) * size + c))
        piece = lax.ppermute(halves[i * block : (i + 1) * block], ("sample", "tensor"), perm)
        arrived.append(piece.astype(jnp.float32))
    mixed = (arrived[0] + arrived[1]).astype(jnp.bfloat16)
    return mixed.reshape(steps, rows, -1)


def split_pairs(cache, heads):
    shaped = cache.reshape(cache.shape[:-1] + (heads, 2, HD))
    return (shaped[..., 0, :], shaped[..., 1, :])


def attend(queries, fresh, cached, prefix, valid, lengths, heads):
    steps_n, rows_n, width = queries.shape
    group = width // (heads * HD)
    scale = HD ** (-0.5)
    q_all = queries.reshape(steps_n, rows_n, heads, group, HD)
    pre_key, pre_val = split_pairs(prefix, heads)
    gen_key, gen_val = split_pairs(cached, heads)
    new_key, new_val = split_pairs(fresh, heads)
    s_pre = (
        jnp.einsum("srkgd,rpkd->srkgp", q_all, pre_key, preferred_element_type=jnp.float32) * scale
    )
    s_gen = (
        jnp.einsum("srkgd,rjkd->srkgj", q_all, gen_key, preferred_element_type=jnp.float32) * scale
    )
    s_new = (
        jnp.einsum("srkgd,urkd->srkgu", q_all, new_key, preferred_element_type=jnp.float32) * scale
    )
    m_pre = (jnp.arange(prefix.shape[1], dtype=jnp.int32)[None, :] < valid[:, None])[
        None, :, None, None, :
    ]
    m_gen = (jnp.arange(cached.shape[1], dtype=jnp.int32)[None, :] < lengths[:, None])[
        None, :, None, None, :
    ]
    order = jnp.arange(steps_n, dtype=jnp.int32)
    m_new = (order[None, :] <= order[:, None])[:, None, None, None, :]
    s_pre = jnp.where(m_pre, s_pre, -jnp.inf)
    s_gen = jnp.where(m_gen, s_gen, -jnp.inf)
    s_new = jnp.where(m_new, s_new, -jnp.inf)
    top = jnp.maximum(
        jnp.maximum(jnp.max(s_pre, -1, keepdims=True), jnp.max(s_gen, -1, keepdims=True)),
        jnp.max(s_new, -1, keepdims=True),
    )
    e_pre = jnp.exp(s_pre - top)
    e_gen = jnp.exp(s_gen - top)
    e_new = jnp.exp(s_new - top)
    total = (
        jnp.sum(e_pre, -1, keepdims=True)
        + jnp.sum(e_gen, -1, keepdims=True)
        + jnp.sum(e_new, -1, keepdims=True)
    )
    w_pre = (e_pre / total).astype(jnp.bfloat16)
    w_gen = (e_gen / total).astype(jnp.bfloat16)
    w_new = (e_new / total).astype(jnp.bfloat16)
    result = jnp.einsum("srkgp,rpkd->srkgd", w_pre, pre_val, preferred_element_type=jnp.float32)
    result = result + jnp.einsum(
        "srkgj,rjkd->srkgd", w_gen, gen_val, preferred_element_type=jnp.float32
    )
    result = result + jnp.einsum(
        "srkgu,urkd->srkgd", w_new, new_val, preferred_element_type=jnp.float32
    )
    return result.reshape(steps_n, rows_n, width).astype(jnp.bfloat16)


def shards(queries, new_kv, gen_kv, prefix_kv, slot_prompt, prefix_blocks, gen_len, out_weight):
    size = lax.axis_size("sample")
    fits = size == 4 and lax.axis_size("tensor") == 4 and prefix_kv.shape[0] == 1
    if fits and queries.shape[1] % 8 == 0:
        return direct(
            queries, new_kv, gen_kv, prefix_kv, slot_prompt, prefix_blocks, gen_len, out_weight, size
        )
    steps_n, rows_n, width = queries.shape
    heads_local = new_kv.shape[2] // (2 * HD)
    all_prefix, all_slots, all_blocks = (
        lax.all_gather(prefix_kv, "sample", axis=0, tiled=True),
        lax.all_gather(slot_prompt, "sample", axis=0, tiled=True),
        lax.all_gather(prefix_blocks, "sample", axis=0, tiled=True),
    )
    prompt_total = all_slots.shape[0]
    inverse = (
        jnp.zeros((prompt_total,), jnp.int32)
        .at[all_slots]
        .set(jnp.arange(prompt_total, dtype=jnp.int32))
    )
    row_ids = lax.axis_index("sample") * rows_n + jnp.arange(rows_n, dtype=jnp.int32)
    picked = inverse[row_ids % prompt_total]
    own_prefix = jnp.take(all_prefix, picked, axis=0)
    valid = jnp.take(all_blocks, picked) * BLOCK
    attended = attend(queries, new_kv, gen_kv, own_prefix, valid, gen_len, heads_local)
    partial_sums = jnp.einsum(
        "srh,hc->src",
        attended,
        lax.all_gather(out_weight, "sample", axis=1, tiled=True),
        preferred_element_type=jnp.float32,
    )
    summed = []
    for step in range(steps_n):
        summed.append(
            lax.psum_scatter(partial_sums[step], "tensor", scatter_dimension=1, tiled=True)
        )
    mixed = jnp.stack(summed, axis=0)
    return mixed.astype(jnp.bfloat16)


def solution(mesh):
    in_specs = (
        P(None, ("groups", "sample"), "tensor"),
        P(None, ("groups", "sample"), "tensor"),
        P(("groups", "sample"), None, "tensor"),
        P(("groups", "sample"), None, "tensor"),
        P(("groups", "sample")),
        P(("groups", "sample")),
        P(("groups", "sample")),
        P("tensor", "sample"),
    )
    out_specs = P(None, ("groups", "sample"), "tensor")
    return jax.shard_map(shards, mesh=mesh, in_specs=in_specs, out_specs=out_specs, check_vma=False)
```

```python
import functools

import jax
import jax.numpy as jnp
from jax import lax
from jax.experimental import pallas as pl
from jax.experimental.pallas import tpu as pltpu
from jax.sharding import PartitionSpec as P

HD = 128
BLOCK = 128
LOW = -1e30
EXTRA = 8


def nt(a, b):
    return lax.dot_general(a, b, (((1,), (1,)), ((), ())), preferred_element_type=jnp.float32)


def nn(a, b):
    return lax.dot_general(a, b, (((1,), (0,)), ((), ())), preferred_element_type=jnp.float32)


def in_hbm(x):
    return pltpu.with_memory_space_constraint(x, pltpu.HBM)


def payload_kernel(prompt_ref, blocks_ref, pre_ref, out_ref, sem):
    keys, kvw = pre_ref.shape[1:]
    copy = pltpu.make_async_copy(pre_ref, out_ref.at[:, pl.ds(0, keys), :], sem)
    copy.start()
    shape = (1, out_ref.shape[1] - keys, kvw // 2)
    out_ref[:, keys:, : kvw // 2] = jnp.full(shape, prompt_ref[0], jnp.float32).astype(jnp.bfloat16)
    out_ref[:, keys:, kvw // 2 :] = jnp.full(shape, blocks_ref[0], jnp.float32).astype(jnp.bfloat16)
    copy.wait()


def make_payload(prefix_kv, slot_prompt, prefix_blocks):
    _, keys, kvw = prefix_kv.shape
    smem = pl.BlockSpec(memory_space=pltpu.SMEM)
    return pl.pallas_call(
        payload_kernel,
        out_shape=jax.ShapeDtypeStruct((1, keys + EXTRA, kvw), prefix_kv.dtype),
        in_specs=[smem, smem, pl.BlockSpec(memory_space=pl.ANY)],
        out_specs=pl.BlockSpec(memory_space=pltpu.VMEM),
        scratch_shapes=[pltpu.SemaphoreType.DMA],
        compiler_params=pltpu.CompilerParams(vmem_limit_bytes=4 << 20),
        name="make_payload",
    )(slot_prompt, prefix_blocks, in_hbm(prefix_kv))


def gen_rows(steps, group, row, len_ref, q_ref, new_ref, kv_ref, acc_ref, ml_ref, q_at):
    batch, keys, kvw = kv_ref.shape
    heads = kvw // (2 * HD)
    span = steps * group
    rows = new_ref.shape[1]
    scale = HD ** (-0.5)
    col = lax.broadcasted_iota(jnp.int32, (span, keys), 1)
    new_col = lax.broadcasted_iota(jnp.int32, (span, steps * rows), 1)
    new_row, new_step = new_col % rows, new_col // rows
    step_of = lax.broadcasted_iota(jnp.int32, (span, steps * rows), 0) // group
    causal = new_step <= step_of
    lane = lax.broadcasted_iota(jnp.int32, (span, HD), 1)
    for h in range(heads):
        base = h * 2 * HD
        at = slice(h * span, (h + 1) * span)
        fresh = new_ref[:, :, base : base + 2 * HD].reshape(steps * rows, 2 * HD)
        qs = [q_ref[q_at + b, at, :] for b in range(batch)]
        scores = [nt(qs[b], kv_ref[b, :, base : base + HD]) for b in range(batch)]
        news = nt(jnp.concatenate(qs, axis=0), fresh[:, :HD])
        exps, new_exps = [], []
        for b in range(batch):
            s = jnp.where(col < len_ref[row + b], scores[b] * scale, LOW)
            n = news[b * span : (b + 1) * span] * scale
            n = jnp.where(causal & (new_row == row + b), n, LOW)
            top = jnp.maximum(
                jnp.max(s, axis=1, keepdims=True), jnp.max(n, axis=1, keepdims=True)
            )
            e, f = jnp.exp(s - top), jnp.exp(n - top)
            total = jnp.sum(e, axis=1, keepdims=True) + jnp.sum(f, axis=1, keepdims=True)
            ml_ref[b, at, :] = jnp.where(lane < HD // 2, top, total)
            exps.append(e.astype(jnp.bfloat16))
            new_exps.append(f.astype(jnp.bfloat16))
        more = nn(jnp.concatenate(new_exps, axis=0), fresh[:, HD:])
        for b in range(batch):
            acc = nn(exps[b], kv_ref[b, :, base + HD : base + 2 * HD])
            acc_ref[b, at, :] = acc + more[b * span : (b + 1) * span]


def early_kernel(
    steps, heads, group, len_ref, q_ref, new_ref, kv_ref, grouped_ref, acc_ref, ml_ref, scr
):
    rows = q_ref.shape[1]
    span = steps * group
    per_row = heads * span
    batch = kv_ref.shape[0]

    @pl.when(pl.program_id(0) == 0)
    def _():
        for s in range(steps):
            for hg in range(heads * group):
                tile = q_ref[s, :, hg * HD : (hg + 1) * HD].astype(jnp.float32)
                start = (hg // group) * span + s * group + hg % group
                scr[pl.ds(start, rows, stride=per_row), :] = tile
        for r in range(rows):
            grouped_ref[r] = scr[r * per_row : (r + 1) * per_row, :].astype(jnp.bfloat16)

    row = pl.program_id(0) * batch
    gen_rows(steps, group, row, len_ref, grouped_ref, new_ref, kv_ref, acc_ref, ml_ref, row)


def late_kernel(steps, group, first, len_ref, q_ref, new_ref, kv_ref, acc_ref, ml_ref):
    row = first + pl.program_id(0) * kv_ref.shape[0]
    gen_rows(steps, group, row, len_ref, q_ref, new_ref, kv_ref, acc_ref, ml_ref, 0)


def gen_attention(queries, grouped, fresh, cached, lengths, heads, first, count, batch):
    steps, rows, width = queries.shape
    kvw = fresh.shape[2]
    group = width // (heads * HD)
    per_row = heads * steps * group
    keys = cached.shape[1]
    sums = jax.ShapeDtypeStruct((count, per_row, HD), jnp.float32)
    skip = first // batch
    tail_specs = [
        pl.BlockSpec((steps, rows, kvw), lambda r, n: (0, 0, 0)),
        pl.BlockSpec((batch, keys, kvw), lambda r, n: (r + skip, 0, 0)),
    ]
    sum_spec = pl.BlockSpec((batch, per_row, HD), lambda r, n: (r, 0, 0))
    if grouped is None:
        kernel = functools.partial(early_kernel, steps, heads, group)
        source = in_hbm(queries)
        in_specs = [pl.BlockSpec((steps, rows, width), lambda r, n: (0, 0, 0))] + tail_specs
        out_shape = (jax.ShapeDtypeStruct((rows, per_row, HD), jnp.bfloat16), sums, sums)
        out_specs = [pl.BlockSpec((rows, per_row, HD), lambda r, n: (0, 0, 0)), sum_spec, sum_spec]
        scratch = [pltpu.VMEM((rows * per_row, HD), jnp.float32)]
        name = "gen_attention_early"
    else:
        kernel = functools.partial(late_kernel, steps, group, first)
        source = grouped
        in_specs = [pl.BlockSpec((batch, per_row, HD), lambda r, n: (r + skip, 0, 0))] + tail_specs
        out_shape = (sums, sums)
        out_specs = [sum_spec, sum_spec]
        scratch = []
        name = "gen_attention_late"
    return pl.pallas_call(
        kernel,
        out_shape=out_shape,
        grid_spec=pltpu.PrefetchScalarGridSpec(
            num_scalar_prefetch=1,
            grid=(count // batch,),
            in_specs=in_specs,
            out_specs=out_specs,
            scratch_shapes=scratch,
        ),
        compiler_params=pltpu.CompilerParams(vmem_limit_bytes=16 << 20),
        cost_estimate=pl.CostEstimate(
            flops=4 * count * per_row * keys * HD,
            bytes_accessed=2 * count * keys * kvw,
            transcendentals=count * per_row * keys,
        ),
        name=name,
    )(lengths, source, in_hbm(fresh), in_hbm(cached))


def add_slot(slots, span, pre_ref, q_ref, acc_refs, ml_refs, put):
    rows = q_ref.shape[0]
    keys = pre_ref.shape[1] - EXTRA
    kvw = pre_ref.shape[2]
    heads = kvw // (2 * HD)
    per_part = rows // len(acc_refs)
    members = rows // slots
    extra = pre_ref[0, keys:, :].astype(jnp.float32)
    prompt = jnp.max(extra[:, :HD]).astype(jnp.int32)
    length = jnp.max(extra[:, kvw // 2 : kvw // 2 + HD]).astype(jnp.int32) * BLOCK
    scale = HD ** (-0.5)
    col = lax.broadcasted_iota(jnp.int32, (span * members, keys), 1)

    def sums_of(refs, i, at):
        return refs[i * slots // per_part][prompt + i * slots % per_part, at, :]

    for h in range(heads):
        base = h * 2 * HD
        at = slice(h * span, (h + 1) * span)
        order = range(members)
        q = jnp.concatenate([q_ref[prompt + i * slots, at, :] for i in order], axis=0)
        ml = jnp.concatenate([sums_of(ml_refs, i, at) for i in order], axis=0)
        acc = jnp.concatenate([sums_of(acc_refs, i, at) for i in order], axis=0)
        s = nt(q, pre_ref[0, :keys, base : base + HD]) * scale
        s = jnp.where(col < length, s, LOW)
        old_top = ml[:, 0:1]
        old_total = ml[:, HD // 2 : HD // 2 + 1]
        top = jnp.maximum(old_top, jnp.max(s, axis=1, keepdims=True))
        e = jnp.exp(s - top)
        carry = jnp.exp(old_top - top)
        total = jnp.sum(e, axis=1, keepdims=True) + carry * old_total
        add = nn(e.astype(jnp.bfloat16), pre_ref[0, :keys, base + HD : base + 2 * HD])
        done = (add + carry * acc) / total
        for i in order:
            put(prompt + i * slots, h, done[i * span : (i + 1) * span])


def first_slots_kernel(slots, parts, span, *refs):
    pre_refs, refs = refs[: slots - 1], refs[slots - 1 :]
    q_ref, refs = refs[0], refs[1:]
    acc_refs, ml_refs, out_ref = refs[:parts], refs[parts : 2 * parts], refs[2 * parts]

    def put(row, h, value):
        out_ref[row, h * span : (h + 1) * span, :] = value

    for pre_ref in pre_refs:
        add_slot(slots, span, pre_ref, q_ref, acc_refs, ml_refs, put)


def last_slot_kernel(slots, parts, steps, group, *refs):
    pre_ref, done_ref, q_ref, refs = refs[0], refs[1], refs[2], refs[3:]
    acc_refs, ml_refs, (out_ref, scr) = refs[:parts], refs[parts : 2 * parts], refs[2 * parts :]
    rows, per_row, _ = q_ref.shape
    span = steps * group
    heads = per_row // span
    for r in range(rows):
        scr[r * per_row : (r + 1) * per_row, :] = done_ref[r]

    def put(row, h, value):
        scr[pl.ds(pl.multiple_of(row * per_row + h * span, span), span), :] = value

    add_slot(slots, span, pre_ref, q_ref, acc_refs, ml_refs, put)
    for s in range(steps):
        for hg in range(heads * group):
            start = (hg // group) * span + s * group + hg % group
            tile = scr[pl.ds(start, rows, stride=per_row), :]
            out_ref[s, :, hg * HD : (hg + 1) * HD] = tile.astype(jnp.bfloat16)


def first_slots(grouped, accs, mls, payloads, steps, heads):
    rows, per_row, _ = grouped.shape
    slots = len(payloads) + 1
    vmem = pl.BlockSpec(memory_space=pltpu.VMEM)
    keys, kvw = payloads[0].shape[1:]
    return pl.pallas_call(
        functools.partial(first_slots_kernel, slots, len(accs), per_row // heads),
        out_shape=jax.ShapeDtypeStruct((rows, per_row, HD), jnp.float32),
        in_specs=[vmem] * (slots + 2 * len(accs)),
        out_specs=vmem,
        compiler_params=pltpu.CompilerParams(vmem_limit_bytes=8 << 20),
        cost_estimate=pl.CostEstimate(
            flops=3 * rows * per_row * keys * HD,
            bytes_accessed=2 * slots * keys * kvw,
            transcendentals=rows * per_row * keys,
        ),
        name="first_slots",
    )(*payloads, grouped, *accs, *mls)


def last_slot(grouped, accs, mls, payload, done, slots, steps, heads):
    rows, per_row, _ = grouped.shape
    group = per_row // (heads * steps)
    vmem = pl.BlockSpec(memory_space=pltpu.VMEM)
    keys, kvw = payload.shape[1:]
    return pl.pallas_call(
        functools.partial(last_slot_kernel, slots, len(accs), steps, group),
        out_shape=jax.ShapeDtypeStruct((steps, rows, heads * group * HD), jnp.bfloat16),
        in_specs=[vmem] * (3 + 2 * len(accs)),
        out_specs=vmem,
        scratch_shapes=[pltpu.VMEM((rows * per_row, HD), jnp.float32)],
        compiler_params=pltpu.CompilerParams(vmem_limit_bytes=8 << 20),
        cost_estimate=pl.CostEstimate(
            flops=rows * per_row * keys * HD,
            bytes_accessed=2 * keys * kvw,
            transcendentals=rows * per_row * keys // slots,
        ),
        name="last_slot",
    )(payload, done, grouped, *accs, *mls)


def project_first_kernel(parts, chunk, *refs):
    att_refs, (w_ref, out_ref, held_ref, lhs, sems) = refs[:parts], refs[parts:]
    steps, rows, width = att_refs[0].shape
    block = steps * rows
    cols = w_ref.shape[1]
    copies = []
    for c in range(cols // chunk):
        at = pl.ds(c * chunk, chunk)
        copies.append(
            pltpu.make_async_copy(w_ref.at[:, at], held_ref.at[:, at], sems.at[c])
        )
        copies[c].start()
    for k in range(parts):
        lhs[k * block : (k + 1) * block, :] = att_refs[k][...].reshape(block, width)
    for c in range(cols // chunk):
        copies[c].wait()
        at = slice(c * chunk, (c + 1) * chunk)
        out_ref[:, at] = nn(lhs[...], held_ref[:, at])


def project_first(attended, weight):
    parts = len(attended)
    steps, rows, width = attended[0].shape
    block = steps * rows
    cols = weight.shape[1]
    chunk = 256
    vmem = pl.BlockSpec(memory_space=pltpu.VMEM)
    return pl.pallas_call(
        functools.partial(project_first_kernel, parts, chunk),
        out_shape=(
            jax.ShapeDtypeStruct((parts * block, cols), jnp.float32),
            jax.ShapeDtypeStruct(weight.shape, weight.dtype),
        ),
        in_specs=[vmem] * parts + [pl.BlockSpec(memory_space=pl.ANY)],
        out_specs=(vmem, vmem),
        scratch_shapes=[
            pltpu.VMEM((parts * block, width), jnp.bfloat16),
            pltpu.SemaphoreType.DMA((cols // chunk,)),
        ],
        compiler_params=pltpu.CompilerParams(vmem_limit_bytes=16 << 20),
        cost_estimate=pl.CostEstimate(
            flops=2 * parts * block * width * cols,
            bytes_accessed=2 * width * cols,
            transcendentals=0,
        ),
        name="project_first",
    )(*attended, in_hbm(weight))


def project_last_kernel(parts, pos_ref, att_ref, first_ref, w_ref, both_ref):
    steps, rows, width = att_ref.shape
    block = steps * rows
    for k in range(parts - 1):
        both_ref[pos_ref[k]] = first_ref[k * block : (k + 1) * block, :]
    both_ref[pos_ref[parts - 1]] = nn(att_ref[...].reshape(block, width), w_ref[...])


def project_last_split_kernel(parts, pos_ref, att_ref, first_ref, w_ref, keep_ref, send_ref, scr):
    project_last_kernel(parts, pos_ref, att_ref, first_ref, w_ref, scr)
    half = parts // 2
    for k in range(half):
        keep_ref[k] = scr[k]
        send_ref[k] = scr[half + k]


def project_last(attended, first, weight, pos, parts):
    steps, rows, width = attended.shape
    block = steps * rows
    cols = weight.shape[1]
    vmem = pl.BlockSpec(memory_space=pltpu.VMEM)
    shape = jax.ShapeDtypeStruct((parts // 2, block, cols), jnp.float32)
    return pl.pallas_call(
        functools.partial(project_last_split_kernel, parts),
        out_shape=(shape, shape),
        in_specs=[pl.BlockSpec(memory_space=pltpu.SMEM)] + [vmem] * 3,
        out_specs=(vmem, vmem),
        scratch_shapes=[pltpu.VMEM((parts, block, cols), jnp.float32)],
        compiler_params=pltpu.CompilerParams(vmem_limit_bytes=8 << 20),
        cost_estimate=pl.CostEstimate(
            flops=2 * block * width * cols,
            bytes_accessed=2 * width * cols,
            transcendentals=0,
        ),
        name="project_last",
    )(pos, attended, first, weight)


def exchange(x, size, flip):
    return lax.ppermute(x, "sample", [(i, i ^ flip) for i in range(size)])


def direct(
    queries, new_kv, gen_kv, prefix_kv, slot_prompt, prefix_blocks, gen_len, out_weight, size
):
    steps, rows, _ = queries.shape
    heads = new_kv.shape[2] // (2 * HD)
    me = lax.axis_index("sample")
    t = lax.axis_index("tensor")
    chip, core = t // 2, t % 2
    flips = (0, 1, 3, 2)
    payload = make_payload(prefix_kv, slot_prompt, prefix_blocks)
    far = exchange(payload, size, 3)
    near = exchange(payload, size, 1)
    half = rows // 2
    grouped, acc0, ml0 = gen_attention(queries, None, new_kv, gen_kv, gen_len, heads, 0, half, 4)
    far, grouped, acc0, ml0 = lax.optimization_barrier((far, grouped, acc0, ml0))
    diag = exchange(far, size, 1)
    acc1, ml1 = gen_attention(queries, grouped, new_kv, gen_kv, gen_len, heads, half, half, 4)
    accs, mls = [acc0, acc1], [ml0, ml1]
    done = first_slots(grouped, accs, mls, [payload, near, far], steps, heads)
    diag, done = lax.optimization_barrier((diag, done))
    own = last_slot(grouped, accs, mls, diag, done, size, steps, heads)
    far = exchange(own, size, 3)
    near = exchange(own, size, 1)
    diag = exchange(far, size, 1)
    first, held = project_first([own, near, far], out_weight)
    diag, first, held = lax.optimization_barrier((diag, first, held))
    source = jnp.stack([me ^ flip for flip in flips])
    keep, send = project_last(diag, first, held, source ^ (2 * core + chip), size)
    got = lax.ppermute(send, "tensor", [(0, 1), (1, 0), (2, 3), (3, 2)])
    halves = (keep + got).astype(jnp.bfloat16)
    arrived = []
    for i in range(2):
        perm = []
        for c in range(size):
            for k in range(size):
                perm.append((c * size + k, (2 * (k % 2) + (i ^ (k // 2))) * size + c))
        piece = lax.ppermute(halves[i], ("sample", "tensor"), perm)
        arrived.append(piece.astype(jnp.float32))
    mixed = (arrived[0] + arrived[1]).astype(jnp.bfloat16)
    return mixed.reshape(steps, rows, -1)


def split_pairs(cache, heads):
    shaped = cache.reshape(cache.shape[:-1] + (heads, 2, HD))
    return (shaped[..., 0, :], shaped[..., 1, :])


def attend(queries, fresh, cached, prefix, valid, lengths, heads):
    steps_n, rows_n, width = queries.shape
    group = width // (heads * HD)
    scale = HD ** (-0.5)
    q_all = queries.reshape(steps_n, rows_n, heads, group, HD)
    pre_key, pre_val = split_pairs(prefix, heads)
    gen_key, gen_val = split_pairs(cached, heads)
    new_key, new_val = split_pairs(fresh, heads)
    s_pre = (
        jnp.einsum("srkgd,rpkd->srkgp", q_all, pre_key, preferred_element_type=jnp.float32) * scale
    )
    s_gen = (
        jnp.einsum("srkgd,rjkd->srkgj", q_all, gen_key, preferred_element_type=jnp.float32) * scale
    )
    s_new = (
        jnp.einsum("srkgd,urkd->srkgu", q_all, new_key, preferred_element_type=jnp.float32) * scale
    )
    m_pre = (jnp.arange(prefix.shape[1], dtype=jnp.int32)[None, :] < valid[:, None])[
        None, :, None, None, :
    ]
    m_gen = (jnp.arange(cached.shape[1], dtype=jnp.int32)[None, :] < lengths[:, None])[
        None, :, None, None, :
    ]
    order = jnp.arange(steps_n, dtype=jnp.int32)
    m_new = (order[None, :] <= order[:, None])[:, None, None, None, :]
    s_pre = jnp.where(m_pre, s_pre, -jnp.inf)
    s_gen = jnp.where(m_gen, s_gen, -jnp.inf)
    s_new = jnp.where(m_new, s_new, -jnp.inf)
    top = jnp.maximum(
        jnp.maximum(jnp.max(s_pre, -1, keepdims=True), jnp.max(s_gen, -1, keepdims=True)),
        jnp.max(s_new, -1, keepdims=True),
    )
    e_pre = jnp.exp(s_pre - top)
    e_gen = jnp.exp(s_gen - top)
    e_new = jnp.exp(s_new - top)
    total = (
        jnp.sum(e_pre, -1, keepdims=True)
        + jnp.sum(e_gen, -1, keepdims=True)
        + jnp.sum(e_new, -1, keepdims=True)
    )
    w_pre = (e_pre / total).astype(jnp.bfloat16)
    w_gen = (e_gen / total).astype(jnp.bfloat16)
    w_new = (e_new / total).astype(jnp.bfloat16)
    result = jnp.einsum("srkgp,rpkd->srkgd", w_pre, pre_val, preferred_element_type=jnp.float32)
    result = result + jnp.einsum(
        "srkgj,rjkd->srkgd", w_gen, gen_val, preferred_element_type=jnp.float32
    )
    result = result + jnp.einsum(
        "srkgu,urkd->srkgd", w_new, new_val, preferred_element_type=jnp.float32
    )
    return result.reshape(steps_n, rows_n, width).astype(jnp.bfloat16)


def shards(queries, new_kv, gen_kv, prefix_kv, slot_prompt, prefix_blocks, gen_len, out_weight):
    size = lax.axis_size("sample")
    fits = size == 4 and lax.axis_size("tensor") == 4 and prefix_kv.shape[0] == 1
    if fits and queries.shape[1] % 8 == 0:
        return direct(
            queries, new_kv, gen_kv, prefix_kv, slot_prompt, prefix_blocks, gen_len, out_weight, size
        )
    steps_n, rows_n, width = queries.shape
    heads_local = new_kv.shape[2] // (2 * HD)
    all_prefix, all_slots, all_blocks = (
        lax.all_gather(prefix_kv, "sample", axis=0, tiled=True),
        lax.all_gather(slot_prompt, "sample", axis=0, tiled=True),
        lax.all_gather(prefix_blocks, "sample", axis=0, tiled=True),
    )
    prompt_total = all_slots.shape[0]
    inverse = (
        jnp.zeros((prompt_total,), jnp.int32)
        .at[all_slots]
        .set(jnp.arange(prompt_total, dtype=jnp.int32))
    )
    row_ids = lax.axis_index("sample") * rows_n + jnp.arange(rows_n, dtype=jnp.int32)
    picked = inverse[row_ids % prompt_total]
    own_prefix = jnp.take(all_prefix, picked, axis=0)
    valid = jnp.take(all_blocks, picked) * BLOCK
    attended = attend(queries, new_kv, gen_kv, own_prefix, valid, gen_len, heads_local)
    partial_sums = jnp.einsum(
        "srh,hc->src",
        attended,
        lax.all_gather(out_weight, "sample", axis=1, tiled=True),
        preferred_element_type=jnp.float32,
    )
    summed = []
    for step in range(steps_n):
        summed.append(
            lax.psum_scatter(partial_sums[step], "tensor", scatter_dimension=1, tiled=True)
        )
    mixed = jnp.stack(summed, axis=0)
    return mixed.astype(jnp.bfloat16)


def solution(mesh):
    in_specs = (
        P(None, ("groups", "sample"), "tensor"),
        P(None, ("groups", "sample"), "tensor"),
        P(("groups", "sample"), None, "tensor"),
        P(("groups", "sample"), None, "tensor"),
        P(("groups", "sample")),
        P(("groups", "sample")),
        P(("groups", "sample")),
        P("tensor", "sample"),
    )
    out_specs = P(None, ("groups", "sample"), "tensor")
    return jax.shard_map(shards, mesh=mesh, in_specs=in_specs, out_specs=out_specs, check_vma=False)
```

```python
import functools

import jax
import jax.numpy as jnp
from jax import lax
from jax.experimental import pallas as pl
from jax.experimental.pallas import tpu as pltpu
from jax.sharding import PartitionSpec as P

HD = 128
BLOCK = 128
LOW = -1e30
EXTRA = 8


def nt(a, b):
    return lax.dot_general(a, b, (((1,), (1,)), ((), ())), preferred_element_type=jnp.float32)


def nn(a, b):
    return lax.dot_general(a, b, (((1,), (0,)), ((), ())), preferred_element_type=jnp.float32)


def in_hbm(x):
    return pltpu.with_memory_space_constraint(x, pltpu.HBM)


def payload_kernel(prompt_ref, blocks_ref, pre_ref, out_ref, sem):
    keys, kvw = pre_ref.shape[1:]
    copy = pltpu.make_async_copy(pre_ref, out_ref.at[:, pl.ds(0, keys), :], sem)
    copy.start()
    shape = (1, out_ref.shape[1] - keys, kvw // 2)
    out_ref[:, keys:, : kvw // 2] = jnp.full(shape, prompt_ref[0], jnp.float32).astype(jnp.bfloat16)
    out_ref[:, keys:, kvw // 2 :] = jnp.full(shape, blocks_ref[0], jnp.float32).astype(jnp.bfloat16)
    copy.wait()


def make_payload(prefix_kv, slot_prompt, prefix_blocks):
    _, keys, kvw = prefix_kv.shape
    smem = pl.BlockSpec(memory_space=pltpu.SMEM)
    return pl.pallas_call(
        payload_kernel,
        out_shape=jax.ShapeDtypeStruct((1, keys + EXTRA, kvw), prefix_kv.dtype),
        in_specs=[smem, smem, pl.BlockSpec(memory_space=pl.ANY)],
        out_specs=pl.BlockSpec(memory_space=pltpu.VMEM),
        scratch_shapes=[pltpu.SemaphoreType.DMA],
        compiler_params=pltpu.CompilerParams(vmem_limit_bytes=4 << 20),
        name="make_payload",
    )(slot_prompt, prefix_blocks, in_hbm(prefix_kv))


def gen_rows(steps, group, row, len_ref, q_ref, new_ref, kv_ref, acc_ref, ml_ref, q_at):
    batch, keys, kvw = kv_ref.shape
    heads = kvw // (2 * HD)
    span = steps * group
    rows = new_ref.shape[1]
    scale = HD ** (-0.5)
    col = lax.broadcasted_iota(jnp.int32, (span, keys), 1)
    new_col = lax.broadcasted_iota(jnp.int32, (span, steps * rows), 1)
    new_row, new_step = new_col % rows, new_col // rows
    step_of = lax.broadcasted_iota(jnp.int32, (span, steps * rows), 0) // group
    causal = new_step <= step_of
    lane = lax.broadcasted_iota(jnp.int32, (span, HD), 1)
    for h in range(heads):
        base = h * 2 * HD
        at = slice(h * span, (h + 1) * span)
        fresh = new_ref[:, :, base : base + 2 * HD].reshape(steps * rows, 2 * HD)
        qs = [q_ref[q_at + b, at, :] for b in range(batch)]
        scores = [nt(qs[b], kv_ref[b, :, base : base + HD]) for b in range(batch)]
        news = nt(jnp.concatenate(qs, axis=0), fresh[:, :HD])
        exps, new_exps = [], []
        for b in range(batch):
            s = jnp.where(col < len_ref[row + b], scores[b] * scale, LOW)
            n = news[b * span : (b + 1) * span] * scale
            n = jnp.where(causal & (new_row == row + b), n, LOW)
            top = jnp.maximum(
                jnp.max(s, axis=1, keepdims=True), jnp.max(n, axis=1, keepdims=True)
            )
            e, f = jnp.exp(s - top), jnp.exp(n - top)
            total = jnp.sum(e, axis=1, keepdims=True) + jnp.sum(f, axis=1, keepdims=True)
            ml_ref[b, at, :] = jnp.where(lane < HD // 2, top, total)
            exps.append(e.astype(jnp.bfloat16))
            new_exps.append(f.astype(jnp.bfloat16))
        more = nn(jnp.concatenate(new_exps, axis=0), fresh[:, HD:])
        for b in range(batch):
            acc = nn(exps[b], kv_ref[b, :, base + HD : base + 2 * HD])
            acc_ref[b, at, :] = acc + more[b * span : (b + 1) * span]


def gen_kernel(
    steps, heads, group, len_ref, q_ref, new_ref, kv_ref, grouped_ref, acc_ref, ml_ref, scr
):
    rows = q_ref.shape[1]
    span = steps * group
    per_row = heads * span
    batch = kv_ref.shape[0]

    @pl.when(pl.program_id(0) == 0)
    def _():
        for s in range(steps):
            for hg in range(heads * group):
                tile = q_ref[s, :, hg * HD : (hg + 1) * HD].astype(jnp.float32)
                start = (hg // group) * span + s * group + hg % group
                scr[pl.ds(start, rows, stride=per_row), :] = tile
        for r in range(rows):
            grouped_ref[r] = scr[r * per_row : (r + 1) * per_row, :].astype(jnp.bfloat16)

    row = pl.program_id(0) * batch
    gen_rows(steps, group, row, len_ref, grouped_ref, new_ref, kv_ref, acc_ref, ml_ref, row)


def gen_attention(queries, fresh, cached, lengths, heads, batch):
    steps, rows, width = queries.shape
    keys, kvw = cached.shape[1:]
    group = width // (heads * HD)
    per_row = heads * steps * group
    sums = jax.ShapeDtypeStruct((rows, per_row, HD), jnp.float32)
    sum_spec = pl.BlockSpec((batch, per_row, HD), lambda r, n: (r, 0, 0))
    return pl.pallas_call(
        functools.partial(gen_kernel, steps, heads, group),
        out_shape=(jax.ShapeDtypeStruct((rows, per_row, HD), jnp.bfloat16), sums, sums),
        grid_spec=pltpu.PrefetchScalarGridSpec(
            num_scalar_prefetch=1,
            grid=(rows // batch,),
            in_specs=[
                pl.BlockSpec((steps, rows, width), lambda r, n: (0, 0, 0)),
                pl.BlockSpec((steps, rows, kvw), lambda r, n: (0, 0, 0)),
                pl.BlockSpec((batch, keys, kvw), lambda r, n: (r, 0, 0)),
            ],
            out_specs=[
                pl.BlockSpec((rows, per_row, HD), lambda r, n: (0, 0, 0)),
                sum_spec,
                sum_spec,
            ],
            scratch_shapes=[pltpu.VMEM((rows * per_row, HD), jnp.float32)],
        ),
        compiler_params=pltpu.CompilerParams(vmem_limit_bytes=16 << 20),
        cost_estimate=pl.CostEstimate(
            flops=4 * rows * per_row * keys * HD,
            bytes_accessed=2 * rows * keys * kvw,
            transcendentals=rows * per_row * keys,
        ),
        name="gen_attention",
    )(lengths, in_hbm(queries), in_hbm(fresh), in_hbm(cached))


def add_slots_kernel(slots, steps, group, count, *refs):
    pre_refs, (q_ref, acc_ref, ml_ref, out_ref, scr) = refs[:count], refs[count:]
    rows = q_ref.shape[0]
    keys = pre_refs[0].shape[1] - EXTRA
    kvw = pre_refs[0].shape[2]
    heads = kvw // (2 * HD)
    span = steps * group
    members = rows // slots
    order = range(members)
    tall = members * span
    scale = HD ** (-0.5)
    col = lax.broadcasted_iota(jnp.int32, (tall, keys), 1)
    for n, pre_ref in enumerate(pre_refs):
        extra = pre_ref[0, keys:, :].astype(jnp.float32)
        prompt = jnp.max(extra[:, :HD]).astype(jnp.int32)
        length = jnp.max(extra[:, kvw // 2 : kvw // 2 + HD]).astype(jnp.int32) * BLOCK
        for h in range(heads):
            base = h * 2 * HD
            at = slice(h * span, (h + 1) * span)
            q = jnp.concatenate([q_ref[prompt + i * slots, at, :] for i in order], axis=0)
            ml = jnp.concatenate([ml_ref[prompt + i * slots, at, :] for i in order], axis=0)
            acc = jnp.concatenate([acc_ref[prompt + i * slots, at, :] for i in order], axis=0)
            s = nt(q, pre_ref[0, :keys, base : base + HD]) * scale
            s = jnp.where(col < length, s, LOW)
            old_top = ml[:, 0:1]
            old_total = ml[:, HD // 2 : HD // 2 + 1]
            top = jnp.maximum(old_top, jnp.max(s, axis=1, keepdims=True))
            e = jnp.exp(s - top)
            carry = jnp.exp(old_top - top)
            total = jnp.sum(e, axis=1, keepdims=True) + carry * old_total
            add = nn(e.astype(jnp.bfloat16), pre_ref[0, :keys, base + HD : base + 2 * HD])
            scr[(n * heads + h) * tall : (n * heads + h + 1) * tall, :] = (add + carry * acc) / total
    tile_rows = members * steps
    for n in range(count):
        for h in range(heads):
            for g in range(group):
                tile = scr[pl.ds((n * heads + h) * tall + g, tile_rows, stride=group), :]
                cols = slice((h * group + g) * HD, (h * group + g + 1) * HD)
                out_ref[n * tile_rows : (n + 1) * tile_rows, cols] = tile.astype(jnp.bfloat16)


def add_slots(grouped, acc, ml, payloads, slots, steps, heads):
    rows, per_row, _ = grouped.shape
    group = per_row // (heads * steps)
    count = len(payloads)
    keys, kvw = payloads[0].shape[1:]
    vmem = pl.BlockSpec(memory_space=pltpu.VMEM)
    shape = (count * rows // slots * steps, heads * group * HD)
    return pl.pallas_call(
        functools.partial(add_slots_kernel, slots, steps, group, count),
        out_shape=jax.ShapeDtypeStruct(shape, jnp.bfloat16),
        in_specs=[vmem] * (count + 3),
        out_specs=vmem,
        scratch_shapes=[pltpu.VMEM((count * rows // slots * per_row, HD), jnp.float32)],
        compiler_params=pltpu.CompilerParams(vmem_limit_bytes=8 << 20),
        cost_estimate=pl.CostEstimate(
            flops=4 * count * rows * per_row * keys * HD // slots,
            bytes_accessed=2 * count * keys * kvw,
            transcendentals=count * rows * per_row * keys // slots,
        ),
        name=f"add_slots_{count}",
    )(*payloads, grouped, acc, ml)


def order_kernel(steps, rows, *refs):
    pre_refs, out_ref = refs[:-1], refs[-1]
    slots = len(pre_refs)
    size = out_ref.shape[0]
    group = size // slots
    place = lax.broadcasted_iota(jnp.int32, (size, size), 0)
    came = lax.broadcasted_iota(jnp.int32, (size, size), 1)
    prompt = jnp.zeros((size, size), jnp.int32)
    for k, pre_ref in enumerate(pre_refs):
        extra = pre_ref[0, pre_ref.shape[1] - EXTRA :, :HD].astype(jnp.float32)
        prompt = jnp.where(came // group == k, jnp.max(extra).astype(jnp.int32), prompt)
    row = prompt + came % group // steps * slots
    hit = place == came % steps * rows + row
    out_ref[...] = jnp.where(hit, 1.0, 0.0).astype(jnp.bfloat16)


def row_order(payloads, steps, rows):
    vmem = pl.BlockSpec(memory_space=pltpu.VMEM)
    return pl.pallas_call(
        functools.partial(order_kernel, steps, rows),
        out_shape=jax.ShapeDtypeStruct((steps * rows, steps * rows), jnp.bfloat16),
        in_specs=[vmem] * len(payloads),
        out_specs=vmem,
        compiler_params=pltpu.CompilerParams(vmem_limit_bytes=4 << 20),
        name="row_order",
    )(*payloads)


def finish_kernel(order_ref, a_ref, b_ref, out_ref):
    total = a_ref[...].astype(jnp.float32) + b_ref[...].astype(jnp.float32)
    out_ref[...] = nn(order_ref[...], total.astype(jnp.bfloat16)).astype(jnp.bfloat16)


def finish(order, a, b):
    vmem = pl.BlockSpec(memory_space=pltpu.VMEM)
    return pl.pallas_call(
        finish_kernel,
        out_shape=jax.ShapeDtypeStruct(a.shape, jnp.bfloat16),
        in_specs=[vmem] * 3,
        out_specs=vmem,
        compiler_params=pltpu.CompilerParams(vmem_limit_bytes=4 << 20),
        name="finish",
    )(order, a, b)


def stack_rows(lhs, refs):
    at = 0
    for ref in refs:
        lhs[at : at + ref.shape[0], :] = ref[...]
        at += ref.shape[0]


def project_first_kernel(parts, chunk, *refs):
    att_refs, (w_ref, out_ref, held_ref, lhs, sems) = refs[:parts], refs[parts:]
    copies = []
    for c in range(w_ref.shape[1] // chunk):
        at = pl.ds(c * chunk, chunk)
        copies.append(pltpu.make_async_copy(w_ref.at[:, at], held_ref.at[:, at], sems.at[c]))
        copies[c].start()
    stack_rows(lhs, att_refs)
    for c in range(w_ref.shape[1] // chunk):
        copies[c].wait()
        at = slice(c * chunk, (c + 1) * chunk)
        out_ref[:, at] = nn(lhs[...], held_ref[:, at])


def project_first(pieces, weight):
    parts = len(pieces)
    tall = sum(piece.shape[0] for piece in pieces)
    width, cols = weight.shape
    chunk = 256
    vmem = pl.BlockSpec(memory_space=pltpu.VMEM)
    return pl.pallas_call(
        functools.partial(project_first_kernel, parts, chunk),
        out_shape=(
            jax.ShapeDtypeStruct((tall, cols), jnp.float32),
            jax.ShapeDtypeStruct(weight.shape, weight.dtype),
        ),
        in_specs=[vmem] * parts + [pl.BlockSpec(memory_space=pl.ANY)],
        out_specs=(vmem, vmem),
        scratch_shapes=[
            pltpu.VMEM((tall, width), jnp.bfloat16),
            pltpu.SemaphoreType.DMA((cols // chunk,)),
        ],
        compiler_params=pltpu.CompilerParams(vmem_limit_bytes=16 << 20),
        cost_estimate=pl.CostEstimate(
            flops=2 * tall * width * cols,
            bytes_accessed=2 * width * cols,
            transcendentals=0,
        ),
        name="project_first",
    )(*pieces, in_hbm(weight))


def project_last_kernel(blocks, parts, pos_ref, *refs):
    att_refs, (first_ref, w_ref, keep_ref, send_ref, lhs, both) = refs[:parts], refs[parts:]
    block = lhs.shape[0]
    half = blocks // 2
    for k in range(blocks - 1):
        both[pos_ref[k]] = first_ref[k * block : (k + 1) * block, :]
    stack_rows(lhs, att_refs)
    both[pos_ref[blocks - 1]] = nn(lhs[...], w_ref[...])
    for k in range(half):
        keep_ref[k] = both[k]
        send_ref[k] = both[half + k]


def project_last(pieces, first, weight, pos, blocks):
    parts = len(pieces)
    block = sum(piece.shape[0] for piece in pieces)
    width, cols = weight.shape
    vmem = pl.BlockSpec(memory_space=pltpu.VMEM)
    shape = jax.ShapeDtypeStruct((blocks // 2, block, cols), jnp.float32)
    return pl.pallas_call(
        functools.partial(project_last_kernel, blocks, parts),
        out_shape=(shape, shape),
        in_specs=[pl.BlockSpec(memory_space=pltpu.SMEM)] + [vmem] * (parts + 2),
        out_specs=(vmem, vmem),
        scratch_shapes=[
            pltpu.VMEM((block, width), jnp.bfloat16),
            pltpu.VMEM((blocks, block, cols), jnp.float32),
        ],
        compiler_params=pltpu.CompilerParams(vmem_limit_bytes=8 << 20),
        cost_estimate=pl.CostEstimate(
            flops=2 * block * width * cols,
            bytes_accessed=2 * width * cols,
            transcendentals=0,
        ),
        name="project_last",
    )(pos, *pieces, first, weight)


def exchange(x, size, flip):
    return lax.ppermute(x, "sample", [(i, i ^ flip) for i in range(size)])


def direct(
    queries, new_kv, gen_kv, prefix_kv, slot_prompt, prefix_blocks, gen_len, out_weight, size
):
    steps, rows, _ = queries.shape
    heads = new_kv.shape[2] // (2 * HD)
    me = lax.axis_index("sample")
    t = lax.axis_index("tensor")
    chip, core = t // 2, t % 2
    flips = (0, 1, 3, 2)
    payload = make_payload(prefix_kv, slot_prompt, prefix_blocks)
    far = exchange(payload, size, 3)
    near = exchange(payload, size, 1)
    grouped, acc, ml = gen_attention(queries, new_kv, gen_kv, gen_len, heads, 4)
    far, grouped, acc, ml = lax.optimization_barrier((far, grouped, acc, ml))
    diag = exchange(far, size, 1)
    most = add_slots(grouped, acc, ml, [payload, near, far], size, steps, heads)
    most_far = exchange(most, size, 3)
    most_near = exchange(most, size, 1)
    diag, _ = lax.optimization_barrier((diag, most))
    rest = add_slots(grouped, acc, ml, [diag], size, steps, heads)
    rest_far = exchange(rest, size, 3)
    rest_near = exchange(rest, size, 1)
    most_far, rest = lax.optimization_barrier((most_far, rest))
    most_diag = exchange(most_far, size, 1)
    rest_diag = exchange(rest_far, size, 1)
    diag, _ = lax.optimization_barrier((diag, rest))
    order = row_order([payload, near, far, diag], steps, rows)
    pieces = [most, rest, most_near, rest_near, most_far, rest_far]
    first, held = project_first(pieces, out_weight)
    most_diag, rest_diag, first, held = lax.optimization_barrier(
        (most_diag, rest_diag, first, held)
    )
    source = jnp.stack([me ^ flip for flip in flips])
    keep, send = project_last([most_diag, rest_diag], first, held, source ^ (2 * core + chip), size)
    got = lax.ppermute(send, "tensor", [(0, 1), (1, 0), (2, 3), (3, 2)])
    halves = (keep + got).astype(jnp.bfloat16)
    arrived = []
    for i in range(2):
        perm = []
        for c in range(size):
            for k in range(size):
                perm.append((c * size + k, (2 * (k % 2) + (i ^ (k // 2))) * size + c))
        piece = lax.ppermute(halves[i], ("sample", "tensor"), perm)
        arrived.append(piece)
    return finish(order, *arrived).reshape(steps, rows, -1)


def split_pairs(cache, heads):
    shaped = cache.reshape(cache.shape[:-1] + (heads, 2, HD))
    return (shaped[..., 0, :], shaped[..., 1, :])


def attend(queries, fresh, cached, prefix, valid, lengths, heads):
    steps_n, rows_n, width = queries.shape
    group = width // (heads * HD)
    scale = HD ** (-0.5)
    q_all = queries.reshape(steps_n, rows_n, heads, group, HD)
    pre_key, pre_val = split_pairs(prefix, heads)
    gen_key, gen_val = split_pairs(cached, heads)
    new_key, new_val = split_pairs(fresh, heads)
    s_pre = (
        jnp.einsum("srkgd,rpkd->srkgp", q_all, pre_key, preferred_element_type=jnp.float32) * scale
    )
    s_gen = (
        jnp.einsum("srkgd,rjkd->srkgj", q_all, gen_key, preferred_element_type=jnp.float32) * scale
    )
    s_new = (
        jnp.einsum("srkgd,urkd->srkgu", q_all, new_key, preferred_element_type=jnp.float32) * scale
    )
    m_pre = (jnp.arange(prefix.shape[1], dtype=jnp.int32)[None, :] < valid[:, None])[
        None, :, None, None, :
    ]
    m_gen = (jnp.arange(cached.shape[1], dtype=jnp.int32)[None, :] < lengths[:, None])[
        None, :, None, None, :
    ]
    order = jnp.arange(steps_n, dtype=jnp.int32)
    m_new = (order[None, :] <= order[:, None])[:, None, None, None, :]
    s_pre = jnp.where(m_pre, s_pre, -jnp.inf)
    s_gen = jnp.where(m_gen, s_gen, -jnp.inf)
    s_new = jnp.where(m_new, s_new, -jnp.inf)
    top = jnp.maximum(
        jnp.maximum(jnp.max(s_pre, -1, keepdims=True), jnp.max(s_gen, -1, keepdims=True)),
        jnp.max(s_new, -1, keepdims=True),
    )
    e_pre = jnp.exp(s_pre - top)
    e_gen = jnp.exp(s_gen - top)
    e_new = jnp.exp(s_new - top)
    total = (
        jnp.sum(e_pre, -1, keepdims=True)
        + jnp.sum(e_gen, -1, keepdims=True)
        + jnp.sum(e_new, -1, keepdims=True)
    )
    w_pre = (e_pre / total).astype(jnp.bfloat16)
    w_gen = (e_gen / total).astype(jnp.bfloat16)
    w_new = (e_new / total).astype(jnp.bfloat16)
    result = jnp.einsum("srkgp,rpkd->srkgd", w_pre, pre_val, preferred_element_type=jnp.float32)
    result = result + jnp.einsum(
        "srkgj,rjkd->srkgd", w_gen, gen_val, preferred_element_type=jnp.float32
    )
    result = result + jnp.einsum(
        "srkgu,urkd->srkgd", w_new, new_val, preferred_element_type=jnp.float32
    )
    return result.reshape(steps_n, rows_n, width).astype(jnp.bfloat16)


def shards(queries, new_kv, gen_kv, prefix_kv, slot_prompt, prefix_blocks, gen_len, out_weight):
    size = lax.axis_size("sample")
    fits = size == 4 and lax.axis_size("tensor") == 4 and prefix_kv.shape[0] == 1
    if fits and queries.shape[0] * queries.shape[1] % (16 * size) == 0:
        return direct(
            queries, new_kv, gen_kv, prefix_kv, slot_prompt, prefix_blocks, gen_len, out_weight, size
        )
    steps_n, rows_n, width = queries.shape
    heads_local = new_kv.shape[2] // (2 * HD)
    all_prefix, all_slots, all_blocks = (
        lax.all_gather(prefix_kv, "sample", axis=0, tiled=True),
        lax.all_gather(slot_prompt, "sample", axis=0, tiled=True),
        lax.all_gather(prefix_blocks, "sample", axis=0, tiled=True),
    )
    prompt_total = all_slots.shape[0]
    inverse = (
        jnp.zeros((prompt_total,), jnp.int32)
        .at[all_slots]
        .set(jnp.arange(prompt_total, dtype=jnp.int32))
    )
    row_ids = lax.axis_index("sample") * rows_n + jnp.arange(rows_n, dtype=jnp.int32)
    picked = inverse[row_ids % prompt_total]
    own_prefix = jnp.take(all_prefix, picked, axis=0)
    valid = jnp.take(all_blocks, picked) * BLOCK
    attended = attend(queries, new_kv, gen_kv, own_prefix, valid, gen_len, heads_local)
    partial_sums = jnp.einsum(
        "srh,hc->src",
        attended,
        lax.all_gather(out_weight, "sample", axis=1, tiled=True),
        preferred_element_type=jnp.float32,
    )
    summed = []
    for step in range(steps_n):
        summed.append(
            lax.psum_scatter(partial_sums[step], "tensor", scatter_dimension=1, tiled=True)
        )
    mixed = jnp.stack(summed, axis=0)
    return mixed.astype(jnp.bfloat16)


def solution(mesh):
    in_specs = (
        P(None, ("groups", "sample"), "tensor"),
        P(None, ("groups", "sample"), "tensor"),
        P(("groups", "sample"), None, "tensor"),
        P(("groups", "sample"), None, "tensor"),
        P(("groups", "sample")),
        P(("groups", "sample")),
        P(("groups", "sample")),
        P("tensor", "sample"),
    )
    out_specs = P(None, ("groups", "sample"), "tensor")
    return jax.shard_map(shards, mesh=mesh, in_specs=in_specs, out_specs=out_specs, check_vma=False)
```

```python
import functools

import jax
import jax.numpy as jnp
from jax import lax
from jax.experimental import pallas as pl
from jax.experimental.pallas import tpu as pltpu
from jax.sharding import PartitionSpec as P


HD = 128
BLOCK = 128
LOW = -1e30
EXTRA = 8


def nt(a, b):
    return lax.dot_general(a, b, (((1,), (1,)), ((), ())), preferred_element_type=jnp.float32)


def nn(a, b):
    return lax.dot_general(a, b, (((1,), (0,)), ((), ())), preferred_element_type=jnp.float32)


def in_hbm(x):
    return pltpu.with_memory_space_constraint(x, pltpu.HBM)


def payload_kernel(prompt_ref, blocks_ref, pre_ref, out_ref, sem):
    keys, kvw = pre_ref.shape[1:]
    copy = pltpu.make_async_copy(pre_ref, out_ref.at[:, pl.ds(0, keys), :], sem)
    copy.start()
    shape = (1, out_ref.shape[1] - keys, kvw // 2)
    out_ref[:, keys:, : kvw // 2] = jnp.full(shape, prompt_ref[0], jnp.float32).astype(jnp.bfloat16)
    out_ref[:, keys:, kvw // 2 :] = jnp.full(shape, blocks_ref[0], jnp.float32).astype(jnp.bfloat16)
    copy.wait()


def make_payload(prefix_kv, slot_prompt, prefix_blocks):
    _, keys, kvw = prefix_kv.shape
    smem = pl.BlockSpec(memory_space=pltpu.SMEM)
    return pl.pallas_call(
        payload_kernel,
        out_shape=jax.ShapeDtypeStruct((1, keys + EXTRA, kvw), prefix_kv.dtype),
        in_specs=[smem, smem, pl.BlockSpec(memory_space=pl.ANY)],
        out_specs=pl.BlockSpec(memory_space=pltpu.VMEM),
        scratch_shapes=[pltpu.SemaphoreType.DMA],
        compiler_params=pltpu.CompilerParams(vmem_limit_bytes=4 << 20),
        name="make_payload",
    )(slot_prompt, prefix_blocks, in_hbm(prefix_kv))


def gen_rows(steps, group, row, len_ref, q_ref, new_ref, kv_ref, acc_ref, ml_ref, q_at):
    batch, keys, kvw = kv_ref.shape
    heads = kvw // (2 * HD)
    span = steps * group
    rows = new_ref.shape[1]
    scale = HD ** (-0.5)
    col = lax.broadcasted_iota(jnp.int32, (span, keys), 1)
    new_col = lax.broadcasted_iota(jnp.int32, (span, steps * rows), 1)
    new_row, new_step = new_col % rows, new_col // rows
    step_of = lax.broadcasted_iota(jnp.int32, (span, steps * rows), 0) // group
    causal = new_step <= step_of
    lane = lax.broadcasted_iota(jnp.int32, (span, HD), 1)
    for h in range(heads):
        base = h * 2 * HD
        at = slice(h * span, (h + 1) * span)
        fresh = new_ref[:, :, base : base + 2 * HD].reshape(steps * rows, 2 * HD)
        qs = [q_ref[q_at + b, at, :] for b in range(batch)]
        scores = [nt(qs[b], kv_ref[b, :, base : base + HD]) for b in range(batch)]
        news = nt(jnp.concatenate(qs, axis=0), fresh[:, :HD])
        exps, new_exps = [], []
        for b in range(batch):
            s = jnp.where(col < len_ref[row + b], scores[b] * scale, LOW)
            n = news[b * span : (b + 1) * span] * scale
            n = jnp.where(causal & (new_row == row + b), n, LOW)
            top = jnp.maximum(
                jnp.max(s, axis=1, keepdims=True), jnp.max(n, axis=1, keepdims=True)
            )
            e, f = jnp.exp(s - top), jnp.exp(n - top)
            total = jnp.sum(e, axis=1, keepdims=True) + jnp.sum(f, axis=1, keepdims=True)
            ml_ref[b, at, :] = jnp.where(lane < HD // 2, top, total)
            exps.append(e.astype(jnp.bfloat16))
            new_exps.append(f.astype(jnp.bfloat16))
        more = nn(jnp.concatenate(new_exps, axis=0), fresh[:, HD:])
        for b in range(batch):
            acc = nn(exps[b], kv_ref[b, :, base + HD : base + 2 * HD])
            acc_ref[b, at, :] = acc + more[b * span : (b + 1) * span]


def gen_kernel(
    steps,
    heads,
    group,
    len_ref,
    q_ref,
    new_ref,
    kv_ref,
    grouped_ref,
    acc_ref,
    ml_ref,
    scr,
):
    rows = q_ref.shape[1]
    span = steps * group
    per_row = heads * span
    batch = kv_ref.shape[0]

    @pl.when(pl.program_id(0) == 0)
    def _():
        for s in range(steps):
            for hg in range(heads * group):
                tile = q_ref[s, :, hg * HD : (hg + 1) * HD].astype(jnp.float32)
                start = (hg // group) * span + s * group + hg % group
                scr[pl.ds(start, rows, stride=per_row), :] = tile
        for r in range(rows):
            grouped_ref[r] = scr[r * per_row : (r + 1) * per_row, :].astype(jnp.bfloat16)

    row = pl.program_id(0) * batch
    gen_rows(steps, group, row, len_ref, grouped_ref, new_ref, kv_ref, acc_ref, ml_ref, row)


def gen_attention(queries, fresh, cached, lengths, heads, batch):
    steps, rows, width = queries.shape
    keys, kvw = cached.shape[1:]
    group = width // (heads * HD)
    per_row = heads * steps * group
    sums = jax.ShapeDtypeStruct((rows, per_row, HD), jnp.float32)
    sum_spec = pl.BlockSpec((batch, per_row, HD), lambda r, n: (r, 0, 0))
    return pl.pallas_call(
        functools.partial(gen_kernel, steps, heads, group),
        out_shape=(
            jax.ShapeDtypeStruct((rows, per_row, HD), jnp.bfloat16),
            sums,
            sums,
        ),
        grid_spec=pltpu.PrefetchScalarGridSpec(
            num_scalar_prefetch=1,
            grid=(rows // batch,),
            in_specs=[
                pl.BlockSpec((steps, rows, width), lambda r, n: (0, 0, 0)),
                pl.BlockSpec((steps, rows, kvw), lambda r, n: (0, 0, 0)),
                pl.BlockSpec((batch, keys, kvw), lambda r, n: (r, 0, 0)),
            ],
            out_specs=[
                pl.BlockSpec((rows, per_row, HD), lambda r, n: (0, 0, 0)),
                sum_spec,
                sum_spec,
            ],
            scratch_shapes=[pltpu.VMEM((rows * per_row, HD), jnp.float32)],
        ),
        compiler_params=pltpu.CompilerParams(vmem_limit_bytes=16 << 20),
        cost_estimate=pl.CostEstimate(
            flops=4 * rows * per_row * keys * HD,
            bytes_accessed=2 * rows * keys * kvw,
            transcendentals=rows * per_row * keys,
        ),
        name="gen_attention",
    )(lengths, in_hbm(queries), in_hbm(fresh), in_hbm(cached))


def add_slots_kernel(slots, steps, group, count, *refs):
    pre_refs, (q_ref, acc_ref, ml_ref, out_ref, scr) = refs[:count], refs[count:]
    rows = q_ref.shape[0]
    keys = pre_refs[0].shape[1] - EXTRA
    kvw = pre_refs[0].shape[2]
    heads = kvw // (2 * HD)
    span = steps * group
    members = rows // slots
    order = range(members)
    tall = members * span
    scale = HD ** (-0.5)
    col = lax.broadcasted_iota(jnp.int32, (tall, keys), 1)
    for n, pre_ref in enumerate(pre_refs):
        extra = pre_ref[0, keys:, :].astype(jnp.float32)
        prompt = jnp.max(extra[:, :HD]).astype(jnp.int32)
        length = jnp.max(extra[:, kvw // 2 : kvw // 2 + HD]).astype(jnp.int32) * BLOCK
        for h in range(heads):
            base = h * 2 * HD
            at = slice(h * span, (h + 1) * span)
            q = jnp.concatenate([q_ref[prompt + i * slots, at, :] for i in order], axis=0)
            ml = jnp.concatenate([ml_ref[prompt + i * slots, at, :] for i in order], axis=0)
            acc = jnp.concatenate([acc_ref[prompt + i * slots, at, :] for i in order], axis=0)
            s = nt(q, pre_ref[0, :keys, base : base + HD]) * scale
            s = jnp.where(col < length, s, LOW)
            old_top = ml[:, 0:1]
            old_total = ml[:, HD // 2 : HD // 2 + 1]
            top = jnp.maximum(old_top, jnp.max(s, axis=1, keepdims=True))
            e = jnp.exp(s - top)
            carry = jnp.exp(old_top - top)
            total = jnp.sum(e, axis=1, keepdims=True) + carry * old_total
            add = nn(e.astype(jnp.bfloat16), pre_ref[0, :keys, base + HD : base + 2 * HD])
            scr[(n * heads + h) * tall : (n * heads + h + 1) * tall, :] = (add + carry * acc) / total
    tile_rows = members * steps
    for n in range(count):
        for h in range(heads):
            for g in range(group):
                tile = scr[pl.ds((n * heads + h) * tall + g, tile_rows, stride=group), :]
                cols = slice((h * group + g) * HD, (h * group + g + 1) * HD)
                out_ref[n * tile_rows : (n + 1) * tile_rows, cols] = tile.astype(jnp.bfloat16)


def add_slots(grouped, acc, ml, payloads, slots, steps, heads):
    rows, per_row, _ = grouped.shape
    group = per_row // (heads * steps)
    count = len(payloads)
    keys, kvw = payloads[0].shape[1:]
    vmem = pl.BlockSpec(memory_space=pltpu.VMEM)
    shape = (count * rows // slots * steps, heads * group * HD)
    return pl.pallas_call(
        functools.partial(add_slots_kernel, slots, steps, group, count),
        out_shape=jax.ShapeDtypeStruct(shape, jnp.bfloat16),
        in_specs=[vmem] * (count + 3),
        out_specs=vmem,
        scratch_shapes=[pltpu.VMEM((count * rows // slots * per_row, HD), jnp.float32)],
        compiler_params=pltpu.CompilerParams(vmem_limit_bytes=8 << 20),
        cost_estimate=pl.CostEstimate(
            flops=4 * count * rows * per_row * keys * HD // slots,
            bytes_accessed=2 * count * keys * kvw,
            transcendentals=count * rows * per_row * keys // slots,
        ),
    )(*payloads, grouped, acc, ml)


def order_kernel(steps, rows, *refs):
    pre_refs, out_ref = refs[:-1], refs[-1]
    slots = len(pre_refs)
    size = out_ref.shape[0]
    group = size // slots
    place = lax.broadcasted_iota(jnp.int32, (size, size), 0)
    came = lax.broadcasted_iota(jnp.int32, (size, size), 1)
    prompt = jnp.zeros((size, size), jnp.int32)
    for k, pre_ref in enumerate(pre_refs):
        extra = pre_ref[0, pre_ref.shape[1] - EXTRA :, :HD].astype(jnp.float32)
        prompt = jnp.where(came // group == k, jnp.max(extra).astype(jnp.int32), prompt)
    row = prompt + came % group // steps * slots
    hit = place == came % steps * rows + row
    out_ref[...] = jnp.where(hit, 1.0, 0.0).astype(jnp.bfloat16)


def row_order(payloads, steps, rows):
    vmem = pl.BlockSpec(memory_space=pltpu.VMEM)
    return pl.pallas_call(
        functools.partial(order_kernel, steps, rows),
        out_shape=jax.ShapeDtypeStruct((steps * rows, steps * rows), jnp.bfloat16),
        in_specs=[vmem] * len(payloads),
        out_specs=vmem,
        compiler_params=pltpu.CompilerParams(vmem_limit_bytes=4 << 20),
        name="row_order",
    )(*payloads)


def finish_kernel(order_ref, a_ref, b_ref, out_ref):
    total = a_ref[...].astype(jnp.float32) + b_ref[...].astype(jnp.float32)
    out_ref[...] = nn(order_ref[...], total.astype(jnp.bfloat16)).astype(jnp.bfloat16)


def finish(order, a, b):
    vmem = pl.BlockSpec(memory_space=pltpu.VMEM)
    return pl.pallas_call(
        finish_kernel,
        out_shape=jax.ShapeDtypeStruct(a.shape, jnp.bfloat16),
        in_specs=[vmem] * 3,
        out_specs=vmem,
        compiler_params=pltpu.CompilerParams(vmem_limit_bytes=4 << 20),
        name="finish",
    )(order, a, b)


def hold_kernel(w_ref, out_ref, sems):
    rows = w_ref.shape[0] // sems.shape[0]
    copies = []
    for c in range(sems.shape[0]):
        at = pl.ds(c * rows, rows)
        copies.append(pltpu.make_async_copy(w_ref.at[at], out_ref.at[at], sems.at[c]))
        copies[c].start()
    for copy in copies:
        copy.wait()


def hold(weight):
    return pl.pallas_call(
        hold_kernel,
        out_shape=jax.ShapeDtypeStruct(weight.shape, weight.dtype),
        in_specs=[pl.BlockSpec(memory_space=pl.ANY)],
        out_specs=pl.BlockSpec(memory_space=pltpu.VMEM),
        scratch_shapes=[pltpu.SemaphoreType.DMA((4,))],
        compiler_params=pltpu.CompilerParams(vmem_limit_bytes=8 << 20),
        name="hold",
    )(in_hbm(weight))


def stack_rows(lhs, refs):
    at = 0
    for ref in refs:
        lhs[at : at + ref.shape[0], :] = ref[...]
        at += ref.shape[0]


def project_first_kernel(parts, *refs):
    att_refs, (w_ref, out_ref, lhs) = refs[:parts], refs[parts:]
    stack_rows(lhs, att_refs)
    out_ref[...] = nn(lhs[...], w_ref[...])


def project_first(pieces, weight):
    parts = len(pieces)
    tall = sum(piece.shape[0] for piece in pieces)
    width, cols = weight.shape
    vmem = pl.BlockSpec(memory_space=pltpu.VMEM)
    return pl.pallas_call(
        functools.partial(project_first_kernel, parts),
        out_shape=jax.ShapeDtypeStruct((tall, cols), jnp.float32),
        in_specs=[vmem] * (parts + 1),
        out_specs=vmem,
        scratch_shapes=[pltpu.VMEM((tall, width), jnp.bfloat16)],
        compiler_params=pltpu.CompilerParams(vmem_limit_bytes=8 << 20),
        cost_estimate=pl.CostEstimate(
            flops=2 * tall * width * cols,
            bytes_accessed=2 * width * cols,
            transcendentals=0,
        ),
        name="project_first",
    )(*pieces, weight)


def project_last_kernel(blocks, first_homes, homes, pos_ref, *refs):
    parts = len(homes)
    att_refs, (first_ref, w_ref, keep_ref, send_ref, lhs, both) = refs[:parts], refs[parts:]
    at = 0
    for home, start, size in first_homes:
        both[pos_ref[home], start : start + size, :] = first_ref[at : at + size, :]
        at += size
    stack_rows(lhs, att_refs)
    sums = nn(lhs[...], w_ref[...])
    at = 0
    for home, start, size in homes:
        both[pos_ref[home], start : start + size, :] = sums[at : at + size]
        at += size
    half = blocks // 2
    for k in range(half):
        keep_ref[k] = both[k]
        send_ref[k] = both[half + k]


def project_last(pieces, homes, first, first_homes, weight, pos, block):
    tall = sum(piece.shape[0] for piece in pieces)
    blocks = pos.shape[0]
    width, cols = weight.shape
    vmem = pl.BlockSpec(memory_space=pltpu.VMEM)
    shape = jax.ShapeDtypeStruct((blocks // 2, block, cols), jnp.float32)
    return pl.pallas_call(
        functools.partial(project_last_kernel, blocks, first_homes, homes),
        out_shape=(shape, shape),
        in_specs=[pl.BlockSpec(memory_space=pltpu.SMEM)] + [vmem] * (len(pieces) + 2),
        out_specs=(vmem, vmem),
        scratch_shapes=[
            pltpu.VMEM((tall, width), jnp.bfloat16),
            pltpu.VMEM((blocks, block, cols), jnp.float32),
        ],
        compiler_params=pltpu.CompilerParams(vmem_limit_bytes=8 << 20),
        cost_estimate=pl.CostEstimate(
            flops=2 * tall * width * cols,
            bytes_accessed=2 * width * cols,
            transcendentals=0,
        ),
        name="project_last",
    )(pos, *pieces, first, weight)


def exchange(x, size, flip):
    return lax.ppermute(x, "sample", [(i, i ^ flip) for i in range(size)])


def direct(
    queries, new_kv, gen_kv, prefix_kv, slot_prompt, prefix_blocks, gen_len, out_weight, size
):
    steps, rows, _ = queries.shape
    heads = new_kv.shape[2] // (2 * HD)
    me = lax.axis_index("sample")
    t = lax.axis_index("tensor")
    chip, core = t // 2, t % 2
    flips = (0, 1, 3, 2)
    payload = make_payload(prefix_kv, slot_prompt, prefix_blocks)
    far = exchange(payload, size, 3)
    near = exchange(payload, size, 1)
    grouped, acc, ml = gen_attention(queries, new_kv, gen_kv, gen_len, heads, 4)
    far, grouped, acc, ml = lax.optimization_barrier((far, grouped, acc, ml))
    diag = exchange(far, size, 1)
    most = add_slots(grouped, acc, ml, [payload, near, far], size, steps, heads)
    most_far = exchange(most, size, 3)
    most_near = exchange(most, size, 1)
    diag, _ = lax.optimization_barrier((diag, most))
    rest = add_slots(grouped, acc, ml, [diag], size, steps, heads)
    rest_far = exchange(rest, size, 3)
    rest_near = exchange(rest, size, 1)
    most_diag = exchange(most_far, size, 1)
    rest_diag = exchange(rest, size, 2)
    order = row_order([payload, near, far, diag], steps, rows)
    much, little = most.shape[0], rest.shape[0]
    held = hold(out_weight)
    first = project_first([most, rest, most_far, most_near], held)
    first_homes = ((0, 0, much), (0, much, little), (2, 0, much), (1, 0, much))
    last = [rest_far, rest_near, rest_diag, most_diag]
    homes = ((2, much, little), (1, much, little), (3, much, little), (3, 0, much))
    *last, first = lax.optimization_barrier((*last, first))
    pos = jnp.stack([me ^ flip for flip in flips]) ^ (2 * core + chip)
    keep, send = project_last(last, homes, first, first_homes, held, pos, much + little)
    got = lax.ppermute(send, "tensor", [(0, 1), (1, 0), (2, 3), (3, 2)])
    halves = (keep + got).astype(jnp.bfloat16)
    arrived = []
    for i in range(2):
        perm = []
        for c in range(size):
            for k in range(size):
                perm.append((c * size + k, (2 * (k % 2) + (i ^ (k // 2))) * size + c))
        piece = lax.ppermute(halves[i], ("sample", "tensor"), perm)
        arrived.append(piece)
    return finish(order, *arrived).reshape(steps, rows, -1)


def split_pairs(cache, heads):
    shaped = cache.reshape(cache.shape[:-1] + (heads, 2, HD))
    return (shaped[..., 0, :], shaped[..., 1, :])


def attend(queries, fresh, cached, prefix, valid, lengths, heads):
    steps_n, rows_n, width = queries.shape
    group = width // (heads * HD)
    scale = HD ** (-0.5)
    q_all = queries.reshape(steps_n, rows_n, heads, group, HD)
    pre_key, pre_val = split_pairs(prefix, heads)
    gen_key, gen_val = split_pairs(cached, heads)
    new_key, new_val = split_pairs(fresh, heads)
    s_pre = (
        jnp.einsum("srkgd,rpkd->srkgp", q_all, pre_key, preferred_element_type=jnp.float32) * scale
    )
    s_gen = (
        jnp.einsum("srkgd,rjkd->srkgj", q_all, gen_key, preferred_element_type=jnp.float32) * scale
    )
    s_new = (
        jnp.einsum("srkgd,urkd->srkgu", q_all, new_key, preferred_element_type=jnp.float32) * scale
    )
    m_pre = (jnp.arange(prefix.shape[1], dtype=jnp.int32)[None, :] < valid[:, None])[
        None, :, None, None, :
    ]
    m_gen = (jnp.arange(cached.shape[1], dtype=jnp.int32)[None, :] < lengths[:, None])[
        None, :, None, None, :
    ]
    order = jnp.arange(steps_n, dtype=jnp.int32)
    m_new = (order[None, :] <= order[:, None])[:, None, None, None, :]
    s_pre = jnp.where(m_pre, s_pre, -jnp.inf)
    s_gen = jnp.where(m_gen, s_gen, -jnp.inf)
    s_new = jnp.where(m_new, s_new, -jnp.inf)
    top = jnp.maximum(
        jnp.maximum(jnp.max(s_pre, -1, keepdims=True), jnp.max(s_gen, -1, keepdims=True)),
        jnp.max(s_new, -1, keepdims=True),
    )
    e_pre = jnp.exp(s_pre - top)
    e_gen = jnp.exp(s_gen - top)
    e_new = jnp.exp(s_new - top)
    total = (
        jnp.sum(e_pre, -1, keepdims=True)
        + jnp.sum(e_gen, -1, keepdims=True)
        + jnp.sum(e_new, -1, keepdims=True)
    )
    w_pre = (e_pre / total).astype(jnp.bfloat16)
    w_gen = (e_gen / total).astype(jnp.bfloat16)
    w_new = (e_new / total).astype(jnp.bfloat16)
    result = jnp.einsum("srkgp,rpkd->srkgd", w_pre, pre_val, preferred_element_type=jnp.float32)
    result = result + jnp.einsum(
        "srkgj,rjkd->srkgd", w_gen, gen_val, preferred_element_type=jnp.float32
    )
    result = result + jnp.einsum(
        "srkgu,urkd->srkgd", w_new, new_val, preferred_element_type=jnp.float32
    )
    return result.reshape(steps_n, rows_n, width).astype(jnp.bfloat16)


def shards(queries, new_kv, gen_kv, prefix_kv, slot_prompt, prefix_blocks, gen_len, out_weight):
    size = lax.axis_size("sample")
    fits = size == 4 and lax.axis_size("tensor") == 4 and prefix_kv.shape[0] == 1
    if fits and queries.shape[0] * queries.shape[1] % (16 * size) == 0:
        return direct(
            queries, new_kv, gen_kv, prefix_kv, slot_prompt, prefix_blocks, gen_len, out_weight, size
        )
    steps_n, rows_n, _ = queries.shape
    heads_local = new_kv.shape[2] // (2 * HD)
    all_prefix, all_slots, all_blocks = (
        lax.all_gather(prefix_kv, "sample", axis=0, tiled=True),
        lax.all_gather(slot_prompt, "sample", axis=0, tiled=True),
        lax.all_gather(prefix_blocks, "sample", axis=0, tiled=True),
    )
    prompt_total = all_slots.shape[0]
    inverse = (
        jnp.zeros((prompt_total,), jnp.int32)
        .at[all_slots]
        .set(jnp.arange(prompt_total, dtype=jnp.int32))
    )
    row_ids = lax.axis_index("sample") * rows_n + jnp.arange(rows_n, dtype=jnp.int32)
    picked = inverse[row_ids % prompt_total]
    own_prefix = jnp.take(all_prefix, picked, axis=0)
    valid = jnp.take(all_blocks, picked) * BLOCK
    attended = attend(queries, new_kv, gen_kv, own_prefix, valid, gen_len, heads_local)
    partial_sums = jnp.einsum(
        "srh,hc->src",
        attended,
        lax.all_gather(out_weight, "sample", axis=1, tiled=True),
        preferred_element_type=jnp.float32,
    )
    summed = []
    for step in range(steps_n):
        summed.append(
            lax.psum_scatter(partial_sums[step], "tensor", scatter_dimension=1, tiled=True)
        )
    mixed = jnp.stack(summed, axis=0)
    return mixed.astype(jnp.bfloat16)


def solution(mesh):
    in_specs = (
        P(None, ("groups", "sample"), "tensor"),
        P(None, ("groups", "sample"), "tensor"),
        P(("groups", "sample"), None, "tensor"),
        P(("groups", "sample"), None, "tensor"),
        P(("groups", "sample")),
        P(("groups", "sample")),
        P(("groups", "sample")),
        P("tensor", "sample"),
    )
    out_specs = P(None, ("groups", "sample"), "tensor")
    return jax.shard_map(
        shards, mesh=mesh, in_specs=in_specs, out_specs=out_specs, check_vma=False
    )
```

```python
import functools

import jax
import jax.numpy as jnp
from jax import lax
from jax.experimental import pallas as pl
from jax.experimental.pallas import tpu as pltpu
from jax.sharding import PartitionSpec as P


HD = 128
BLOCK = 128
LOW = -1e30
EXTRA = 8
MIX = 3


def nt(a, b):
    return lax.dot_general(a, b, (((1,), (1,)), ((), ())), preferred_element_type=jnp.float32)


def nn(a, b):
    return lax.dot_general(a, b, (((1,), (0,)), ((), ())), preferred_element_type=jnp.float32)


def in_hbm(x):
    return pltpu.with_memory_space_constraint(x, pltpu.HBM)


def payload_kernel(prompt_ref, blocks_ref, pre_ref, out_ref, sem):
    keys, kvw = pre_ref.shape[1:]
    copy = pltpu.make_async_copy(pre_ref, out_ref.at[:, pl.ds(0, keys), :], sem)
    copy.start()
    shape = (1, out_ref.shape[1] - keys, kvw // 2)
    out_ref[:, keys:, : kvw // 2] = jnp.full(shape, prompt_ref[0], jnp.float32).astype(jnp.bfloat16)
    out_ref[:, keys:, kvw // 2 :] = jnp.full(shape, blocks_ref[0], jnp.float32).astype(jnp.bfloat16)
    copy.wait()


def make_payload(prefix_kv, slot_prompt, prefix_blocks):
    _, keys, kvw = prefix_kv.shape
    smem = pl.BlockSpec(memory_space=pltpu.SMEM)
    return pl.pallas_call(
        payload_kernel,
        out_shape=jax.ShapeDtypeStruct((1, keys + EXTRA, kvw), prefix_kv.dtype),
        in_specs=[smem, smem, pl.BlockSpec(memory_space=pl.ANY)],
        out_specs=pl.BlockSpec(memory_space=pltpu.VMEM),
        scratch_shapes=[pltpu.SemaphoreType.DMA],
        compiler_params=pltpu.CompilerParams(vmem_limit_bytes=4 << 20),
        name="make_payload",
    )(slot_prompt, prefix_blocks, in_hbm(prefix_kv))


def gen_rows(steps, group, row, len_ref, q_ref, new_ref, kv_ref, acc_ref, ml_ref, q_at):
    batch, keys, kvw = kv_ref.shape
    heads = kvw // (2 * HD)
    span = steps * group
    rows = new_ref.shape[1]
    scale = HD ** (-0.5)
    col = lax.broadcasted_iota(jnp.int32, (span, keys), 1)
    new_col = lax.broadcasted_iota(jnp.int32, (span, steps * rows), 1)
    new_row, new_step = new_col % rows, new_col // rows
    step_of = lax.broadcasted_iota(jnp.int32, (span, steps * rows), 0) // group
    causal = new_step <= step_of
    lane = lax.broadcasted_iota(jnp.int32, (span, HD), 1)
    for h in range(heads):
        base = h * 2 * HD
        at = slice(h * span, (h + 1) * span)
        fresh = new_ref[:, :, base : base + 2 * HD].reshape(steps * rows, 2 * HD)
        qs = [q_ref[q_at + b, at, :] for b in range(batch)]
        scores = [nt(qs[b], kv_ref[b, :, base : base + HD]) for b in range(batch)]
        news = nt(jnp.concatenate(qs, axis=0), fresh[:, :HD])
        exps, new_exps = [], []
        for b in range(batch):
            s = jnp.where(col < len_ref[row + b], scores[b] * scale, LOW)
            n = news[b * span : (b + 1) * span] * scale
            n = jnp.where(causal & (new_row == row + b), n, LOW)
            top = jnp.maximum(
                jnp.max(s, axis=1, keepdims=True), jnp.max(n, axis=1, keepdims=True)
            )
            e, f = jnp.exp(s - top), jnp.exp(n - top)
            total = jnp.sum(e, axis=1, keepdims=True) + jnp.sum(f, axis=1, keepdims=True)
            ml_ref[b, at, :] = jnp.where(lane < HD // 2, top, total)
            exps.append(e.astype(jnp.bfloat16))
            new_exps.append(f.astype(jnp.bfloat16))
        more = nn(jnp.concatenate(new_exps, axis=0), fresh[:, HD:])
        for b in range(batch):
            acc = nn(exps[b], kv_ref[b, :, base + HD : base + 2 * HD])
            acc_ref[b, at, :] = acc + more[b * span : (b + 1) * span]


def gen_kernel(
    steps,
    heads,
    group,
    len_ref,
    q_ref,
    new_ref,
    kv_ref,
    grouped_ref,
    acc_ref,
    ml_ref,
    scr,
):
    rows = q_ref.shape[1]
    span = steps * group
    per_row = heads * span
    batch = kv_ref.shape[0]

    @pl.when(pl.program_id(0) == 0)
    def _():
        for s in range(steps):
            for hg in range(heads * group):
                tile = q_ref[s, :, hg * HD : (hg + 1) * HD].astype(jnp.float32)
                start = (hg // group) * span + s * group + hg % group
                scr[pl.ds(start, rows, stride=per_row), :] = tile
        for r in range(rows):
            grouped_ref[r] = scr[r * per_row : (r + 1) * per_row, :].astype(jnp.bfloat16)

    row = pl.program_id(0) * batch
    gen_rows(steps, group, row, len_ref, grouped_ref, new_ref, kv_ref, acc_ref, ml_ref, row)


def gen_attention(queries, fresh, cached, lengths, heads, batch):
    steps, rows, width = queries.shape
    keys, kvw = cached.shape[1:]
    group = width // (heads * HD)
    per_row = heads * steps * group
    sums = jax.ShapeDtypeStruct((rows, per_row, HD), jnp.float32)
    sum_spec = pl.BlockSpec((batch, per_row, HD), lambda r, n: (r, 0, 0))
    return pl.pallas_call(
        functools.partial(gen_kernel, steps, heads, group),
        out_shape=(
            jax.ShapeDtypeStruct((rows, per_row, HD), jnp.bfloat16),
            sums,
            sums,
        ),
        grid_spec=pltpu.PrefetchScalarGridSpec(
            num_scalar_prefetch=1,
            grid=(rows // batch,),
            in_specs=[
                pl.BlockSpec((steps, rows, width), lambda r, n: (0, 0, 0)),
                pl.BlockSpec((steps, rows, kvw), lambda r, n: (0, 0, 0)),
                pl.BlockSpec((batch, keys, kvw), lambda r, n: (r, 0, 0)),
            ],
            out_specs=[
                pl.BlockSpec((rows, per_row, HD), lambda r, n: (0, 0, 0)),
                sum_spec,
                sum_spec,
            ],
            scratch_shapes=[pltpu.VMEM((rows * per_row, HD), jnp.float32)],
        ),
        compiler_params=pltpu.CompilerParams(vmem_limit_bytes=16 << 20),
        cost_estimate=pl.CostEstimate(
            flops=4 * rows * per_row * keys * HD,
            bytes_accessed=2 * rows * keys * kvw,
            transcendentals=rows * per_row * keys,
        ),
        name="gen_attention",
    )(lengths, in_hbm(queries), in_hbm(fresh), in_hbm(cached))


def add_slots_kernel(slots, steps, group, count, *refs):
    pre_refs, (q_ref, acc_ref, ml_ref, out_ref, scr) = refs[:count], refs[count:]
    rows = q_ref.shape[0]
    keys = pre_refs[0].shape[1] - EXTRA
    kvw = pre_refs[0].shape[2]
    heads = kvw // (2 * HD)
    span = steps * group
    members = rows // slots
    order = range(members)
    tall = members * span
    scale = HD ** (-0.5)
    col = lax.broadcasted_iota(jnp.int32, (tall, keys), 1)
    for n, pre_ref in enumerate(pre_refs):
        extra = pre_ref[0, keys:, :].astype(jnp.float32)
        prompt = jnp.max(extra[:, :HD]).astype(jnp.int32)
        length = jnp.max(extra[:, kvw // 2 : kvw // 2 + HD]).astype(jnp.int32) * BLOCK
        for h in range(heads):
            base = h * 2 * HD
            at = slice(h * span, (h + 1) * span)
            q = jnp.concatenate([q_ref[prompt + i * slots, at, :] for i in order], axis=0)
            ml = jnp.concatenate([ml_ref[prompt + i * slots, at, :] for i in order], axis=0)
            acc = jnp.concatenate([acc_ref[prompt + i * slots, at, :] for i in order], axis=0)
            s = nt(q, pre_ref[0, :keys, base : base + HD]) * scale
            s = jnp.where(col < length, s, LOW)
            old_top = ml[:, 0:1]
            old_total = ml[:, HD // 2 : HD // 2 + 1]
            top = jnp.maximum(old_top, jnp.max(s, axis=1, keepdims=True))
            e = jnp.exp(s - top)
            carry = jnp.exp(old_top - top)
            total = jnp.sum(e, axis=1, keepdims=True) + carry * old_total
            add = nn(e.astype(jnp.bfloat16), pre_ref[0, :keys, base + HD : base + 2 * HD])
            scr[(n * heads + h) * tall : (n * heads + h + 1) * tall, :] = (add + carry * acc) / total
    tile_rows = members * steps
    for n in range(count):
        for h in range(heads):
            for g in range(group):
                tile = scr[pl.ds((n * heads + h) * tall + g, tile_rows, stride=group), :]
                cols = slice((h * group + g) * HD, (h * group + g + 1) * HD)
                out_ref[n * tile_rows : (n + 1) * tile_rows, cols] = tile.astype(jnp.bfloat16)


def add_slots(grouped, acc, ml, payloads, slots, steps, heads):
    rows, per_row, _ = grouped.shape
    group = per_row // (heads * steps)
    count = len(payloads)
    keys, kvw = payloads[0].shape[1:]
    vmem = pl.BlockSpec(memory_space=pltpu.VMEM)
    shape = (count * rows // slots * steps, heads * group * HD)
    return pl.pallas_call(
        functools.partial(add_slots_kernel, slots, steps, group, count),
        out_shape=jax.ShapeDtypeStruct(shape, jnp.bfloat16),
        in_specs=[vmem] * (count + 3),
        out_specs=vmem,
        scratch_shapes=[pltpu.VMEM((count * rows // slots * per_row, HD), jnp.float32)],
        compiler_params=pltpu.CompilerParams(vmem_limit_bytes=8 << 20),
        cost_estimate=pl.CostEstimate(
            flops=4 * count * rows * per_row * keys * HD // slots,
            bytes_accessed=2 * count * keys * kvw,
            transcendentals=count * rows * per_row * keys // slots,
        ),
    )(*payloads, grouped, acc, ml)


def order_kernel(steps, rows, *refs):
    pre_refs, out_ref = refs[:-1], refs[-1]
    slots = len(pre_refs)
    size = out_ref.shape[0]
    group = size // slots
    place = lax.broadcasted_iota(jnp.int32, (size, size), 0)
    came = lax.broadcasted_iota(jnp.int32, (size, size), 1)
    prompt = jnp.zeros((size, size), jnp.int32)
    for k, pre_ref in enumerate(pre_refs):
        extra = pre_ref[0, pre_ref.shape[1] - EXTRA :, :HD].astype(jnp.float32)
        prompt = jnp.where(came // group == k, jnp.max(extra).astype(jnp.int32), prompt)
    row = prompt + came % group // steps * slots
    hit = place == came % steps * rows + row
    out_ref[...] = jnp.where(hit, 1.0, 0.0).astype(jnp.bfloat16)


def row_order(payloads, steps, rows):
    vmem = pl.BlockSpec(memory_space=pltpu.VMEM)
    return pl.pallas_call(
        functools.partial(order_kernel, steps, rows),
        out_shape=jax.ShapeDtypeStruct((steps * rows, steps * rows), jnp.bfloat16),
        in_specs=[vmem] * len(payloads),
        out_specs=vmem,
        compiler_params=pltpu.CompilerParams(vmem_limit_bytes=4 << 20),
        name="row_order",
    )(*payloads)


def finish_kernel(order_ref, a_ref, b_ref, out_ref):
    total = a_ref[...].astype(jnp.float32) + b_ref[...].astype(jnp.float32)
    out_ref[...] = nn(order_ref[...], total.astype(jnp.bfloat16)).astype(jnp.bfloat16)


def finish(order, a, b):
    vmem = pl.BlockSpec(memory_space=pltpu.VMEM)
    return pl.pallas_call(
        finish_kernel,
        out_shape=jax.ShapeDtypeStruct(a.shape, jnp.bfloat16),
        in_specs=[vmem] * 3,
        out_specs=vmem,
        compiler_params=pltpu.CompilerParams(vmem_limit_bytes=4 << 20),
        name="finish",
    )(order, a, b)


def hold_kernel(w_ref, out_ref, sems):
    rows = w_ref.shape[0] // sems.shape[0]
    copies = []
    for c in range(sems.shape[0]):
        at = pl.ds(c * rows, rows)
        copies.append(pltpu.make_async_copy(w_ref.at[at], out_ref.at[at], sems.at[c]))
        copies[c].start()
    for copy in copies:
        copy.wait()


def hold(weight):
    return pl.pallas_call(
        hold_kernel,
        out_shape=jax.ShapeDtypeStruct(weight.shape, weight.dtype),
        in_specs=[pl.BlockSpec(memory_space=pl.ANY)],
        out_specs=pl.BlockSpec(memory_space=pltpu.VMEM),
        scratch_shapes=[pltpu.SemaphoreType.DMA((4,))],
        compiler_params=pltpu.CompilerParams(vmem_limit_bytes=8 << 20),
        name="hold",
    )(in_hbm(weight))


def stack_rows(lhs, refs):
    at = 0
    for ref in refs:
        lhs[at : at + ref.shape[0], :] = ref[...]
        at += ref.shape[0]


def project_first_kernel(parts, *refs):
    att_refs, (w_ref, out_ref, lhs) = refs[:parts], refs[parts:]
    stack_rows(lhs, att_refs)
    out_ref[...] = nn(lhs[...], w_ref[...])


def project_first(pieces, weight):
    parts = len(pieces)
    tall = sum(piece.shape[0] for piece in pieces)
    width, cols = weight.shape
    vmem = pl.BlockSpec(memory_space=pltpu.VMEM)
    return pl.pallas_call(
        functools.partial(project_first_kernel, parts),
        out_shape=jax.ShapeDtypeStruct((tall, cols), jnp.float32),
        in_specs=[vmem] * (parts + 1),
        out_specs=vmem,
        scratch_shapes=[pltpu.VMEM((tall, width), jnp.bfloat16)],
        compiler_params=pltpu.CompilerParams(vmem_limit_bytes=8 << 20),
        cost_estimate=pl.CostEstimate(
            flops=2 * tall * width * cols,
            bytes_accessed=2 * width * cols,
            transcendentals=0,
        ),
        name="project_first",
    )(*pieces, weight)


def project_last_kernel(blocks, first_homes, homes, pos_ref, *refs):
    parts = len(homes)
    att_refs, (first_ref, w_ref, keep_ref, send_ref, lhs, both) = refs[:parts], refs[parts:]
    at = 0
    for home, start, size in first_homes:
        both[pos_ref[home], start : start + size, :] = first_ref[at : at + size, :]
        at += size
    stack_rows(lhs, att_refs)
    sums = nn(lhs[...], w_ref[...])
    at = 0
    for home, start, size in homes:
        both[pos_ref[home], start : start + size, :] = sums[at : at + size]
        at += size
    half = blocks // 2
    for k in range(half):
        keep_ref[k] = both[k]
        send_ref[k] = both[half + k]


def project_last(pieces, homes, first, first_homes, weight, pos, block):
    tall = sum(piece.shape[0] for piece in pieces)
    blocks = pos.shape[0]
    width, cols = weight.shape
    vmem = pl.BlockSpec(memory_space=pltpu.VMEM)
    shape = jax.ShapeDtypeStruct((blocks // 2, block, cols), jnp.float32)
    return pl.pallas_call(
        functools.partial(project_last_kernel, blocks, first_homes, homes),
        out_shape=(shape, shape),
        in_specs=[pl.BlockSpec(memory_space=pltpu.SMEM)] + [vmem] * (len(pieces) + 2),
        out_specs=(vmem, vmem),
        scratch_shapes=[
            pltpu.VMEM((tall, width), jnp.bfloat16),
            pltpu.VMEM((blocks, block, cols), jnp.float32),
        ],
        compiler_params=pltpu.CompilerParams(vmem_limit_bytes=8 << 20),
        cost_estimate=pl.CostEstimate(
            flops=2 * tall * width * cols,
            bytes_accessed=2 * width * cols,
            transcendentals=0,
        ),
        name="project_last",
    )(pos, *pieces, first, weight)


def exchange(x, size, flip):
    return lax.ppermute(x, "sample", [(i, i ^ flip) for i in range(size)])


def direct(
    queries, new_kv, gen_kv, prefix_kv, slot_prompt, prefix_blocks, gen_len, out_weight, size
):
    steps, rows, _ = queries.shape
    heads = new_kv.shape[2] // (2 * HD)
    me = lax.axis_index("sample")
    t = lax.axis_index("tensor")
    chip, core = t // 2, t % 2
    flips = (0, 1, 3, 2)
    payload = make_payload(prefix_kv, slot_prompt, prefix_blocks)
    far = exchange(payload, size, 3)
    near = exchange(payload, size, 1)
    grouped, acc, ml = gen_attention(queries, new_kv, gen_kv, gen_len, heads, 4)
    far, grouped, acc, ml = lax.optimization_barrier((far, grouped, acc, ml))
    diag = exchange(far, size, 1)
    most = add_slots(grouped, acc, ml, [payload, near, far], size, steps, heads)
    most_far = exchange(most, size, 3)
    most_near = exchange(most, size, 1)
    diag, _ = lax.optimization_barrier((diag, most))
    rest = add_slots(grouped, acc, ml, [diag], size, steps, heads)
    rest_far = exchange(rest, size, 3)
    rest_near = exchange(rest, size, 1)
    most_diag = exchange(most_far, size, 1)
    rest_diag = exchange(rest, size, 2)
    order = row_order([payload, near, far, diag], steps, rows)
    much, little = most.shape[0], rest.shape[0]
    held = hold(out_weight)
    first = project_first([most, rest, most_far, most_near], held)
    first_homes = ((0, 0, much), (0, much, little), (2, 0, much), (1, 0, much))
    last = [rest_far, rest_near, rest_diag, most_diag]
    homes = ((2, much, little), (1, much, little), (3, much, little), (3, 0, much))
    *last, first = lax.optimization_barrier((*last, first))
    pos = jnp.stack([me ^ flip for flip in flips]) ^ (2 * core + chip) ^ MIX
    keep, send = project_last(last, homes, first, first_homes, held, pos, much + little)
    got = lax.ppermute(send, "tensor", [(0, 1), (1, 0), (2, 3), (3, 2)])
    halves = (keep + got).astype(jnp.bfloat16)
    arrived = []
    for i in range(2):
        perm = []
        for c in range(size):
            for k in range(size):
                perm.append((c * size + k, (2 * (k % 2) + (i ^ (k // 2)) ^ MIX) * size + c))
        piece = lax.ppermute(halves[i], ("sample", "tensor"), perm)
        arrived.append(piece)
    return finish(order, *arrived).reshape(steps, rows, -1)


def split_pairs(cache, heads):
    shaped = cache.reshape(cache.shape[:-1] + (heads, 2, HD))
    return (shaped[..., 0, :], shaped[..., 1, :])


def attend(queries, fresh, cached, prefix, valid, lengths, heads):
    steps_n, rows_n, width = queries.shape
    group = width // (heads * HD)
    scale = HD ** (-0.5)
    q_all = queries.reshape(steps_n, rows_n, heads, group, HD)
    pre_key, pre_val = split_pairs(prefix, heads)
    gen_key, gen_val = split_pairs(cached, heads)
    new_key, new_val = split_pairs(fresh, heads)
    s_pre = (
        jnp.einsum("srkgd,rpkd->srkgp", q_all, pre_key, preferred_element_type=jnp.float32) * scale
    )
    s_gen = (
        jnp.einsum("srkgd,rjkd->srkgj", q_all, gen_key, preferred_element_type=jnp.float32) * scale
    )
    s_new = (
        jnp.einsum("srkgd,urkd->srkgu", q_all, new_key, preferred_element_type=jnp.float32) * scale
    )
    m_pre = (jnp.arange(prefix.shape[1], dtype=jnp.int32)[None, :] < valid[:, None])[
        None, :, None, None, :
    ]
    m_gen = (jnp.arange(cached.shape[1], dtype=jnp.int32)[None, :] < lengths[:, None])[
        None, :, None, None, :
    ]
    order = jnp.arange(steps_n, dtype=jnp.int32)
    m_new = (order[None, :] <= order[:, None])[:, None, None, None, :]
    s_pre = jnp.where(m_pre, s_pre, -jnp.inf)
    s_gen = jnp.where(m_gen, s_gen, -jnp.inf)
    s_new = jnp.where(m_new, s_new, -jnp.inf)
    top = jnp.maximum(
        jnp.maximum(jnp.max(s_pre, -1, keepdims=True), jnp.max(s_gen, -1, keepdims=True)),
        jnp.max(s_new, -1, keepdims=True),
    )
    e_pre = jnp.exp(s_pre - top)
    e_gen = jnp.exp(s_gen - top)
    e_new = jnp.exp(s_new - top)
    total = (
        jnp.sum(e_pre, -1, keepdims=True)
        + jnp.sum(e_gen, -1, keepdims=True)
        + jnp.sum(e_new, -1, keepdims=True)
    )
    w_pre = (e_pre / total).astype(jnp.bfloat16)
    w_gen = (e_gen / total).astype(jnp.bfloat16)
    w_new = (e_new / total).astype(jnp.bfloat16)
    result = jnp.einsum("srkgp,rpkd->srkgd", w_pre, pre_val, preferred_element_type=jnp.float32)
    result = result + jnp.einsum(
        "srkgj,rjkd->srkgd", w_gen, gen_val, preferred_element_type=jnp.float32
    )
    result = result + jnp.einsum(
        "srkgu,urkd->srkgd", w_new, new_val, preferred_element_type=jnp.float32
    )
    return result.reshape(steps_n, rows_n, width).astype(jnp.bfloat16)


def shards(queries, new_kv, gen_kv, prefix_kv, slot_prompt, prefix_blocks, gen_len, out_weight):
    size = lax.axis_size("sample")
    fits = size == 4 and lax.axis_size("tensor") == 4 and prefix_kv.shape[0] == 1
    if fits and queries.shape[0] * queries.shape[1] % (16 * size) == 0:
        return direct(
            queries, new_kv, gen_kv, prefix_kv, slot_prompt, prefix_blocks, gen_len, out_weight, size
        )
    steps_n, rows_n, _ = queries.shape
    heads_local = new_kv.shape[2] // (2 * HD)
    all_prefix, all_slots, all_blocks = (
        lax.all_gather(prefix_kv, "sample", axis=0, tiled=True),
        lax.all_gather(slot_prompt, "sample", axis=0, tiled=True),
        lax.all_gather(prefix_blocks, "sample", axis=0, tiled=True),
    )
    prompt_total = all_slots.shape[0]
    inverse = (
        jnp.zeros((prompt_total,), jnp.int32)
        .at[all_slots]
        .set(jnp.arange(prompt_total, dtype=jnp.int32))
    )
    row_ids = lax.axis_index("sample") * rows_n + jnp.arange(rows_n, dtype=jnp.int32)
    picked = inverse[row_ids % prompt_total]
    own_prefix = jnp.take(all_prefix, picked, axis=0)
    valid = jnp.take(all_blocks, picked) * BLOCK
    attended = attend(queries, new_kv, gen_kv, own_prefix, valid, gen_len, heads_local)
    partial_sums = jnp.einsum(
        "srh,hc->src",
        attended,
        lax.all_gather(out_weight, "sample", axis=1, tiled=True),
        preferred_element_type=jnp.float32,
    )
    summed = []
    for step in range(steps_n):
        summed.append(
            lax.psum_scatter(partial_sums[step], "tensor", scatter_dimension=1, tiled=True)
        )
    mixed = jnp.stack(summed, axis=0)
    return mixed.astype(jnp.bfloat16)


def solution(mesh):
    in_specs = (
        P(None, ("groups", "sample"), "tensor"),
        P(None, ("groups", "sample"), "tensor"),
        P(("groups", "sample"), None, "tensor"),
        P(("groups", "sample"), None, "tensor"),
        P(("groups", "sample")),
        P(("groups", "sample")),
        P(("groups", "sample")),
        P("tensor", "sample"),
    )
    out_specs = P(None, ("groups", "sample"), "tensor")
    return jax.shard_map(
        shards, mesh=mesh, in_specs=in_specs, out_specs=out_specs, check_vma=False
    )
```

```python
import functools

import jax
import jax.numpy as jnp
from jax import lax
from jax.experimental import pallas as pl
from jax.experimental.pallas import tpu as pltpu
from jax.sharding import PartitionSpec as P


HD = 128
BLOCK = 128
LOW = -1e30
EXTRA = 8
FLIPS = (0, 1, 3, 2)
MIX = 3


def nt(a, b):
    return lax.dot_general(a, b, (((1,), (1,)), ((), ())), preferred_element_type=jnp.float32)


def nn(a, b):
    return lax.dot_general(a, b, (((1,), (0,)), ((), ())), preferred_element_type=jnp.float32)


def in_hbm(x):
    return pltpu.with_memory_space_constraint(x, pltpu.HBM)


def payload_kernel(prompt_ref, blocks_ref, pre_ref, out_ref, sems):
    _, keys, kvw = pre_ref.shape
    copies = []
    for c in range(kvw // HD):
        source = pre_ref.at[0, :, pl.ds(c * HD, HD)]
        target = out_ref.at[pl.ds(c * keys, keys), :]
        copies.append(pltpu.make_async_copy(source, target, sems.at[c]))
        copies[c].start()
    lane = lax.broadcasted_iota(jnp.int32, (EXTRA, HD), 1)
    ids = jnp.where(lane < HD // 2, prompt_ref[0], blocks_ref[0])
    out_ref[keys * kvw // HD :, :] = ids.astype(jnp.float32).astype(jnp.bfloat16)
    for copy in copies:
        copy.wait()


def make_payload(prefix_kv, slot_prompt, prefix_blocks):
    _, keys, kvw = prefix_kv.shape
    smem = pl.BlockSpec(memory_space=pltpu.SMEM)
    return pl.pallas_call(
        payload_kernel,
        out_shape=jax.ShapeDtypeStruct((keys * kvw // HD + EXTRA, HD), prefix_kv.dtype),
        in_specs=[smem, smem, pl.BlockSpec(memory_space=pl.ANY)],
        out_specs=pl.BlockSpec(memory_space=pltpu.VMEM),
        scratch_shapes=[pltpu.SemaphoreType.DMA((kvw // HD,))],
        compiler_params=pltpu.CompilerParams(vmem_limit_bytes=4 << 20),
        name="make_payload",
    )(slot_prompt, prefix_blocks, in_hbm(prefix_kv))


def gen_rows(steps, group, row, len_ref, q_ref, new_ref, kv_ref, acc_ref, ml_ref, q_at):
    batch, keys, kvw = kv_ref.shape
    heads = kvw // (2 * HD)
    span = steps * group
    rows = new_ref.shape[1]
    scale = HD ** (-0.5)
    col = lax.broadcasted_iota(jnp.int32, (span, keys), 1)
    new_col = lax.broadcasted_iota(jnp.int32, (span, steps * rows), 1)
    new_row, new_step = new_col % rows, new_col // rows
    step_of = lax.broadcasted_iota(jnp.int32, (span, steps * rows), 0) // group
    causal = new_step <= step_of
    lane = lax.broadcasted_iota(jnp.int32, (span, HD), 1)
    for h in range(heads):
        base = h * 2 * HD
        at = slice(h * span, (h + 1) * span)
        fresh = new_ref[:, :, base : base + 2 * HD].reshape(steps * rows, 2 * HD)
        qs = [q_ref[q_at + b, at, :] for b in range(batch)]
        scores = [nt(qs[b], kv_ref[b, :, base : base + HD]) for b in range(batch)]
        news = nt(jnp.concatenate(qs, axis=0), fresh[:, :HD])
        exps, new_exps = [], []
        for b in range(batch):
            s = jnp.where(col < len_ref[row + b], scores[b] * scale, LOW)
            n = news[b * span : (b + 1) * span] * scale
            n = jnp.where(causal & (new_row == row + b), n, LOW)
            top = jnp.maximum(
                jnp.max(s, axis=1, keepdims=True), jnp.max(n, axis=1, keepdims=True)
            )
            e, f = jnp.exp(s - top), jnp.exp(n - top)
            total = jnp.sum(e, axis=1, keepdims=True) + jnp.sum(f, axis=1, keepdims=True)
            ml_ref[b, at, :] = jnp.where(lane < HD // 2, top, total)
            exps.append(e.astype(jnp.bfloat16))
            new_exps.append(f.astype(jnp.bfloat16))
        more = nn(jnp.concatenate(new_exps, axis=0), fresh[:, HD:])
        for b in range(batch):
            acc = nn(exps[b], kv_ref[b, :, base + HD : base + 2 * HD])
            acc_ref[b, at, :] = acc + more[b * span : (b + 1) * span]


def gen_kernel(
    steps,
    heads,
    group,
    len_ref,
    q_ref,
    new_ref,
    kv_ref,
    grouped_ref,
    acc_ref,
    ml_ref,
    scr,
):
    rows = q_ref.shape[1]
    span = steps * group
    per_row = heads * span
    batch = kv_ref.shape[0]

    @pl.when(pl.program_id(0) == 0)
    def _():
        for s in range(steps):
            for hg in range(heads * group):
                tile = q_ref[s, :, hg * HD : (hg + 1) * HD].astype(jnp.float32)
                start = (hg // group) * span + s * group + hg % group
                scr[pl.ds(start, rows, stride=per_row), :] = tile
        for r in range(rows):
            grouped_ref[r] = scr[r * per_row : (r + 1) * per_row, :].astype(jnp.bfloat16)

    row = pl.program_id(0) * batch
    gen_rows(steps, group, row, len_ref, grouped_ref, new_ref, kv_ref, acc_ref, ml_ref, row)


def gen_attention(queries, fresh, cached, lengths, heads, batch):
    steps, rows, width = queries.shape
    keys, kvw = cached.shape[1:]
    group = width // (heads * HD)
    per_row = heads * steps * group
    sums = jax.ShapeDtypeStruct((rows, per_row, HD), jnp.float32)
    sum_spec = pl.BlockSpec((batch, per_row, HD), lambda r, n: (r, 0, 0))
    return pl.pallas_call(
        functools.partial(gen_kernel, steps, heads, group),
        out_shape=(
            jax.ShapeDtypeStruct((rows, per_row, HD), jnp.bfloat16),
            sums,
            sums,
        ),
        grid_spec=pltpu.PrefetchScalarGridSpec(
            num_scalar_prefetch=1,
            grid=(rows // batch,),
            in_specs=[
                pl.BlockSpec((steps, rows, width), lambda r, n: (0, 0, 0)),
                pl.BlockSpec((steps, rows, kvw), lambda r, n: (0, 0, 0)),
                pl.BlockSpec((batch, keys, kvw), lambda r, n: (r, 0, 0)),
            ],
            out_specs=[
                pl.BlockSpec((rows, per_row, HD), lambda r, n: (0, 0, 0)),
                sum_spec,
                sum_spec,
            ],
            scratch_shapes=[pltpu.VMEM((rows * per_row, HD), jnp.float32)],
        ),
        compiler_params=pltpu.CompilerParams(vmem_limit_bytes=16 << 20),
        cost_estimate=pl.CostEstimate(
            flops=4 * rows * per_row * keys * HD,
            bytes_accessed=2 * rows * keys * kvw,
            transcendentals=rows * per_row * keys,
        ),
        name="gen_attention",
    )(lengths, in_hbm(queries), in_hbm(fresh), in_hbm(cached))


def add_slots_kernel(slots, steps, group, heads, count, *refs):
    pre_refs, (q_ref, acc_ref, ml_ref, out_ref, scr) = refs[:count], refs[count:]
    rows = q_ref.shape[0]
    keys = (pre_refs[0].shape[0] - EXTRA) // (2 * heads)
    span = steps * group
    members = rows // slots
    order = range(members)
    tall = members * span
    scale = HD ** (-0.5)
    col = lax.broadcasted_iota(jnp.int32, (tall, keys), 1)
    for n, pre_ref in enumerate(pre_refs):
        extra = pre_ref[2 * heads * keys :, :].astype(jnp.float32)
        prompt = jnp.max(extra[:, : HD // 2]).astype(jnp.int32)
        length = jnp.max(extra[:, HD // 2 :]).astype(jnp.int32) * BLOCK
        for h in range(heads):
            base = h * 2 * keys
            at = slice(h * span, (h + 1) * span)
            q = jnp.concatenate([q_ref[prompt + i * slots, at, :] for i in order], axis=0)
            ml = jnp.concatenate([ml_ref[prompt + i * slots, at, :] for i in order], axis=0)
            acc = jnp.concatenate([acc_ref[prompt + i * slots, at, :] for i in order], axis=0)
            s = nt(q, pre_ref[base : base + keys, :]) * scale
            s = jnp.where(col < length, s, LOW)
            old_top = ml[:, 0:1]
            old_total = ml[:, HD // 2 : HD // 2 + 1]
            top = jnp.maximum(old_top, jnp.max(s, axis=1, keepdims=True))
            e = jnp.exp(s - top)
            carry = jnp.exp(old_top - top)
            total = jnp.sum(e, axis=1, keepdims=True) + carry * old_total
            add = nn(e.astype(jnp.bfloat16), pre_ref[base + keys : base + 2 * keys, :])
            scr[(n * heads + h) * tall : (n * heads + h + 1) * tall, :] = (add + carry * acc) / total
    tile_rows = members * steps
    for n in range(count):
        for h in range(heads):
            for g in range(group):
                tile = scr[pl.ds((n * heads + h) * tall + g, tile_rows, stride=group), :]
                cols = slice((h * group + g) * HD, (h * group + g + 1) * HD)
                out_ref[n * tile_rows : (n + 1) * tile_rows, cols] = tile.astype(jnp.bfloat16)


def add_slots(grouped, acc, ml, payloads, slots, steps, heads):
    rows, per_row, _ = grouped.shape
    group = per_row // (heads * steps)
    count = len(payloads)
    keys = (payloads[0].shape[0] - EXTRA) // (2 * heads)
    vmem = pl.BlockSpec(memory_space=pltpu.VMEM)
    shape = (count * rows // slots * steps, heads * group * HD)
    return pl.pallas_call(
        functools.partial(add_slots_kernel, slots, steps, group, heads, count),
        out_shape=jax.ShapeDtypeStruct(shape, jnp.bfloat16),
        in_specs=[vmem] * (count + 3),
        out_specs=vmem,
        scratch_shapes=[pltpu.VMEM((count * rows // slots * per_row, HD), jnp.float32)],
        compiler_params=pltpu.CompilerParams(vmem_limit_bytes=8 << 20),
        cost_estimate=pl.CostEstimate(
            flops=4 * count * rows * per_row * keys * HD // slots,
            bytes_accessed=4 * count * keys * heads * HD,
            transcendentals=count * rows * per_row * keys // slots,
        ),
    )(*payloads, grouped, acc, ml)


def order_kernel(steps, rows, *refs):
    pre_refs, out_ref = refs[:-1], refs[-1]
    slots = len(pre_refs)
    size = out_ref.shape[0]
    group = size // slots
    place = lax.broadcasted_iota(jnp.int32, (size, size), 0)
    came = lax.broadcasted_iota(jnp.int32, (size, size), 1)
    prompt = jnp.zeros((size, size), jnp.int32)
    for k, pre_ref in enumerate(pre_refs):
        extra = pre_ref[pre_ref.shape[0] - EXTRA :, : HD // 2].astype(jnp.float32)
        prompt = jnp.where(came // group == k, jnp.max(extra).astype(jnp.int32), prompt)
    row = prompt + came % group // steps * slots
    hit = place == came % steps * rows + row
    out_ref[...] = jnp.where(hit, 1.0, 0.0).astype(jnp.bfloat16)


def row_order(payloads, steps, rows):
    vmem = pl.BlockSpec(memory_space=pltpu.VMEM)
    return pl.pallas_call(
        functools.partial(order_kernel, steps, rows),
        out_shape=jax.ShapeDtypeStruct((steps * rows, steps * rows), jnp.bfloat16),
        in_specs=[vmem] * len(payloads),
        out_specs=vmem,
        compiler_params=pltpu.CompilerParams(vmem_limit_bytes=4 << 20),
        name="row_order",
    )(*payloads)


def finish_kernel(order_ref, a_ref, b_ref, out_ref):
    total = a_ref[...].astype(jnp.float32) + b_ref[...].astype(jnp.float32)
    out_ref[...] = nn(order_ref[...], total.astype(jnp.bfloat16)).astype(jnp.bfloat16)


def finish(order, a, b):
    vmem = pl.BlockSpec(memory_space=pltpu.VMEM)
    return pl.pallas_call(
        finish_kernel,
        out_shape=jax.ShapeDtypeStruct(a.shape, jnp.bfloat16),
        in_specs=[vmem] * 3,
        out_specs=vmem,
        compiler_params=pltpu.CompilerParams(vmem_limit_bytes=4 << 20),
        name="finish",
    )(order, a, b)


def hold_kernel(w_ref, out_ref, sems):
    rows = w_ref.shape[0] // sems.shape[0]
    copies = []
    for c in range(sems.shape[0]):
        at = pl.ds(c * rows, rows)
        copies.append(pltpu.make_async_copy(w_ref.at[at], out_ref.at[at], sems.at[c]))
        copies[c].start()
    for copy in copies:
        copy.wait()


def hold(weight):
    return pl.pallas_call(
        hold_kernel,
        out_shape=jax.ShapeDtypeStruct(weight.shape, weight.dtype),
        in_specs=[pl.BlockSpec(memory_space=pl.ANY)],
        out_specs=pl.BlockSpec(memory_space=pltpu.VMEM),
        scratch_shapes=[pltpu.SemaphoreType.DMA((4,))],
        compiler_params=pltpu.CompilerParams(vmem_limit_bytes=8 << 20),
        name="hold",
    )(in_hbm(weight))


def stack_rows(lhs, refs):
    at = 0
    for ref in refs:
        lhs[at : at + ref.shape[0], :] = ref[...]
        at += ref.shape[0]


def project_first_kernel(parts, *refs):
    att_refs, (w_ref, out_ref, lhs) = refs[:parts], refs[parts:]
    stack_rows(lhs, att_refs)
    out_ref[...] = nn(lhs[...], w_ref[...])


def project_first(pieces, weight):
    parts = len(pieces)
    tall = sum(piece.shape[0] for piece in pieces)
    width, cols = weight.shape
    vmem = pl.BlockSpec(memory_space=pltpu.VMEM)
    return pl.pallas_call(
        functools.partial(project_first_kernel, parts),
        out_shape=jax.ShapeDtypeStruct((tall, cols), jnp.float32),
        in_specs=[vmem] * (parts + 1),
        out_specs=vmem,
        scratch_shapes=[pltpu.VMEM((tall, width), jnp.bfloat16)],
        compiler_params=pltpu.CompilerParams(vmem_limit_bytes=8 << 20),
        cost_estimate=pl.CostEstimate(
            flops=2 * tall * width * cols,
            bytes_accessed=2 * width * cols,
            transcendentals=0,
        ),
        name="project_first",
    )(*pieces, weight)


def project_last_kernel(blocks, first_homes, homes, *refs):
    parts = len(homes)
    me, t = lax.axis_index("sample"), lax.axis_index("tensor")
    mine = (2 * (t % 2) + t // 2) ^ MIX
    pos = [me ^ flip ^ mine for flip in FLIPS]
    att_refs, (first_ref, w_ref, keep_ref, send_ref, lhs, both) = refs[:parts], refs[parts:]
    at = 0
    for home, start, size in first_homes:
        both[pos[home], start : start + size, :] = first_ref[at : at + size, :]
        at += size
    stack_rows(lhs, att_refs)
    sums = nn(lhs[...], w_ref[...])
    at = 0
    for home, start, size in homes:
        both[pos[home], start : start + size, :] = sums[at : at + size]
        at += size
    half = blocks // 2
    for k in range(half):
        keep_ref[k] = both[k]
        send_ref[k] = both[half + k]


def project_last(pieces, homes, first, first_homes, weight, block):
    tall = sum(piece.shape[0] for piece in pieces)
    blocks = len(FLIPS)
    width, cols = weight.shape
    vmem = pl.BlockSpec(memory_space=pltpu.VMEM)
    shape = jax.ShapeDtypeStruct((blocks // 2, block, cols), jnp.float32)
    return pl.pallas_call(
        functools.partial(project_last_kernel, blocks, first_homes, homes),
        out_shape=(shape, shape),
        in_specs=[vmem] * (len(pieces) + 2),
        out_specs=(vmem, vmem),
        scratch_shapes=[
            pltpu.VMEM((tall, width), jnp.bfloat16),
            pltpu.VMEM((blocks, block, cols), jnp.float32),
        ],
        compiler_params=pltpu.CompilerParams(vmem_limit_bytes=8 << 20),
        cost_estimate=pl.CostEstimate(
            flops=2 * tall * width * cols,
            bytes_accessed=2 * width * cols,
            transcendentals=0,
        ),
        name="project_last",
    )(*pieces, first, weight)


def exchange(x, size, flip):
    return lax.ppermute(x, "sample", [(i, i ^ flip) for i in range(size)])


def direct(
    queries, new_kv, gen_kv, prefix_kv, slot_prompt, prefix_blocks, gen_len, out_weight, size
):
    steps, rows, _ = queries.shape
    heads = new_kv.shape[2] // (2 * HD)
    payload = make_payload(prefix_kv, slot_prompt, prefix_blocks)
    far = exchange(payload, size, 3)
    near = exchange(payload, size, 1)
    grouped, acc, ml = gen_attention(queries, new_kv, gen_kv, gen_len, heads, 4)
    far, grouped, acc, ml = lax.optimization_barrier((far, grouped, acc, ml))
    diag = exchange(far, size, 1)
    most = add_slots(grouped, acc, ml, [payload, near, far], size, steps, heads)
    most_far = exchange(most, size, 3)
    most_near = exchange(most, size, 1)
    diag, _ = lax.optimization_barrier((diag, most))
    rest = add_slots(grouped, acc, ml, [diag], size, steps, heads)
    rest_far = exchange(rest, size, 3)
    rest_near = exchange(rest, size, 1)
    most_diag = exchange(most_far, size, 1)
    rest_diag = exchange(rest, size, 2)
    order = row_order([payload, near, far, diag], steps, rows)
    much, little = most.shape[0], rest.shape[0]
    held = hold(out_weight)
    first = project_first([most, rest, most_far, most_near], held)
    first_homes = ((0, 0, much), (0, much, little), (2, 0, much), (1, 0, much))
    last = [rest_far, rest_near, rest_diag, most_diag]
    homes = ((2, much, little), (1, much, little), (3, much, little), (3, 0, much))
    *last, first = lax.optimization_barrier((*last, first))
    keep, send = project_last(last, homes, first, first_homes, held, much + little)
    got = lax.ppermute(send, "tensor", [(0, 1), (1, 0), (2, 3), (3, 2)])
    halves = (keep + got).astype(jnp.bfloat16)
    arrived = []
    for i in range(2):
        perm = []
        for c in range(size):
            for k in range(size):
                perm.append((c * size + k, (2 * (k % 2) + (i ^ (k // 2)) ^ MIX) * size + c))
        piece = lax.ppermute(halves[i], ("sample", "tensor"), perm)
        arrived.append(piece)
    return finish(order, *arrived).reshape(steps, rows, -1)


def split_pairs(cache, heads):
    shaped = cache.reshape(cache.shape[:-1] + (heads, 2, HD))
    return (shaped[..., 0, :], shaped[..., 1, :])


def attend(queries, fresh, cached, prefix, valid, lengths, heads):
    steps_n, rows_n, width = queries.shape
    group = width // (heads * HD)
    scale = HD ** (-0.5)
    q_all = queries.reshape(steps_n, rows_n, heads, group, HD)
    pre_key, pre_val = split_pairs(prefix, heads)
    gen_key, gen_val = split_pairs(cached, heads)
    new_key, new_val = split_pairs(fresh, heads)
    s_pre = (
        jnp.einsum("srkgd,rpkd->srkgp", q_all, pre_key, preferred_element_type=jnp.float32) * scale
    )
    s_gen = (
        jnp.einsum("srkgd,rjkd->srkgj", q_all, gen_key, preferred_element_type=jnp.float32) * scale
    )
    s_new = (
        jnp.einsum("srkgd,urkd->srkgu", q_all, new_key, preferred_element_type=jnp.float32) * scale
    )
    m_pre = (jnp.arange(prefix.shape[1], dtype=jnp.int32)[None, :] < valid[:, None])[
        None, :, None, None, :
    ]
    m_gen = (jnp.arange(cached.shape[1], dtype=jnp.int32)[None, :] < lengths[:, None])[
        None, :, None, None, :
    ]
    order = jnp.arange(steps_n, dtype=jnp.int32)
    m_new = (order[None, :] <= order[:, None])[:, None, None, None, :]
    s_pre = jnp.where(m_pre, s_pre, -jnp.inf)
    s_gen = jnp.where(m_gen, s_gen, -jnp.inf)
    s_new = jnp.where(m_new, s_new, -jnp.inf)
    top = jnp.maximum(
        jnp.maximum(jnp.max(s_pre, -1, keepdims=True), jnp.max(s_gen, -1, keepdims=True)),
        jnp.max(s_new, -1, keepdims=True),
    )
    e_pre = jnp.exp(s_pre - top)
    e_gen = jnp.exp(s_gen - top)
    e_new = jnp.exp(s_new - top)
    total = (
        jnp.sum(e_pre, -1, keepdims=True)
        + jnp.sum(e_gen, -1, keepdims=True)
        + jnp.sum(e_new, -1, keepdims=True)
    )
    w_pre = (e_pre / total).astype(jnp.bfloat16)
    w_gen = (e_gen / total).astype(jnp.bfloat16)
    w_new = (e_new / total).astype(jnp.bfloat16)
    result = jnp.einsum("srkgp,rpkd->srkgd", w_pre, pre_val, preferred_element_type=jnp.float32)
    result = result + jnp.einsum(
        "srkgj,rjkd->srkgd", w_gen, gen_val, preferred_element_type=jnp.float32
    )
    result = result + jnp.einsum(
        "srkgu,urkd->srkgd", w_new, new_val, preferred_element_type=jnp.float32
    )
    return result.reshape(steps_n, rows_n, width).astype(jnp.bfloat16)


def shards(queries, new_kv, gen_kv, prefix_kv, slot_prompt, prefix_blocks, gen_len, out_weight):
    size = lax.axis_size("sample")
    fits = size == 4 and lax.axis_size("tensor") == 4 and prefix_kv.shape[0] == 1
    if fits and queries.shape[0] * queries.shape[1] % (16 * size) == 0:
        return direct(
            queries, new_kv, gen_kv, prefix_kv, slot_prompt, prefix_blocks, gen_len, out_weight, size
        )
    steps_n, rows_n, _ = queries.shape
    heads_local = new_kv.shape[2] // (2 * HD)
    all_prefix, all_slots, all_blocks = (
        lax.all_gather(prefix_kv, "sample", axis=0, tiled=True),
        lax.all_gather(slot_prompt, "sample", axis=0, tiled=True),
        lax.all_gather(prefix_blocks, "sample", axis=0, tiled=True),
    )
    prompt_total = all_slots.shape[0]
    inverse = (
        jnp.zeros((prompt_total,), jnp.int32)
        .at[all_slots]
        .set(jnp.arange(prompt_total, dtype=jnp.int32))
    )
    row_ids = lax.axis_index("sample") * rows_n + jnp.arange(rows_n, dtype=jnp.int32)
    picked = inverse[row_ids % prompt_total]
    own_prefix = jnp.take(all_prefix, picked, axis=0)
    valid = jnp.take(all_blocks, picked) * BLOCK
    attended = attend(queries, new_kv, gen_kv, own_prefix, valid, gen_len, heads_local)
    partial_sums = jnp.einsum(
        "srh,hc->src",
        attended,
        lax.all_gather(out_weight, "sample", axis=1, tiled=True),
        preferred_element_type=jnp.float32,
    )
    summed = []
    for step in range(steps_n):
        summed.append(
            lax.psum_scatter(partial_sums[step], "tensor", scatter_dimension=1, tiled=True)
        )
    mixed = jnp.stack(summed, axis=0)
    return mixed.astype(jnp.bfloat16)


def solution(mesh):
    in_specs = (
        P(None, ("groups", "sample"), "tensor"),
        P(None, ("groups", "sample"), "tensor"),
        P(("groups", "sample"), None, "tensor"),
        P(("groups", "sample"), None, "tensor"),
        P(("groups", "sample")),
        P(("groups", "sample")),
        P(("groups", "sample")),
        P("tensor", "sample"),
    )
    out_specs = P(None, ("groups", "sample"), "tensor")
    return jax.shard_map(
        shards, mesh=mesh, in_specs=in_specs, out_specs=out_specs, check_vma=False
    )
```

```python
import functools

import jax
import jax.numpy as jnp
from jax import lax
from jax.experimental import pallas as pl
from jax.experimental.pallas import tpu as pltpu
from jax.sharding import PartitionSpec as P


HD = 128
BLOCK = 128
LOW = -1e30
EXTRA = 8
FLIPS = (0, 1, 3, 2)
MIX = 3


def nt(a, b):
    return lax.dot_general(a, b, (((1,), (1,)), ((), ())), preferred_element_type=jnp.float32)


def nn(a, b):
    return lax.dot_general(a, b, (((1,), (0,)), ((), ())), preferred_element_type=jnp.float32)


def in_hbm(x):
    return pltpu.with_memory_space_constraint(x, pltpu.HBM)


def payload_kernel(prompt_ref, blocks_ref, pre_ref, out_ref, part_ref, sems):
    _, keys, kvw = pre_ref.shape
    copies = []
    for c in range(kvw // HD):
        source = pre_ref.at[0, :, pl.ds(c * HD, HD)]
        target = out_ref.at[pl.ds(c * keys, keys), :]
        copies.append(pltpu.make_async_copy(source, target, sems.at[0, c]))
        copies[-1].start()
    for c in range(kvw // HD // 2):
        source = pre_ref.at[0, :, pl.ds(c * HD, HD)]
        target = part_ref.at[pl.ds(c * keys, keys), :]
        copies.append(pltpu.make_async_copy(source, target, sems.at[1, c]))
        copies[-1].start()
    lane = lax.broadcasted_iota(jnp.int32, (EXTRA, HD), 1)
    ids = jnp.where(lane < HD // 2, prompt_ref[0], blocks_ref[0])
    out_ref[keys * kvw // HD :, :] = ids.astype(jnp.float32).astype(jnp.bfloat16)
    for copy in copies:
        copy.wait()


def make_payload(prefix_kv, slot_prompt, prefix_blocks):
    _, keys, kvw = prefix_kv.shape
    smem = pl.BlockSpec(memory_space=pltpu.SMEM)
    return pl.pallas_call(
        payload_kernel,
        out_shape=(
            jax.ShapeDtypeStruct((keys * kvw // HD + EXTRA, HD), prefix_kv.dtype),
            jax.ShapeDtypeStruct((keys * kvw // HD // 2, HD), prefix_kv.dtype),
        ),
        in_specs=[smem, smem, pl.BlockSpec(memory_space=pl.ANY)],
        out_specs=[pl.BlockSpec(memory_space=pltpu.VMEM)] * 2,
        scratch_shapes=[pltpu.SemaphoreType.DMA((2, kvw // HD))],
        compiler_params=pltpu.CompilerParams(vmem_limit_bytes=4 << 20),
        name="make_payload",
    )(slot_prompt, prefix_blocks, in_hbm(prefix_kv))


def gen_rows(steps, group, row, len_ref, q_ref, new_ref, kv_ref, acc_ref, ml_ref, q_at):
    batch, keys, kvw = kv_ref.shape
    heads = kvw // (2 * HD)
    span = steps * group
    rows = new_ref.shape[1]
    scale = HD ** (-0.5)
    col = lax.broadcasted_iota(jnp.int32, (span, keys), 1)
    new_col = lax.broadcasted_iota(jnp.int32, (span, steps * rows), 1)
    new_row, new_step = new_col % rows, new_col // rows
    step_of = lax.broadcasted_iota(jnp.int32, (span, steps * rows), 0) // group
    causal = new_step <= step_of
    lane = lax.broadcasted_iota(jnp.int32, (span, HD), 1)
    for h in range(heads):
        base = h * 2 * HD
        at = slice(h * span, (h + 1) * span)
        fresh = new_ref[:, :, base : base + 2 * HD].reshape(steps * rows, 2 * HD)
        qs = [q_ref[q_at + b, at, :] for b in range(batch)]
        scores = [nt(qs[b], kv_ref[b, :, base : base + HD]) for b in range(batch)]
        news = nt(jnp.concatenate(qs, axis=0), fresh[:, :HD])
        exps, new_exps = [], []
        for b in range(batch):
            s = jnp.where(col < len_ref[row + b], scores[b] * scale, LOW)
            n = news[b * span : (b + 1) * span] * scale
            n = jnp.where(causal & (new_row == row + b), n, LOW)
            top = jnp.maximum(
                jnp.max(s, axis=1, keepdims=True), jnp.max(n, axis=1, keepdims=True)
            )
            e, f = jnp.exp(s - top), jnp.exp(n - top)
            total = jnp.sum(e, axis=1, keepdims=True) + jnp.sum(f, axis=1, keepdims=True)
            ml_ref[b, at, :] = jnp.where(lane < HD // 2, top, total)
            exps.append(e.astype(jnp.bfloat16))
            new_exps.append(f.astype(jnp.bfloat16))
        more = nn(jnp.concatenate(new_exps, axis=0), fresh[:, HD:])
        for b in range(batch):
            acc = nn(exps[b], kv_ref[b, :, base + HD : base + 2 * HD])
            acc_ref[b, at, :] = acc + more[b * span : (b + 1) * span]


def gen_kernel(
    steps,
    heads,
    group,
    len_ref,
    q_ref,
    new_ref,
    kv_ref,
    grouped_ref,
    acc_ref,
    ml_ref,
    scr,
):
    rows = q_ref.shape[1]
    span = steps * group
    per_row = heads * span
    batch = kv_ref.shape[0]

    @pl.when(pl.program_id(0) == 0)
    def _():
        for s in range(steps):
            for hg in range(heads * group):
                tile = q_ref[s, :, hg * HD : (hg + 1) * HD].astype(jnp.float32)
                start = (hg // group) * span + s * group + hg % group
                scr[pl.ds(start, rows, stride=per_row), :] = tile
        for r in range(rows):
            grouped_ref[r] = scr[r * per_row : (r + 1) * per_row, :].astype(jnp.bfloat16)

    row = pl.program_id(0) * batch
    gen_rows(steps, group, row, len_ref, grouped_ref, new_ref, kv_ref, acc_ref, ml_ref, row)


def gen_attention(queries, fresh, cached, lengths, heads, batch):
    steps, rows, width = queries.shape
    keys, kvw = cached.shape[1:]
    group = width // (heads * HD)
    per_row = heads * steps * group
    sums = jax.ShapeDtypeStruct((rows, per_row, HD), jnp.float32)
    sum_spec = pl.BlockSpec((batch, per_row, HD), lambda r, n: (r, 0, 0))
    return pl.pallas_call(
        functools.partial(gen_kernel, steps, heads, group),
        out_shape=(
            jax.ShapeDtypeStruct((rows, per_row, HD), jnp.bfloat16),
            sums,
            sums,
        ),
        grid_spec=pltpu.PrefetchScalarGridSpec(
            num_scalar_prefetch=1,
            grid=(rows // batch,),
            in_specs=[
                pl.BlockSpec((steps, rows, width), lambda r, n: (0, 0, 0)),
                pl.BlockSpec((steps, rows, kvw), lambda r, n: (0, 0, 0)),
                pl.BlockSpec((batch, keys, kvw), lambda r, n: (r, 0, 0)),
            ],
            out_specs=[
                pl.BlockSpec((rows, per_row, HD), lambda r, n: (0, 0, 0)),
                sum_spec,
                sum_spec,
            ],
            scratch_shapes=[pltpu.VMEM((rows * per_row, HD), jnp.float32)],
        ),
        compiler_params=pltpu.CompilerParams(vmem_limit_bytes=16 << 20),
        cost_estimate=pl.CostEstimate(
            flops=4 * rows * per_row * keys * HD,
            bytes_accessed=2 * rows * keys * kvw,
            transcendentals=rows * per_row * keys,
        ),
        name="gen_attention",
    )(lengths, in_hbm(queries), in_hbm(fresh), in_hbm(cached))


def add_slots_kernel(slots, steps, group, heads, parts, keys, *refs):
    (q_ref, acc_ref, ml_ref, out_ref, scr), count = refs[sum(parts) :], len(parts)
    rows = q_ref.shape[0]
    span = steps * group
    members = rows // slots
    order = range(members)
    tall = members * span
    scale = HD ** (-0.5)
    col = lax.broadcasted_iota(jnp.int32, (tall, keys), 1)
    for n in range(count):
        pre_refs = refs[sum(parts[:n]) : sum(parts[: n + 1])]
        extra = pre_refs[-1][pre_refs[-1].shape[0] - EXTRA :, :].astype(jnp.float32)
        prompt = jnp.max(extra[:, : HD // 2]).astype(jnp.int32)
        length = jnp.max(extra[:, HD // 2 :]).astype(jnp.int32) * BLOCK
        for h in range(heads):
            pre_ref = pre_refs[h * parts[n] // heads]
            base = h % (heads // parts[n]) * 2 * keys
            at = slice(h * span, (h + 1) * span)
            q = jnp.concatenate([q_ref[prompt + i * slots, at, :] for i in order], axis=0)
            ml = jnp.concatenate([ml_ref[prompt + i * slots, at, :] for i in order], axis=0)
            acc = jnp.concatenate([acc_ref[prompt + i * slots, at, :] for i in order], axis=0)
            s = nt(q, pre_ref[base : base + keys, :]) * scale
            s = jnp.where(col < length, s, LOW)
            old_top = ml[:, 0:1]
            old_total = ml[:, HD // 2 : HD // 2 + 1]
            top = jnp.maximum(old_top, jnp.max(s, axis=1, keepdims=True))
            e = jnp.exp(s - top)
            carry = jnp.exp(old_top - top)
            total = jnp.sum(e, axis=1, keepdims=True) + carry * old_total
            add = nn(e.astype(jnp.bfloat16), pre_ref[base + keys : base + 2 * keys, :])
            scr[(n * heads + h) * tall : (n * heads + h + 1) * tall, :] = (add + carry * acc) / total
    tile_rows = members * steps
    for n in range(count):
        for h in range(heads):
            for g in range(group):
                tile = scr[pl.ds((n * heads + h) * tall + g, tile_rows, stride=group), :]
                cols = slice((h * group + g) * HD, (h * group + g + 1) * HD)
                out_ref[n * tile_rows : (n + 1) * tile_rows, cols] = tile.astype(jnp.bfloat16)


def add_slots(grouped, acc, ml, payloads, slots, steps, heads, keys):
    rows, per_row, _ = grouped.shape
    group = per_row // (heads * steps)
    count = len(payloads)
    parts = [len(payload) for payload in payloads]
    vmem = pl.BlockSpec(memory_space=pltpu.VMEM)
    shape = (count * rows // slots * steps, heads * group * HD)
    return pl.pallas_call(
        functools.partial(add_slots_kernel, slots, steps, group, heads, parts, keys),
        out_shape=jax.ShapeDtypeStruct(shape, jnp.bfloat16),
        in_specs=[vmem] * (sum(parts) + 3),
        out_specs=vmem,
        scratch_shapes=[pltpu.VMEM((count * rows // slots * per_row, HD), jnp.float32)],
        compiler_params=pltpu.CompilerParams(vmem_limit_bytes=8 << 20),
        cost_estimate=pl.CostEstimate(
            flops=4 * count * rows * per_row * keys * HD // slots,
            bytes_accessed=4 * count * keys * heads * HD,
            transcendentals=count * rows * per_row * keys // slots,
        ),
    )(*sum(payloads, []), grouped, acc, ml)


def order_kernel(steps, rows, *refs):
    pre_refs, out_ref = refs[:-1], refs[-1]
    slots = len(pre_refs)
    size = out_ref.shape[0]
    group = size // slots
    place = lax.broadcasted_iota(jnp.int32, (size, size), 0)
    came = lax.broadcasted_iota(jnp.int32, (size, size), 1)
    prompt = jnp.zeros((size, size), jnp.int32)
    for k, pre_ref in enumerate(pre_refs):
        extra = pre_ref[pre_ref.shape[0] - EXTRA :, : HD // 2].astype(jnp.float32)
        prompt = jnp.where(came // group == k, jnp.max(extra).astype(jnp.int32), prompt)
    row = prompt + came % group // steps * slots
    hit = place == came % steps * rows + row
    out_ref[...] = jnp.where(hit, 1.0, 0.0).astype(jnp.bfloat16)


def row_order(payloads, steps, rows):
    vmem = pl.BlockSpec(memory_space=pltpu.VMEM)
    return pl.pallas_call(
        functools.partial(order_kernel, steps, rows),
        out_shape=jax.ShapeDtypeStruct((steps * rows, steps * rows), jnp.bfloat16),
        in_specs=[vmem] * len(payloads),
        out_specs=vmem,
        compiler_params=pltpu.CompilerParams(vmem_limit_bytes=4 << 20),
        name="row_order",
    )(*payloads)


def finish_kernel(order_ref, a_ref, b_ref, out_ref):
    total = a_ref[...].astype(jnp.float32) + b_ref[...].astype(jnp.float32)
    out_ref[...] = nn(order_ref[...], total.astype(jnp.bfloat16)).astype(jnp.bfloat16)


def finish(order, a, b):
    vmem = pl.BlockSpec(memory_space=pltpu.VMEM)
    return pl.pallas_call(
        finish_kernel,
        out_shape=jax.ShapeDtypeStruct(a.shape, jnp.bfloat16),
        in_specs=[vmem] * 3,
        out_specs=vmem,
        compiler_params=pltpu.CompilerParams(vmem_limit_bytes=4 << 20),
        name="finish",
    )(order, a, b)


def hold_kernel(w_ref, out_ref, sems):
    rows = w_ref.shape[0] // sems.shape[0]
    copies = []
    for c in range(sems.shape[0]):
        at = pl.ds(c * rows, rows)
        copies.append(pltpu.make_async_copy(w_ref.at[at], out_ref.at[at], sems.at[c]))
        copies[c].start()
    for copy in copies:
        copy.wait()


def hold(weight):
    return pl.pallas_call(
        hold_kernel,
        out_shape=jax.ShapeDtypeStruct(weight.shape, weight.dtype),
        in_specs=[pl.BlockSpec(memory_space=pl.ANY)],
        out_specs=pl.BlockSpec(memory_space=pltpu.VMEM),
        scratch_shapes=[pltpu.SemaphoreType.DMA((4,))],
        compiler_params=pltpu.CompilerParams(vmem_limit_bytes=8 << 20),
        name="hold",
    )(in_hbm(weight))


def stack_rows(lhs, refs):
    at = 0
    for ref in refs:
        lhs[at : at + ref.shape[0], :] = ref[...]
        at += ref.shape[0]


def project_first_kernel(parts, *refs):
    att_refs, (w_ref, out_ref, lhs) = refs[:parts], refs[parts:]
    stack_rows(lhs, att_refs)
    out_ref[...] = nn(lhs[...], w_ref[...])


def project_first(pieces, weight):
    parts = len(pieces)
    tall = sum(piece.shape[0] for piece in pieces)
    width, cols = weight.shape
    vmem = pl.BlockSpec(memory_space=pltpu.VMEM)
    return pl.pallas_call(
        functools.partial(project_first_kernel, parts),
        out_shape=jax.ShapeDtypeStruct((tall, cols), jnp.float32),
        in_specs=[vmem] * (parts + 1),
        out_specs=vmem,
        scratch_shapes=[pltpu.VMEM((tall, width), jnp.bfloat16)],
        compiler_params=pltpu.CompilerParams(vmem_limit_bytes=8 << 20),
        cost_estimate=pl.CostEstimate(
            flops=2 * tall * width * cols,
            bytes_accessed=2 * width * cols,
            transcendentals=0,
        ),
        name="project_first",
    )(*pieces, weight)


def project_last_kernel(blocks, first_homes, homes, *refs):
    parts = len(homes)
    me, t = lax.axis_index("sample"), lax.axis_index("tensor")
    mine = (2 * (t % 2) + t // 2) ^ MIX
    pos = [me ^ flip ^ mine for flip in FLIPS]
    att_refs, (first_ref, w_ref, keep_ref, send_ref, lhs, both) = refs[:parts], refs[parts:]
    at = 0
    for home, start, size in first_homes:
        both[pos[home], start : start + size, :] = first_ref[at : at + size, :]
        at += size
    stack_rows(lhs, att_refs)
    sums = nn(lhs[...], w_ref[...])
    at = 0
    for home, start, size in homes:
        both[pos[home], start : start + size, :] = sums[at : at + size]
        at += size
    half = blocks // 2
    for k in range(half):
        keep_ref[k] = both[k]
        send_ref[k] = both[half + k]


def project_last(pieces, homes, first, first_homes, weight, block):
    tall = sum(piece.shape[0] for piece in pieces)
    blocks = len(FLIPS)
    width, cols = weight.shape
    vmem = pl.BlockSpec(memory_space=pltpu.VMEM)
    shape = jax.ShapeDtypeStruct((blocks // 2, block, cols), jnp.float32)
    return pl.pallas_call(
        functools.partial(project_last_kernel, blocks, first_homes, homes),
        out_shape=(shape, shape),
        in_specs=[vmem] * (len(pieces) + 2),
        out_specs=(vmem, vmem),
        scratch_shapes=[
            pltpu.VMEM((tall, width), jnp.bfloat16),
            pltpu.VMEM((blocks, block, cols), jnp.float32),
        ],
        compiler_params=pltpu.CompilerParams(vmem_limit_bytes=8 << 20),
        cost_estimate=pl.CostEstimate(
            flops=2 * tall * width * cols,
            bytes_accessed=2 * width * cols,
            transcendentals=0,
        ),
        name="project_last",
    )(*pieces, first, weight)


def exchange(x, size, flip):
    return lax.ppermute(x, "sample", [(i, i ^ flip) for i in range(size)])


def direct(
    queries, new_kv, gen_kv, prefix_kv, slot_prompt, prefix_blocks, gen_len, out_weight, size
):
    steps, rows, _ = queries.shape
    heads = new_kv.shape[2] // (2 * HD)
    payload, part = make_payload(prefix_kv, slot_prompt, prefix_blocks)
    keys = prefix_kv.shape[1]
    far = exchange(payload, size, 3)
    near = exchange(payload, size, 1)
    direct_half = exchange(part, size, 2)
    grouped, acc, ml = gen_attention(queries, new_kv, gen_kv, gen_len, heads, 4)
    far, grouped, acc, ml = lax.optimization_barrier((far, grouped, acc, ml))
    diag = exchange(far[part.shape[0] :], size, 1)
    most = add_slots(grouped, acc, ml, [[payload], [far]], size, steps, heads, keys)
    most_far = exchange(most, size, 3)
    most_near = exchange(most, size, 1)
    near, direct_half, diag, _ = lax.optimization_barrier((near, direct_half, diag, most))
    rest = add_slots(grouped, acc, ml, [[near], [direct_half, diag]], size, steps, heads, keys)
    rest_far = exchange(rest, size, 3)
    rest_near = exchange(rest, size, 1)
    most_diag = exchange(most_far, size, 1)
    rest_diag = exchange(rest, size, 2)
    order = row_order([payload, far, near, diag], steps, rows)
    much, little = most.shape[0], rest.shape[0]
    held = hold(out_weight)
    first = project_first([most, rest, most_far, most_near], held)
    first_homes = ((0, 0, much), (0, much, little), (2, 0, much), (1, 0, much))
    last = [rest_far, rest_near, rest_diag, most_diag]
    homes = ((2, much, little), (1, much, little), (3, much, little), (3, 0, much))
    *last, first = lax.optimization_barrier((*last, first))
    keep, send = project_last(last, homes, first, first_homes, held, much + little)
    got = lax.ppermute(send, "tensor", [(0, 1), (1, 0), (2, 3), (3, 2)])
    halves = (keep + got).astype(jnp.bfloat16)
    arrived = []
    for i in range(2):
        perm = []
        for c in range(size):
            for k in range(size):
                perm.append((c * size + k, (2 * (k % 2) + (i ^ (k // 2)) ^ MIX) * size + c))
        piece = lax.ppermute(halves[i], ("sample", "tensor"), perm)
        arrived.append(piece)
    return finish(order, *arrived).reshape(steps, rows, -1)


def split_pairs(cache, heads):
    shaped = cache.reshape(cache.shape[:-1] + (heads, 2, HD))
    return (shaped[..., 0, :], shaped[..., 1, :])


def attend(queries, fresh, cached, prefix, valid, lengths, heads):
    steps_n, rows_n, width = queries.shape
    group = width // (heads * HD)
    scale = HD ** (-0.5)
    q_all = queries.reshape(steps_n, rows_n, heads, group, HD)
    pre_key, pre_val = split_pairs(prefix, heads)
    gen_key, gen_val = split_pairs(cached, heads)
    new_key, new_val = split_pairs(fresh, heads)
    s_pre = (
        jnp.einsum("srkgd,rpkd->srkgp", q_all, pre_key, preferred_element_type=jnp.float32) * scale
    )
    s_gen = (
        jnp.einsum("srkgd,rjkd->srkgj", q_all, gen_key, preferred_element_type=jnp.float32) * scale
    )
    s_new = (
        jnp.einsum("srkgd,urkd->srkgu", q_all, new_key, preferred_element_type=jnp.float32) * scale
    )
    m_pre = (jnp.arange(prefix.shape[1], dtype=jnp.int32)[None, :] < valid[:, None])[
        None, :, None, None, :
    ]
    m_gen = (jnp.arange(cached.shape[1], dtype=jnp.int32)[None, :] < lengths[:, None])[
        None, :, None, None, :
    ]
    order = jnp.arange(steps_n, dtype=jnp.int32)
    m_new = (order[None, :] <= order[:, None])[:, None, None, None, :]
    s_pre = jnp.where(m_pre, s_pre, -jnp.inf)
    s_gen = jnp.where(m_gen, s_gen, -jnp.inf)
    s_new = jnp.where(m_new, s_new, -jnp.inf)
    top = jnp.maximum(
        jnp.maximum(jnp.max(s_pre, -1, keepdims=True), jnp.max(s_gen, -1, keepdims=True)),
        jnp.max(s_new, -1, keepdims=True),
    )
    e_pre = jnp.exp(s_pre - top)
    e_gen = jnp.exp(s_gen - top)
    e_new = jnp.exp(s_new - top)
    total = (
        jnp.sum(e_pre, -1, keepdims=True)
        + jnp.sum(e_gen, -1, keepdims=True)
        + jnp.sum(e_new, -1, keepdims=True)
    )
    w_pre = (e_pre / total).astype(jnp.bfloat16)
    w_gen = (e_gen / total).astype(jnp.bfloat16)
    w_new = (e_new / total).astype(jnp.bfloat16)
    result = jnp.einsum("srkgp,rpkd->srkgd", w_pre, pre_val, preferred_element_type=jnp.float32)
    result = result + jnp.einsum(
        "srkgj,rjkd->srkgd", w_gen, gen_val, preferred_element_type=jnp.float32
    )
    result = result + jnp.einsum(
        "srkgu,urkd->srkgd", w_new, new_val, preferred_element_type=jnp.float32
    )
    return result.reshape(steps_n, rows_n, width).astype(jnp.bfloat16)


def shards(queries, new_kv, gen_kv, prefix_kv, slot_prompt, prefix_blocks, gen_len, out_weight):
    size = lax.axis_size("sample")
    fits = size == 4 and lax.axis_size("tensor") == 4 and prefix_kv.shape[0] == 1
    fits = fits and new_kv.shape[2] % (4 * HD) == 0
    if fits and queries.shape[0] * queries.shape[1] % (16 * size) == 0:
        return direct(
            queries, new_kv, gen_kv, prefix_kv, slot_prompt, prefix_blocks, gen_len, out_weight, size
        )
    steps_n, rows_n, _ = queries.shape
    heads_local = new_kv.shape[2] // (2 * HD)
    all_prefix, all_slots, all_blocks = (
        lax.all_gather(prefix_kv, "sample", axis=0, tiled=True),
        lax.all_gather(slot_prompt, "sample", axis=0, tiled=True),
        lax.all_gather(prefix_blocks, "sample", axis=0, tiled=True),
    )
    prompt_total = all_slots.shape[0]
    inverse = (
        jnp.zeros((prompt_total,), jnp.int32)
        .at[all_slots]
        .set(jnp.arange(prompt_total, dtype=jnp.int32))
    )
    row_ids = lax.axis_index("sample") * rows_n + jnp.arange(rows_n, dtype=jnp.int32)
    picked = inverse[row_ids % prompt_total]
    own_prefix = jnp.take(all_prefix, picked, axis=0)
    valid = jnp.take(all_blocks, picked) * BLOCK
    attended = attend(queries, new_kv, gen_kv, own_prefix, valid, gen_len, heads_local)
    partial_sums = jnp.einsum(
        "srh,hc->src",
        attended,
        lax.all_gather(out_weight, "sample", axis=1, tiled=True),
        preferred_element_type=jnp.float32,
    )
    summed = []
    for step in range(steps_n):
        summed.append(
            lax.psum_scatter(partial_sums[step], "tensor", scatter_dimension=1, tiled=True)
        )
    mixed = jnp.stack(summed, axis=0)
    return mixed.astype(jnp.bfloat16)


def solution(mesh):
    in_specs = (
        P(None, ("groups", "sample"), "tensor"),
        P(None, ("groups", "sample"), "tensor"),
        P(("groups", "sample"), None, "tensor"),
        P(("groups", "sample"), None, "tensor"),
        P(("groups", "sample")),
        P(("groups", "sample")),
        P(("groups", "sample")),
        P("tensor", "sample"),
    )
    out_specs = P(None, ("groups", "sample"), "tensor")
    return jax.shard_map(
        shards, mesh=mesh, in_specs=in_specs, out_specs=out_specs, check_vma=False
    )
```

```python
import functools

import jax
import jax.numpy as jnp
from jax import lax
from jax.experimental import pallas as pl
from jax.experimental.pallas import tpu as pltpu
from jax.sharding import PartitionSpec as P


HD = 128
BLOCK = 128
LOW = -1e30
EXTRA = 8
FLIPS = (0, 1, 3, 2)
MIX = 3


def nt(a, b):
    return lax.dot_general(a, b, (((1,), (1,)), ((), ())), preferred_element_type=jnp.float32)


def nn(a, b):
    return lax.dot_general(a, b, (((1,), (0,)), ((), ())), preferred_element_type=jnp.float32)


def in_hbm(x):
    return pltpu.with_memory_space_constraint(x, pltpu.HBM)


def payload_kernel(prompt_ref, blocks_ref, pre_ref, out_ref, part_ref, sems):
    _, keys, kvw = pre_ref.shape
    copies = []
    for c in range(kvw // HD):
        source = pre_ref.at[0, :, pl.ds(c * HD, HD)]
        target = out_ref.at[pl.ds(c * keys, keys), :]
        copies.append(pltpu.make_async_copy(source, target, sems.at[0, c]))
        copies[-1].start()
    for c in range(kvw // HD // 2):
        source = pre_ref.at[0, :, pl.ds(c * HD, HD)]
        target = part_ref.at[pl.ds(c * keys, keys), :]
        copies.append(pltpu.make_async_copy(source, target, sems.at[1, c]))
        copies[-1].start()
    lane = lax.broadcasted_iota(jnp.int32, (EXTRA, HD), 1)
    ids = jnp.where(lane < HD // 2, prompt_ref[0], blocks_ref[0])
    out_ref[keys * kvw // HD :, :] = ids.astype(jnp.float32).astype(jnp.bfloat16)
    for copy in copies:
        copy.wait()


def make_payload(prefix_kv, slot_prompt, prefix_blocks):
    _, keys, kvw = prefix_kv.shape
    smem = pl.BlockSpec(memory_space=pltpu.SMEM)
    return pl.pallas_call(
        payload_kernel,
        out_shape=(
            jax.ShapeDtypeStruct((keys * kvw // HD + EXTRA, HD), prefix_kv.dtype),
            jax.ShapeDtypeStruct((keys * kvw // HD // 2, HD), prefix_kv.dtype),
        ),
        in_specs=[smem, smem, pl.BlockSpec(memory_space=pl.ANY)],
        out_specs=[pl.BlockSpec(memory_space=pltpu.VMEM)] * 2,
        scratch_shapes=[pltpu.SemaphoreType.DMA((2, kvw // HD))],
        compiler_params=pltpu.CompilerParams(vmem_limit_bytes=4 << 20),
        name="make_payload",
    )(slot_prompt, prefix_blocks, in_hbm(prefix_kv))


def gen_rows(steps, group, row, len_ref, q_ref, new_ref, kv_ref, acc_ref, ml_ref, q_at):
    batch, keys, kvw = kv_ref.shape
    heads = kvw // (2 * HD)
    span = steps * group
    rows = new_ref.shape[1]
    scale = HD ** (-0.5)
    col = lax.broadcasted_iota(jnp.int32, (span, keys), 1)
    new_col = lax.broadcasted_iota(jnp.int32, (span, steps * rows), 1)
    new_row, new_step = new_col % rows, new_col // rows
    step_of = lax.broadcasted_iota(jnp.int32, (span, steps * rows), 0) // group
    causal = new_step <= step_of
    lane = lax.broadcasted_iota(jnp.int32, (span, HD), 1)
    for h in range(heads):
        base = h * 2 * HD
        at = slice(h * span, (h + 1) * span)
        fresh = new_ref[:, :, base : base + 2 * HD].reshape(steps * rows, 2 * HD)
        qs = [q_ref[q_at + b, at, :] for b in range(batch)]
        scores = [nt(qs[b], kv_ref[b, :, base : base + HD]) for b in range(batch)]
        news = nt(jnp.concatenate(qs, axis=0), fresh[:, :HD])
        exps, new_exps = [], []
        for b in range(batch):
            s = jnp.where(col < len_ref[row + b], scores[b] * scale, LOW)
            n = news[b * span : (b + 1) * span] * scale
            n = jnp.where(causal & (new_row == row + b), n, LOW)
            top = jnp.maximum(
                jnp.max(s, axis=1, keepdims=True), jnp.max(n, axis=1, keepdims=True)
            )
            e, f = jnp.exp(s - top), jnp.exp(n - top)
            total = jnp.sum(e, axis=1, keepdims=True) + jnp.sum(f, axis=1, keepdims=True)
            ml_ref[b, at, :] = jnp.where(lane < HD // 2, top, total)
            exps.append(e.astype(jnp.bfloat16))
            new_exps.append(f.astype(jnp.bfloat16))
        more = nn(jnp.concatenate(new_exps, axis=0), fresh[:, HD:])
        for b in range(batch):
            acc = nn(exps[b], kv_ref[b, :, base + HD : base + 2 * HD])
            acc_ref[b, at, :] = acc + more[b * span : (b + 1) * span]


def gen_kernel(
    steps,
    heads,
    group,
    len_ref,
    q_ref,
    new_ref,
    kv_ref,
    grouped_ref,
    acc_ref,
    ml_ref,
    scr,
):
    rows = q_ref.shape[1]
    span = steps * group
    per_row = heads * span
    batch = kv_ref.shape[0]

    @pl.when(pl.program_id(0) == 0)
    def _():
        for s in range(steps):
            for hg in range(heads * group):
                tile = q_ref[s, :, hg * HD : (hg + 1) * HD].astype(jnp.float32)
                start = (hg // group) * span + s * group + hg % group
                scr[pl.ds(start, rows, stride=per_row), :] = tile
        for r in range(rows):
            grouped_ref[r] = scr[r * per_row : (r + 1) * per_row, :].astype(jnp.bfloat16)

    row = pl.program_id(0) * batch
    gen_rows(steps, group, row, len_ref, grouped_ref, new_ref, kv_ref, acc_ref, ml_ref, row)


def gen_attention(queries, fresh, cached, lengths, heads, batch):
    steps, rows, width = queries.shape
    keys, kvw = cached.shape[1:]
    group = width // (heads * HD)
    per_row = heads * steps * group
    sums = jax.ShapeDtypeStruct((rows, per_row, HD), jnp.float32)
    sum_spec = pl.BlockSpec((batch, per_row, HD), lambda r, n: (r, 0, 0))
    return pl.pallas_call(
        functools.partial(gen_kernel, steps, heads, group),
        out_shape=(
            jax.ShapeDtypeStruct((rows, per_row, HD), jnp.bfloat16),
            sums,
            sums,
        ),
        grid_spec=pltpu.PrefetchScalarGridSpec(
            num_scalar_prefetch=1,
            grid=(rows // batch,),
            in_specs=[
                pl.BlockSpec((steps, rows, width), lambda r, n: (0, 0, 0)),
                pl.BlockSpec((steps, rows, kvw), lambda r, n: (0, 0, 0)),
                pl.BlockSpec((batch, keys, kvw), lambda r, n: (r, 0, 0)),
            ],
            out_specs=[
                pl.BlockSpec((rows, per_row, HD), lambda r, n: (0, 0, 0)),
                sum_spec,
                sum_spec,
            ],
            scratch_shapes=[pltpu.VMEM((rows * per_row, HD), jnp.float32)],
        ),
        compiler_params=pltpu.CompilerParams(vmem_limit_bytes=16 << 20),
        cost_estimate=pl.CostEstimate(
            flops=4 * rows * per_row * keys * HD,
            bytes_accessed=2 * rows * keys * kvw,
            transcendentals=rows * per_row * keys,
        ),
        name="gen_attention",
    )(lengths, in_hbm(queries), in_hbm(fresh), in_hbm(cached))


def add_slots_kernel(slots, steps, group, heads, parts, keys, *refs):
    (q_ref, acc_ref, ml_ref, out_ref, scr), count = refs[sum(parts) :], len(parts)
    rows = q_ref.shape[0]
    span = steps * group
    members = rows // slots
    order = range(members)
    tall = members * span
    scale = HD ** (-0.5)
    col = lax.broadcasted_iota(jnp.int32, (tall, keys), 1)
    for n in range(count):
        pre_refs = refs[sum(parts[:n]) : sum(parts[: n + 1])]
        extra = pre_refs[-1][pre_refs[-1].shape[0] - EXTRA :, :].astype(jnp.float32)
        prompt = jnp.max(extra[:, : HD // 2]).astype(jnp.int32)
        length = jnp.max(extra[:, HD // 2 :]).astype(jnp.int32) * BLOCK
        for h in range(heads):
            pre_ref = pre_refs[h * parts[n] // heads]
            base = h % (heads // parts[n]) * 2 * keys
            at = slice(h * span, (h + 1) * span)
            q = jnp.concatenate([q_ref[prompt + i * slots, at, :] for i in order], axis=0)
            ml = jnp.concatenate([ml_ref[prompt + i * slots, at, :] for i in order], axis=0)
            acc = jnp.concatenate([acc_ref[prompt + i * slots, at, :] for i in order], axis=0)
            s = nt(q, pre_ref[base : base + keys, :]) * scale
            s = jnp.where(col < length, s, LOW)
            old_top = ml[:, 0:1]
            old_total = ml[:, HD // 2 : HD // 2 + 1]
            top = jnp.maximum(old_top, jnp.max(s, axis=1, keepdims=True))
            e = jnp.exp(s - top)
            carry = jnp.exp(old_top - top)
            total = jnp.sum(e, axis=1, keepdims=True) + carry * old_total
            add = nn(e.astype(jnp.bfloat16), pre_ref[base + keys : base + 2 * keys, :])
            scr[(n * heads + h) * tall : (n * heads + h + 1) * tall, :] = (add + carry * acc) / total
    tile_rows = members * steps
    for n in range(count):
        for h in range(heads):
            for g in range(group):
                tile = scr[pl.ds((n * heads + h) * tall + g, tile_rows, stride=group), :]
                cols = slice((h * group + g) * HD, (h * group + g + 1) * HD)
                out_ref[n * tile_rows : (n + 1) * tile_rows, cols] = tile.astype(jnp.bfloat16)


def add_slots(grouped, acc, ml, payloads, slots, steps, heads, keys):
    rows, per_row, _ = grouped.shape
    group = per_row // (heads * steps)
    count = len(payloads)
    parts = [len(payload) for payload in payloads]
    vmem = pl.BlockSpec(memory_space=pltpu.VMEM)
    shape = (count * rows // slots * steps, heads * group * HD)
    return pl.pallas_call(
        functools.partial(add_slots_kernel, slots, steps, group, heads, parts, keys),
        out_shape=jax.ShapeDtypeStruct(shape, jnp.bfloat16),
        in_specs=[vmem] * (sum(parts) + 3),
        out_specs=vmem,
        scratch_shapes=[pltpu.VMEM((count * rows // slots * per_row, HD), jnp.float32)],
        compiler_params=pltpu.CompilerParams(vmem_limit_bytes=8 << 20),
        cost_estimate=pl.CostEstimate(
            flops=4 * count * rows * per_row * keys * HD // slots,
            bytes_accessed=4 * count * keys * heads * HD,
            transcendentals=count * rows * per_row * keys // slots,
        ),
    )(*sum(payloads, []), grouped, acc, ml)


def order_kernel(steps, rows, *refs):
    pre_refs, out_ref = refs[:-1], refs[-1]
    slots = len(pre_refs)
    size = out_ref.shape[0]
    group = size // slots
    place = lax.broadcasted_iota(jnp.int32, (size, size), 0)
    came = lax.broadcasted_iota(jnp.int32, (size, size), 1)
    prompt = jnp.zeros((size, size), jnp.int32)
    for k, pre_ref in enumerate(pre_refs):
        extra = pre_ref[pre_ref.shape[0] - EXTRA :, : HD // 2].astype(jnp.float32)
        prompt = jnp.where(came // group == k, jnp.max(extra).astype(jnp.int32), prompt)
    row = prompt + came % group // steps * slots
    hit = place == came % steps * rows + row
    out_ref[...] = jnp.where(hit, 1.0, 0.0).astype(jnp.bfloat16)


def row_order(payloads, steps, rows):
    vmem = pl.BlockSpec(memory_space=pltpu.VMEM)
    return pl.pallas_call(
        functools.partial(order_kernel, steps, rows),
        out_shape=jax.ShapeDtypeStruct((steps * rows, steps * rows), jnp.bfloat16),
        in_specs=[vmem] * len(payloads),
        out_specs=vmem,
        compiler_params=pltpu.CompilerParams(vmem_limit_bytes=4 << 20),
        name="row_order",
    )(*payloads)


def finish_kernel(order_ref, a_ref, b_ref, out_ref):
    total = a_ref[...].astype(jnp.float32) + b_ref[...].astype(jnp.float32)
    out_ref[...] = nn(order_ref[...], total.astype(jnp.bfloat16)).astype(jnp.bfloat16)


def finish(order, a, b):
    vmem = pl.BlockSpec(memory_space=pltpu.VMEM)
    return pl.pallas_call(
        finish_kernel,
        out_shape=jax.ShapeDtypeStruct(a.shape, jnp.bfloat16),
        in_specs=[vmem] * 3,
        out_specs=vmem,
        compiler_params=pltpu.CompilerParams(vmem_limit_bytes=4 << 20),
        name="finish",
    )(order, a, b)


def hold_kernel(w_ref, out_ref, sems):
    rows = w_ref.shape[0] // sems.shape[0]
    copies = []
    for c in range(sems.shape[0]):
        at = pl.ds(c * rows, rows)
        copies.append(pltpu.make_async_copy(w_ref.at[at], out_ref.at[at], sems.at[c]))
        copies[c].start()
    for copy in copies:
        copy.wait()


def hold(weight):
    return pl.pallas_call(
        hold_kernel,
        out_shape=jax.ShapeDtypeStruct(weight.shape, weight.dtype),
        in_specs=[pl.BlockSpec(memory_space=pl.ANY)],
        out_specs=pl.BlockSpec(memory_space=pltpu.VMEM),
        scratch_shapes=[pltpu.SemaphoreType.DMA((4,))],
        compiler_params=pltpu.CompilerParams(vmem_limit_bytes=8 << 20),
        name="hold",
    )(in_hbm(weight))


def stack_rows(lhs, refs):
    at = 0
    for ref in refs:
        lhs[at : at + ref.shape[0], :] = ref[...]
        at += ref.shape[0]


def project_first_kernel(parts, *refs):
    att_refs, (w_ref, out_ref, lhs) = refs[:parts], refs[parts:]
    stack_rows(lhs, att_refs)
    out_ref[...] = nn(lhs[...], w_ref[...])


def project_first(pieces, weight):
    parts = len(pieces)
    tall = sum(piece.shape[0] for piece in pieces)
    width, cols = weight.shape
    vmem = pl.BlockSpec(memory_space=pltpu.VMEM)
    return pl.pallas_call(
        functools.partial(project_first_kernel, parts),
        out_shape=jax.ShapeDtypeStruct((tall, cols), jnp.float32),
        in_specs=[vmem] * (parts + 1),
        out_specs=vmem,
        scratch_shapes=[pltpu.VMEM((tall, width), jnp.bfloat16)],
        compiler_params=pltpu.CompilerParams(vmem_limit_bytes=8 << 20),
        cost_estimate=pl.CostEstimate(
            flops=2 * tall * width * cols,
            bytes_accessed=2 * width * cols,
            transcendentals=0,
        ),
        name="project_first",
    )(*pieces, weight)


def project_last_kernel(blocks, first_homes, homes, *refs):
    parts = len(homes)
    me, t = lax.axis_index("sample"), lax.axis_index("tensor")
    mine = (2 * (t % 2) + t // 2) ^ MIX
    pos = [me ^ flip ^ mine for flip in FLIPS]
    att_refs, (first_ref, w_ref, keep_ref, send_ref, lhs, both) = refs[:parts], refs[parts:]
    at = 0
    for home, start, size in first_homes:
        both[pos[home], start : start + size, :] = first_ref[at : at + size, :]
        at += size
    stack_rows(lhs, att_refs)
    sums = nn(lhs[...], w_ref[...])
    at = 0
    for home, start, size in homes:
        both[pos[home], start : start + size, :] = sums[at : at + size]
        at += size
    half = blocks // 2
    for k in range(half):
        keep_ref[k] = both[k]
        send_ref[k] = both[half + k].astype(send_ref.dtype)


def project_last(pieces, homes, first, first_homes, weight, block):
    tall = sum(piece.shape[0] for piece in pieces)
    blocks = len(FLIPS)
    width, cols = weight.shape
    vmem = pl.BlockSpec(memory_space=pltpu.VMEM)
    shape = jax.ShapeDtypeStruct((blocks // 2, block, cols), jnp.float32)
    return pl.pallas_call(
        functools.partial(project_last_kernel, blocks, first_homes, homes),
        out_shape=(shape, jax.ShapeDtypeStruct(shape.shape, jnp.bfloat16)),
        in_specs=[vmem] * (len(pieces) + 2),
        out_specs=(vmem, vmem),
        scratch_shapes=[
            pltpu.VMEM((tall, width), jnp.bfloat16),
            pltpu.VMEM((blocks, block, cols), jnp.float32),
        ],
        compiler_params=pltpu.CompilerParams(vmem_limit_bytes=8 << 20),
        cost_estimate=pl.CostEstimate(
            flops=2 * tall * width * cols,
            bytes_accessed=2 * width * cols,
            transcendentals=0,
        ),
        name="project_last",
    )(*pieces, first, weight)


def exchange(x, size, flip):
    return lax.ppermute(x, "sample", [(i, i ^ flip) for i in range(size)])


def direct(
    queries, new_kv, gen_kv, prefix_kv, slot_prompt, prefix_blocks, gen_len, out_weight, size
):
    steps, rows, _ = queries.shape
    heads = new_kv.shape[2] // (2 * HD)
    payload, part = make_payload(prefix_kv, slot_prompt, prefix_blocks)
    keys = prefix_kv.shape[1]
    far = exchange(payload, size, 3)
    near = exchange(payload, size, 1)
    direct_half = exchange(part, size, 2)
    grouped, acc, ml = gen_attention(queries, new_kv, gen_kv, gen_len, heads, 8)
    far, grouped, acc, ml = lax.optimization_barrier((far, grouped, acc, ml))
    diag = exchange(far[part.shape[0] :], size, 1)
    most = add_slots(grouped, acc, ml, [[payload], [far]], size, steps, heads, keys)
    most_far = exchange(most, size, 3)
    most_near = exchange(most, size, 1)
    near, direct_half, diag, _ = lax.optimization_barrier((near, direct_half, diag, most))
    rest = add_slots(grouped, acc, ml, [[near], [direct_half, diag]], size, steps, heads, keys)
    rest_far = exchange(rest, size, 3)
    rest_near = exchange(rest, size, 1)
    most_diag = exchange(most_far, size, 1)
    rest_diag = exchange(rest, size, 2)
    order = row_order([payload, far, near, diag], steps, rows)
    much, little = most.shape[0], rest.shape[0]
    held = hold(out_weight)
    first = project_first([most, rest, most_far, most_near], held)
    first_homes = ((0, 0, much), (0, much, little), (2, 0, much), (1, 0, much))
    last = [rest_far, rest_near, rest_diag, most_diag]
    homes = ((2, much, little), (1, much, little), (3, much, little), (3, 0, much))
    *last, first = lax.optimization_barrier((*last, first))
    keep, send = project_last(last, homes, first, first_homes, held, much + little)
    got = lax.ppermute(send, "tensor", [(0, 1), (1, 0), (2, 3), (3, 2)])
    halves = (keep + got).astype(jnp.bfloat16)
    arrived = []
    for i in range(2):
        perm = []
        for c in range(size):
            for k in range(size):
                perm.append((c * size + k, (2 * (k % 2) + (i ^ (k // 2)) ^ MIX) * size + c))
        piece = lax.ppermute(halves[i], ("sample", "tensor"), perm)
        arrived.append(piece)
    return finish(order, *arrived).reshape(steps, rows, -1)


def split_pairs(cache, heads):
    shaped = cache.reshape(cache.shape[:-1] + (heads, 2, HD))
    return (shaped[..., 0, :], shaped[..., 1, :])


def attend(queries, fresh, cached, prefix, valid, lengths, heads):
    steps_n, rows_n, width = queries.shape
    group = width // (heads * HD)
    scale = HD ** (-0.5)
    q_all = queries.reshape(steps_n, rows_n, heads, group, HD)
    pre_key, pre_val = split_pairs(prefix, heads)
    gen_key, gen_val = split_pairs(cached, heads)
    new_key, new_val = split_pairs(fresh, heads)
    s_pre = (
        jnp.einsum("srkgd,rpkd->srkgp", q_all, pre_key, preferred_element_type=jnp.float32) * scale
    )
    s_gen = (
        jnp.einsum("srkgd,rjkd->srkgj", q_all, gen_key, preferred_element_type=jnp.float32) * scale
    )
    s_new = (
        jnp.einsum("srkgd,urkd->srkgu", q_all, new_key, preferred_element_type=jnp.float32) * scale
    )
    m_pre = (jnp.arange(prefix.shape[1], dtype=jnp.int32)[None, :] < valid[:, None])[
        None, :, None, None, :
    ]
    m_gen = (jnp.arange(cached.shape[1], dtype=jnp.int32)[None, :] < lengths[:, None])[
        None, :, None, None, :
    ]
    order = jnp.arange(steps_n, dtype=jnp.int32)
    m_new = (order[None, :] <= order[:, None])[:, None, None, None, :]
    s_pre = jnp.where(m_pre, s_pre, -jnp.inf)
    s_gen = jnp.where(m_gen, s_gen, -jnp.inf)
    s_new = jnp.where(m_new, s_new, -jnp.inf)
    top = jnp.maximum(
        jnp.maximum(jnp.max(s_pre, -1, keepdims=True), jnp.max(s_gen, -1, keepdims=True)),
        jnp.max(s_new, -1, keepdims=True),
    )
    e_pre = jnp.exp(s_pre - top)
    e_gen = jnp.exp(s_gen - top)
    e_new = jnp.exp(s_new - top)
    total = (
        jnp.sum(e_pre, -1, keepdims=True)
        + jnp.sum(e_gen, -1, keepdims=True)
        + jnp.sum(e_new, -1, keepdims=True)
    )
    w_pre = (e_pre / total).astype(jnp.bfloat16)
    w_gen = (e_gen / total).astype(jnp.bfloat16)
    w_new = (e_new / total).astype(jnp.bfloat16)
    result = jnp.einsum("srkgp,rpkd->srkgd", w_pre, pre_val, preferred_element_type=jnp.float32)
    result = result + jnp.einsum(
        "srkgj,rjkd->srkgd", w_gen, gen_val, preferred_element_type=jnp.float32
    )
    result = result + jnp.einsum(
        "srkgu,urkd->srkgd", w_new, new_val, preferred_element_type=jnp.float32
    )
    return result.reshape(steps_n, rows_n, width).astype(jnp.bfloat16)


def shards(queries, new_kv, gen_kv, prefix_kv, slot_prompt, prefix_blocks, gen_len, out_weight):
    size = lax.axis_size("sample")
    fits = size == 4 and lax.axis_size("tensor") == 4 and prefix_kv.shape[0] == 1
    fits = fits and new_kv.shape[2] % (4 * HD) == 0
    if fits and queries.shape[0] * queries.shape[1] % (16 * size) == 0:
        return direct(
            queries, new_kv, gen_kv, prefix_kv, slot_prompt, prefix_blocks, gen_len, out_weight, size
        )
    steps_n, rows_n, _ = queries.shape
    heads_local = new_kv.shape[2] // (2 * HD)
    all_prefix, all_slots, all_blocks = (
        lax.all_gather(prefix_kv, "sample", axis=0, tiled=True),
        lax.all_gather(slot_prompt, "sample", axis=0, tiled=True),
        lax.all_gather(prefix_blocks, "sample", axis=0, tiled=True),
    )
    prompt_total = all_slots.shape[0]
    inverse = (
        jnp.zeros((prompt_total,), jnp.int32)
        .at[all_slots]
        .set(jnp.arange(prompt_total, dtype=jnp.int32))
    )
    row_ids = lax.axis_index("sample") * rows_n + jnp.arange(rows_n, dtype=jnp.int32)
    picked = inverse[row_ids % prompt_total]
    own_prefix = jnp.take(all_prefix, picked, axis=0)
    valid = jnp.take(all_blocks, picked) * BLOCK
    attended = attend(queries, new_kv, gen_kv, own_prefix, valid, gen_len, heads_local)
    partial_sums = jnp.einsum(
        "srh,hc->src",
        attended,
        lax.all_gather(out_weight, "sample", axis=1, tiled=True),
        preferred_element_type=jnp.float32,
    )
    summed = []
    for step in range(steps_n):
        summed.append(
            lax.psum_scatter(partial_sums[step], "tensor", scatter_dimension=1, tiled=True)
        )
    mixed = jnp.stack(summed, axis=0)
    return mixed.astype(jnp.bfloat16)


def solution(mesh):
    in_specs = (
        P(None, ("groups", "sample"), "tensor"),
        P(None, ("groups", "sample"), "tensor"),
        P(("groups", "sample"), None, "tensor"),
        P(("groups", "sample"), None, "tensor"),
        P(("groups", "sample")),
        P(("groups", "sample")),
        P(("groups", "sample")),
        P("tensor", "sample"),
    )
    out_specs = P(None, ("groups", "sample"), "tensor")
    return jax.shard_map(
        shards, mesh=mesh, in_specs=in_specs, out_specs=out_specs, check_vma=False
    )
```
